32 devices in a mesh: band: 16 (over z, x, core), seq: 2 (over y).
Axes of the slice: x: 2, y: 2, z: 4, core: 2. Of those that a mesh axis runs over, the one named last changes fastest.
Arguments:
- tokens: bfloat16 [4, 1536, 1024], P('seq', 'band'), may hold values from -6 to 6
- segment_ids: int32 [4, 1536], P('seq'), may hold values from -1 to 2, as said below
- qkv_weight: bfloat16 [1024, 3072], P('seq'), may hold values from -0.1875 to 0.1875
- out_weight: bfloat16 [1024, 1024], P('seq'), may hold values from -3 to 3
- up_weight: bfloat16 [1024, 4096], P('seq'), may hold values from -0.1875 to 0.1875
- down_weight: bfloat16 [4096, 1024], P('seq'), may hold values from -0.09375 to 0.09375
- gain_first: bfloat16 [1024], P('seq'), may hold values from 0.5 to 1.5
- gain_second: bfloat16 [1024], P('seq'), may hold values from 0.5 to 1.5
- out_cotangent: bfloat16 [4, 1536, 1024], P('seq', 'band'), may hold values from -6 to 6
Outputs:
- layer_out: bfloat16 [4, 1536, 1024], P('seq', 'band')
- token_grad: float32 [4, 1536, 1024], P('seq', 'band')
- qkv_grad: float32 [1024, 3072], P('seq')
- outproj_grad: float32 [1024, 1024], P('seq')
- up_grad: float32 [1024, 4096], P('seq')
- down_grad: float32 [4096, 1024], P('seq')
- gain_first_grad: float32 [1024], P('seq')
- gain_second_grad: float32 [1024], P('seq')
The draws below stay inside these ranges and needn't reach their ends.
Inputs may be any that keep to these rules, and one draw needn't show every extreme that they name: `segment_ids`: in each sequence the ids run 0, then 1, then 2, then -1 over four non-empty runs of positions, in that order; the run of 0 covers at least half, rounded down, of the positions that are not -1.
All inputs are finite; a program needn't handle non-finite values.
Results may differ from the reference program's by a relative error of at most 0.025.
Values may be sent and summed in bfloat16 or wider, within the bound.
A program may use at most 320 MiB of HBM per device.

```python
import math
import jax
import jax.numpy as jnp
from jax import lax

D = 1024
HEADS = 16
HEAD_DIM = 64
FF = 4096
SEQS = 4
LENGTH = 1536


def draw_segment_ids(key, part):
    parts = jax.random.split(jax.random.fold_in(key, 17), 3)
    padding = jax.random.randint(parts[0], (SEQS,), 1, LENGTH // 8 + 2)
    used = LENGTH - padding
    first = jax.random.randint(parts[1], (SEQS,), used // 2, 3 * used // 4 + 1)
    rest = used - first
    second = first + jax.random.randint(parts[2], (SEQS,), rest // 4 + 1, 3 * rest // 4 + 2)
    places = jnp.arange(LENGTH, dtype=jnp.int32)[None, :]
    ids = jnp.where(places < first[:, None], 0, jnp.where(places < second[:, None], 1, jnp.where(places < used[:, None], 2, -1)))
    return ids.astype(jnp.int32)


def block_levels(own_key, dims, pieces, least, top_value):
    gain = 1.0
    for axis_at, shards_of in pieces:
        steps = jax.random.uniform(jax.random.fold_in(jax.random.fold_in(own_key, 6), axis_at), (shards_of,), jnp.float32, least / len(pieces), top_value / len(pieces))
        gain = gain * jnp.repeat(jnp.exp(steps), dims[axis_at] // shards_of).reshape((-1,) + (1,) * (len(dims) - 1 - axis_at))
    return gain


def centred(key, dims, scale, limit, pieces=(), kind=jnp.bfloat16):
    loudness = block_levels(key, dims, pieces, -0.22, 0.18) if pieces else 1.0
    entries = jax.random.normal(key, dims, jnp.float32) * scale * loudness
    return jnp.minimum(jnp.maximum(entries, -limit), limit).astype(kind)


def setup_inputs(seed: int = 0) -> dict:
    keys = jax.random.split(jax.random.key(seed), 10)
    return {
        "tokens": centred(keys[0], (SEQS, LENGTH, D), 1.0, 6.0, ((0, 2), (1, 16))),
        "segment_ids": draw_segment_ids(jax.random.fold_in(keys[9], 71), 0),
        "qkv_weight": centred(keys[2], (D, 3 * D), D ** -0.5, 0.1875, ((0, 2),)),
        "out_weight": centred(keys[3], (D, D), (max(1, 6 * D // LENGTH)) ** -0.5, 3.0, ((0, 2),)),
        "up_weight": centred(keys[4], (D, FF), D ** -0.5, 0.1875, ((0, 2),)),
        "down_weight": centred(keys[5], (FF, D), FF ** -0.5, 0.09375, ((0, 2),)),
        "gain_first": jnp.clip(1.0 + 0.1 * jax.random.normal(keys[6], (D,), jnp.float32), 0.5, 1.5).astype(jnp.bfloat16),
        "gain_second": jnp.clip(1.0 + 0.1 * jax.random.normal(keys[7], (D,), jnp.float32), 0.5, 1.5).astype(jnp.bfloat16),
        "out_cotangent": centred(keys[8], (SEQS, LENGTH, D), 1.0, 6.0, ((0, 2), (1, 16))),
    }


EPS = 1e-06
NEG = -1e+30

@jax.custom_vjp
def low(v):
    return lax.optimization_barrier(v.astype(jnp.bfloat16)).astype(jnp.float32)

@jax.custom_vjp
def low_back(v):
    return v

def low_keep(v):
    return (low(v), None)

def low_pass(kept, grad):
    return (grad,)

def back_keep(v):
    return (v, None)

def back_low(kept, grad):
    return (low(grad),)
low.defvjp(low_keep, low_pass)
low_back.defvjp(back_keep, back_low)

def matmul(left, right):
    return jnp.dot(left, right, precision=lax.Precision.HIGHEST)

def layer_norm(values):
    centre = values - lax.optimization_barrier(jnp.mean(values, axis=-1, keepdims=True))
    return centre * lax.rsqrt(lax.optimization_barrier(jnp.mean(centre * centre, axis=-1, keepdims=True)) + EPS)

def layer(inputs, seg_row, qkv_weight, out_weight, up_weight, down_weight, gain_first, gain_second):
    seq_len = inputs.shape[0]
    valid = (seg_row >= 0).astype(jnp.float32)[:, None]
    h_one = low(layer_norm(inputs) * gain_first)
    qkv = low(low_back(matmul(h_one, qkv_weight)))
    queries = qkv[:, :D].reshape(seq_len, HEADS, HEAD_DIM)
    key_rows = qkv[:, D:2 * D].reshape(seq_len, HEADS, HEAD_DIM)
    value_rows = qkv[:, 2 * D:].reshape(seq_len, HEADS, HEAD_DIM)
    block = math.gcd(seq_len, 512)
    blocks = seq_len // block

    def attend(item):
        query_block, seg_block = item
        scores = jnp.einsum('qhd,khd->hqk', query_block, key_rows, precision=lax.Precision.HIGHEST) * HEAD_DIM ** (-0.5)
        scores = low_back(scores)
        mask = (seg_block[:, None] == seg_row[None, :])[None]
        probs = jax.nn.softmax(jnp.where(mask, scores, NEG), axis=-1)
        result = jnp.einsum('hqk,khd->qhd', low(probs), value_rows, precision=lax.Precision.HIGHEST)
        return result.reshape(block, D)
    attention = lax.map(jax.checkpoint(attend), (queries.reshape(blocks, block, HEADS, HEAD_DIM), seg_row.reshape(blocks, block)))
    attention = attention.reshape(seq_len, D)
    attn_low = low(low_back(attention))
    resid = inputs + valid * low_back(matmul(attn_low, out_weight))
    h_two = low(layer_norm(resid) * gain_second)
    pre_act = low_back(matmul(h_two, up_weight))
    hidden_low = low(jax.nn.gelu(pre_act, approximate=False))
    return resid + valid * matmul(hidden_low, down_weight)

def reference(tokens, segment_ids, qkv_weight, out_weight, up_weight, down_weight, gain_first, gain_second, out_cotangent):
    weights = (qkv_weight.astype(jnp.float32), out_weight.astype(jnp.float32), up_weight.astype(jnp.float32), down_weight.astype(jnp.float32), gain_first.astype(jnp.float32), gain_second.astype(jnp.float32))

    def per_sequence(totals, item):
        inputs, seg_row, cotangent = item

        def forward(values, qkv_w, out_w, up_w, down_w, gain_a, gain_b):
            return layer(values, seg_row, qkv_w, out_w, up_w, down_w, gain_a, gain_b)
        result, pull = jax.vjp(forward, inputs.astype(jnp.float32), *weights)
        grads = pull(cotangent.astype(jnp.float32))
        summed = tuple((total + grad for total, grad in zip(totals, grads[1:])))
        return (summed, (result.astype(jnp.bfloat16), grads[0]))
    start = tuple((jnp.zeros_like(weight) for weight in weights))
    totals, (outputs, input_grads) = lax.scan(per_sequence, start, (tokens, segment_ids, out_cotangent))
    return (outputs, input_grads, totals[0], totals[1], totals[2], totals[3], totals[4], totals[5])
```

```python
import functools
import math

import jax
import jax.numpy as jnp
from jax import lax
from jax.experimental import pallas as pl
from jax.experimental.pallas import tpu as pltpu
from jax.sharding import PartitionSpec as P

HEADS = 16
HEAD_DIM = 64


EPS = 1e-06
NEG = -1e30
ROOT_HALF = 0.7071067811865476
DENSITY = 0.3989422804014327


def layer_norm(values, gain):
    centre = values - jnp.mean(values, axis=-1, keepdims=True)
    inv_std = lax.rsqrt(jnp.mean(centre * centre, axis=-1, keepdims=True) + EPS)
    normed = centre * inv_std
    return (normed * gain, normed, inv_std)


def norm_back(grad_in, gain, normed, inv_std):
    scaled = grad_in * gain
    mean_one = jnp.mean(scaled, axis=-1, keepdims=True)
    mean_two = jnp.mean(scaled * normed, axis=-1, keepdims=True)
    gain_grad = jnp.sum((grad_in * normed).reshape(-1, grad_in.shape[-1]), axis=0)
    return (inv_std * (scaled - mean_one - normed * mean_two), gain_grad)


def split_heads(matrix):
    return matrix.reshape(matrix.shape[:-1] + (HEADS, HEAD_DIM))


def masked_scores(query_part, key_part, query_seg, key_seg):
    scores = jnp.einsum(
        "qhd,khd->hqk", query_part, key_part, preferred_element_type=jnp.float32
    ) * HEAD_DIM ** (-0.5)
    return (scores, (query_seg[:, None] == key_seg[None, :])[None])


def key_terms(
    query_part, dout_part, lse_part, delta_part, query_seg, key_part, value_part, key_seg
):
    scores, mask = masked_scores(query_part, key_part, query_seg, key_seg)
    probs = jnp.where(mask, jnp.exp(scores - lse_part[:, :, None]), 0.0)
    value_grad = jnp.einsum(
        "hqk,qhd->khd", probs.astype(jnp.bfloat16), dout_part, preferred_element_type=jnp.float32
    )
    prob_grad = jnp.einsum(
        "qhd,khd->hqk", dout_part, value_part, preferred_element_type=jnp.float32
    )
    score_grad = (probs * (prob_grad - delta_part[:, :, None])).astype(jnp.bfloat16)
    key_grad = jnp.einsum(
        "hqk,qhd->khd", score_grad, query_part, preferred_element_type=jnp.float32
    ) * HEAD_DIM ** (-0.5)
    return (key_grad, value_grad)


def online_step(query_part, query_seg):

    def step(state, item):
        key_block, value_block, seg_block = item
        run_max, run_sum, run_acc = state
        scores, mask = masked_scores(query_part, split_heads(key_block), query_seg, seg_block)
        masked = jnp.where(mask, scores, NEG)
        top = jnp.maximum(run_max, jnp.max(masked, axis=-1))
        correct = jnp.exp(run_max - top)
        probs = jnp.where(mask, jnp.exp(masked - top[:, :, None]), 0.0)
        update = jnp.einsum(
            "hqk,khd->hqd",
            probs.astype(jnp.bfloat16),
            split_heads(value_block),
            preferred_element_type=jnp.float32,
        )
        return (
            (
                top,
                run_sum * correct + jnp.sum(probs, axis=-1),
                run_acc * correct[:, :, None] + update,
            ),
            None,
        )

    return step


def per_device(
    tokens,
    segment_ids,
    qkv_weight,
    out_weight,
    up_weight,
    down_weight,
    gain_first,
    gain_second,
    out_cotangent,
):
    seqs_here = tokens.shape[0]
    tok_rows = tokens.shape[1]
    width = tokens.shape[2]
    my_seg = lax.dynamic_slice_in_dim(segment_ids, lax.axis_index("band") * tok_rows, tok_rows, 1)
    valid = (my_seg >= 0).astype(jnp.float32)[:, :, None]
    qkv_full, out_full, up_full, down_full, gain_one, gain_two = (
        lax.all_gather(qkv_weight, "seq", axis=0, tiled=True),
        lax.all_gather(out_weight, "seq", axis=0, tiled=True),
        lax.all_gather(up_weight, "seq", axis=0, tiled=True),
        lax.all_gather(down_weight, "seq", axis=0, tiled=True),
        lax.all_gather(gain_first, "seq", axis=0, tiled=True),
        lax.all_gather(gain_second, "seq", axis=0, tiled=True),
    )
    gain_one = gain_one.astype(jnp.float32)
    gain_two = gain_two.astype(jnp.float32)
    inputs = tokens.astype(jnp.float32)
    first_h, first_n, first_s = layer_norm(inputs, gain_one)
    first_low = first_h.astype(jnp.bfloat16)
    qkv_rows = jnp.einsum(
        "std,de->ste", first_low, qkv_full, preferred_element_type=jnp.float32
    ).astype(jnp.bfloat16)
    query_rows = qkv_rows[:, :, :width]
    key_rows = qkv_rows[:, :, width : 2 * width]
    value_rows = qkv_rows[:, :, 2 * width :]
    query_heads = split_heads(query_rows)

    def online(carry, pieces):
        key_piece, value_piece = pieces
        count = key_piece.shape[1]
        sub = math.gcd(count, 4 * tok_rows)
        results = []
        for member in range(seqs_here):
            state = (carry[0][member], carry[1][member], carry[2][member])
            stacked = (
                key_piece[member].reshape(count // sub, sub, width),
                value_piece[member].reshape(count // sub, sub, width),
                segment_ids[member].reshape(count // sub, sub),
            )
            state, _ = lax.scan(online_step(query_heads[member], my_seg[member]), state, stacked)
            results.append(state)
        return tuple((jnp.stack([result[part] for result in results]) for part in range(3)))

    start_state = (
        jnp.full((seqs_here, HEADS, tok_rows), NEG, jnp.float32),
        jnp.zeros((seqs_here, HEADS, tok_rows), jnp.float32),
        jnp.zeros((seqs_here, HEADS, tok_rows, HEAD_DIM), jnp.float32),
    )
    run_max, run_sum, run_acc = online(
        start_state,
        (
            lax.all_gather(key_rows, "band", axis=1, tiled=True),
            lax.all_gather(value_rows, "band", axis=1, tiled=True),
        ),
    )
    log_norm = run_max + jnp.log(run_sum)
    attn_heads = jnp.transpose(run_acc / run_sum[:, :, :, None], (0, 2, 1, 3))
    attn_rows = attn_heads.reshape(seqs_here, tok_rows, width)
    attn_low = attn_rows.astype(jnp.bfloat16)
    resid = inputs + valid * jnp.einsum(
        "std,de->ste", attn_low, out_full, preferred_element_type=jnp.float32
    )
    second_h, second_n, second_s = layer_norm(resid, gain_two)
    second_low = second_h.astype(jnp.bfloat16)
    pre_act = jnp.einsum("std,df->stf", second_low, up_full, preferred_element_type=jnp.float32)
    hidden_low = jax.nn.gelu(pre_act, approximate=False).astype(jnp.bfloat16)
    branch_two = jnp.einsum(
        "stf,fd->std", hidden_low, down_full, preferred_element_type=jnp.float32
    )
    layer_out = (resid + valid * branch_two).astype(jnp.bfloat16)
    grad_out = out_cotangent.astype(jnp.float32)
    grad_two = (valid * grad_out).astype(jnp.bfloat16)
    down_grad = jnp.einsum("stf,std->fd", hidden_low, grad_two, preferred_element_type=jnp.float32)
    hidden_grad = jnp.einsum("std,fd->stf", grad_two, down_full, preferred_element_type=jnp.float32)
    slope = 0.5 * (1.0 + lax.erf(pre_act * ROOT_HALF)) + pre_act * DENSITY * jnp.exp(
        -0.5 * pre_act * pre_act
    )
    pre_grad = (hidden_grad * slope).astype(jnp.bfloat16)
    up_grad = jnp.einsum("std,stf->df", second_low, pre_grad, preferred_element_type=jnp.float32)
    second_grad = jnp.einsum("stf,df->std", pre_grad, up_full, preferred_element_type=jnp.float32)
    norm_grad, gain_two_grad = norm_back(second_grad, gain_two, second_n, second_s)
    resid_grad = grad_out + norm_grad
    branch_grad = (valid * resid_grad).astype(jnp.bfloat16)
    outproj_grad = jnp.einsum(
        "std,ste->de", attn_low, branch_grad, preferred_element_type=jnp.float32
    )
    attn_grad = jnp.einsum(
        "ste,de->std", branch_grad, out_full, preferred_element_type=jnp.float32
    ).astype(jnp.bfloat16)
    dout_heads = split_heads(attn_grad)
    delta = jnp.transpose(jnp.sum(dout_heads.astype(jnp.float32) * attn_heads, axis=-1), (0, 2, 1))
    key_all, value_all = (
        lax.all_gather(key_rows, "band", axis=1, tiled=True),
        lax.all_gather(value_rows, "band", axis=1, tiled=True),
    )
    seq_len = key_all.shape[1]
    sub_all = math.gcd(seq_len, 4 * tok_rows)
    query_parts = []
    for member in range(seqs_here):
        blocks_all = (
            key_all[member].reshape(seq_len // sub_all, sub_all, width),
            value_all[member].reshape(seq_len // sub_all, sub_all, width),
            segment_ids[member].reshape(seq_len // sub_all, sub_all),
        )
        query_part = query_heads[member]
        dout_part = dout_heads[member]
        lse_part = log_norm[member]
        delta_part = delta[member]
        seg_part = my_seg[member]

        def query_step(
            total,
            item,
            query_part=query_part,
            dout_part=dout_part,
            lse_part=lse_part,
            delta_part=delta_part,
            seg_part=seg_part,
        ):
            key_block, value_block, seg_block = item
            scores, mask = masked_scores(query_part, split_heads(key_block), seg_part, seg_block)
            probs = jnp.where(mask, jnp.exp(scores - lse_part[:, :, None]), 0.0)
            prob_grad = jnp.einsum(
                "qhd,khd->hqk",
                dout_part,
                split_heads(value_block),
                preferred_element_type=jnp.float32,
            )
            score_grad = (probs * (prob_grad - delta_part[:, :, None])).astype(jnp.bfloat16)
            return (
                total
                + jnp.einsum(
                    "hqk,khd->qhd",
                    score_grad,
                    split_heads(key_block),
                    preferred_element_type=jnp.float32,
                ),
                None,
            )

        member_grad, _ = lax.scan(
            query_step, jnp.zeros((tok_rows, HEADS, HEAD_DIM), jnp.float32), blocks_all
        )
        query_parts.append(member_grad)
    query_grad = (jnp.stack(query_parts) * HEAD_DIM ** (-0.5)).reshape(seqs_here, tok_rows, width)
    count = lax.axis_size("band") * tok_rows
    sub = math.gcd(count, 4 * tok_rows)
    columns = []
    for member in range(seqs_here):
        key_part = key_all[member]
        value_part = value_all[member]
        seg_part = segment_ids[member]

        def one_block(item, member=member):
            key_block, value_block, seg_block = item
            key_grad, value_grad = key_terms(
                query_heads[member],
                dout_heads[member],
                log_norm[member],
                delta[member],
                my_seg[member],
                split_heads(key_block),
                split_heads(value_block),
                seg_block,
            )
            return jnp.concatenate(
                [key_grad.reshape(sub, width), value_grad.reshape(sub, width)], axis=-1
            )

        stacked = (
            key_part.reshape(count // sub, sub, width),
            value_part.reshape(count // sub, sub, width),
            seg_part.reshape(count // sub, sub),
        )
        columns.append(lax.map(one_block, stacked).reshape(count, 2 * width))
    both_grads = lax.psum_scatter(
        jnp.stack(columns, axis=1).astype(jnp.bfloat16), "band", scatter_dimension=0, tiled=True
    ).astype(jnp.float32)
    both_grads = jnp.transpose(both_grads, (1, 0, 2))
    key_grad = both_grads[:, :, :width]
    value_grad = both_grads[:, :, width:]
    qkv_grad_low = jnp.concatenate([query_grad, key_grad, value_grad], axis=-1).astype(jnp.bfloat16)
    qkv_grad = jnp.einsum(
        "std,ste->de", first_low, qkv_grad_low, preferred_element_type=jnp.float32
    )
    first_grad = jnp.einsum(
        "ste,de->std", qkv_grad_low, qkv_full, preferred_element_type=jnp.float32
    )
    in_grad, gain_one_grad = norm_back(first_grad, gain_one, first_n, first_s)
    token_grad = resid_grad + in_grad
    shares = (
        lax.psum_scatter(
            qkv_grad.astype(jnp.bfloat16), "seq", scatter_dimension=0, tiled=True
        ).astype(jnp.float32),
        lax.psum_scatter(
            outproj_grad.astype(jnp.bfloat16), "seq", scatter_dimension=0, tiled=True
        ).astype(jnp.float32),
        lax.psum_scatter(
            up_grad.astype(jnp.bfloat16), "seq", scatter_dimension=0, tiled=True
        ).astype(jnp.float32),
        lax.psum_scatter(
            down_grad.astype(jnp.bfloat16), "seq", scatter_dimension=0, tiled=True
        ).astype(jnp.float32),
        lax.psum_scatter(
            gain_one_grad.astype(jnp.bfloat16), "seq", scatter_dimension=0, tiled=True
        ).astype(jnp.float32),
        lax.psum_scatter(
            gain_two_grad.astype(jnp.bfloat16), "seq", scatter_dimension=0, tiled=True
        ).astype(jnp.float32),
    )
    summed = (
        lax.psum(shares[0].astype(jnp.bfloat16), "band").astype(jnp.float32),
        lax.psum(shares[1].astype(jnp.bfloat16), "band").astype(jnp.float32),
        lax.psum(shares[2].astype(jnp.bfloat16), "band").astype(jnp.float32),
        lax.psum(shares[3].astype(jnp.bfloat16), "band").astype(jnp.float32),
        lax.psum(shares[4].astype(jnp.bfloat16), "band").astype(jnp.float32),
        lax.psum(shares[5].astype(jnp.bfloat16), "band").astype(jnp.float32),
    )
    qkv_out, outproj_out, up_out, down_out, gain_one_out, gain_two_out = summed
    return (
        layer_out,
        token_grad,
        qkv_out,
        outproj_out,
        up_out,
        down_out,
        gain_one_out,
        gain_two_out,
    )


MESH = pl.DeviceIdType.MESH
BF = jnp.bfloat16
F32 = jnp.float32
SCALE = HEAD_DIM ** (-0.5)


def place():
    b = lax.axis_index("band")
    y = lax.axis_index("seq")
    return b, y, b // 4, (b // 2) % 2, b % 2


def meet(peers):
    sem = pltpu.get_barrier_semaphore()
    for peer in peers:
        pl.semaphore_signal(sem, inc=1, device_id=peer, device_id_type=MESH)
    pl.semaphore_wait(sem, len(peers))


def send(src, dst, ssem, rsem, peer):
    copy = pltpu.make_async_remote_copy(
        src_ref=src, dst_ref=dst, send_sem=ssem, recv_sem=rsem, device_id=peer, device_id_type=MESH
    )
    copy.start()
    return copy


def comm_call(body, name, cid, outs, scratch, n_in):
    vm = pl.BlockSpec(memory_space=pltpu.VMEM)
    return pl.pallas_call(
        body,
        out_shape=[jax.ShapeDtypeStruct(s, d) for s, d in outs],
        in_specs=[vm] * n_in,
        out_specs=[vm] * len(outs),
        scratch_shapes=scratch,
        compiler_params=pltpu.CompilerParams(collective_id=cid, has_side_effects=True),
        name=name,
    )


def dma(n):
    return pltpu.SemaphoreType.DMA((n,))


def norm_rows(v):
    centre = v - jnp.mean(v, axis=-1, keepdims=True)
    inv_std = lax.rsqrt(jnp.mean(centre * centre, axis=-1, keepdims=True) + EPS)
    return centre * inv_std, inv_std


def open_body(tok, seg, wqkv, gains, tok_all, seg_all, w_sel, gains_all, ss, rs):
    b, y, z, x, c = place()
    core, over = (b + 1 - 2 * c, y), (b, 1 - y)
    meet([core, over])
    cps = []
    for m in range(2):
        cps.append(send(tok.at[m], tok_all.at[2 * y + m, c], ss.at[m], rs.at[m], over))
    cps.append(send(seg, seg_all.at[y], ss.at[2], rs.at[2], over))
    cps.append(send(gains, gains_all.at[y], ss.at[3], rs.at[3], over))
    k = 4
    far = (1 - y) * 2 + c
    own = y * 2 + c
    for hp in range(2):
        for p in range(3):
            col = pl.multiple_of(p * 1024 + far * 256 + hp * 128, 128)
            dst = w_sel.at[y, :, pl.ds(hp * 384 + p * 128, 128)]
            cps.append(send(wqkv.at[:, pl.ds(col, 128)], dst, ss.at[k], rs.at[k], over))
            k += 1
    side = []
    for m in range(2):
        side.append(send(tok.at[m], tok_all.at[2 * y + m, c], ss.at[k], rs.at[k], core))
        k += 1
    for hp in range(2):
        for p in range(3):
            col = pl.multiple_of(p * 1024 + own * 256 + hp * 128, 128)
            w_sel[y, :, hp * 384 + p * 128 : hp * 384 + p * 128 + 128] = wqkv[:, pl.ds(col, 128)]
    for m in range(2):
        tok_all[2 * y + m, c] = tok[m]
    seg_all[y] = seg[...]
    gains_all[y] = gains[...]
    for m in range(2):
        cps[m].wait_recv()
        got = tok_all.at[2 * (1 - y) + m, c]
        side.append(send(got, got, ss.at[k], rs.at[k], core))
        k += 1
    for m in range(2):
        cps[m].wait_send()
    for cp in cps[2:] + side:
        cp.wait()


def open_call(tok, seg, wqkv, gains):
    return comm_call(
        open_body,
        "open_column",
        1,
        [((4, 2, 96, 1024), BF), ((2, 2, 1536), jnp.int32), ((2, 512, 768), BF), ((2, 8, 512), F32)],
        [dma(14), dma(14)],
        4,
    )(tok, seg, wqkv, gains)


def chips(b, c, y):
    j = b // 2
    res = []
    for k in range(1, 8):
        jd = (j + k) % 8
        res.append((jd, (jd * 2 + c, y)))
    return res


def to_heads_body(qkv, up, att, up_sel, ss, rs):
    b, y, z, x, c = place()
    over = (b, 1 - y)
    others = chips(b, c, y)
    meet([over] + [peer for _, peer in others])
    j = b // 2
    cps = []
    far = pl.multiple_of(((1 - y) * 2 + c) * 1024, 1024)
    own = pl.multiple_of((y * 2 + c) * 1024, 1024)
    cps.append(send(up.at[:, pl.ds(far, 1024)], up_sel.at[y], ss.at[0], rs.at[0], over))
    for k, (jd, peer) in enumerate(others):
        col = pl.multiple_of((jd % 2) * 384, 128)
        cps.append(
            send(qkv.at[jd // 2, :, pl.ds(col, 384)], att.at[j], ss.at[k + 1], rs.at[k + 1], peer)
        )
    att[j] = qkv[z, :, pl.ds(pl.multiple_of(x * 384, 128), 384)]
    up_sel[y] = up[:, pl.ds(own, 1024)]
    for cp in cps:
        cp.wait()


def to_heads(qkv, up):
    return comm_call(
        to_heads_body,
        "to_heads",
        2,
        [((8, 192, 384), BF), ((2, 512, 1024), BF)],
        [dma(8), dma(8)],
        2,
    )(qkv, up)


def from_heads_body(attn, cot, rows, cot_all, ss, rs):
    b, y, z, x, c = place()
    core, over = (b + 1 - 2 * c, y), (b, 1 - y)
    others = chips(b, c, y)
    meet([core, over] + [peer for _, peer in others])
    col = pl.multiple_of(x * 128, 128)
    cps, side = [], []
    for k, (jd, peer) in enumerate(others):
        cps.append(send(attn.at[jd], rows.at[z, :, pl.ds(col, 128)], ss.at[k], rs.at[k], peer))
    k = 7
    near = []
    for m in range(2):
        near.append(send(cot.at[m], cot_all.at[2 * y + m, c], ss.at[k], rs.at[k], over))
        k += 1
    for m in range(2):
        side.append(send(cot.at[m], cot_all.at[2 * y + m, c], ss.at[k], rs.at[k], core))
        k += 1
    rows[z, :, pl.ds(col, 128)] = attn[b // 2]
    for m in range(2):
        cot_all[2 * y + m, c] = cot[m]
    for m in range(2):
        near[m].wait_recv()
        got = cot_all.at[2 * (1 - y) + m, c]
        side.append(send(got, got, ss.at[k], rs.at[k], core))
        k += 1
    for cp in near:
        cp.wait_send()
    for cp in cps + side:
        cp.wait()


def from_heads(attn, cot):
    return comm_call(
        from_heads_body,
        "from_heads",
        3,
        [((4, 192, 256), BF), ((4, 2, 96, 1024), BF)],
        [dma(13), dma(13)],
        2,
    )(attn, cot)


def column_sum(part, got, mid, fin, ss, rs, b, y, c):
    core, over = (b + 1 - 2 * c, y), (b, 1 - y)
    first = []
    for m in range(2):
        q = 2 * (1 - y) + m
        first.append(send(part.at[q, 1 - c], got.at[q], ss.at[m], rs.at[m], core))
    for m in range(2):
        q = 2 * y + m
        first.append(send(part.at[q, 1 - c], got.at[q], ss.at[2 + m], rs.at[2 + m], core))
    second = []
    for m in range(2):
        q = 2 * (1 - y) + m
        first[m].wait_recv()
        mid[m] = (part[q, c].astype(F32) + got[q].astype(F32)).astype(BF)
        second.append(send(mid.at[m], fin.at[m], ss.at[4 + m], rs.at[4 + m], over))
    sums = []
    for m in range(2):
        q = 2 * y + m
        first[2 + m].wait_recv()
        second[m].wait_recv()
        sums.append(part[q, c].astype(F32) + got[q].astype(F32) + fin[m].astype(F32))
    for cp in first + second:
        cp.wait_send()
    return sums


def column_spread(own, full, ss, rs, k, b, y, c):
    core, over = (b + 1 - 2 * c, y), (b, 1 - y)
    near, side = [], []
    for m in range(2):
        near.append(send(own.at[m], full.at[2 * y + m, c], ss.at[k], rs.at[k], over))
        side.append(send(own.at[m], full.at[2 * y + m, c], ss.at[k + 1], rs.at[k + 1], core))
        k += 2
    for m in range(2):
        full[2 * y + m, c] = own[m]
    for m in range(2):
        near[m].wait_recv()
        got = full.at[2 * (1 - y) + m, c]
        side.append(send(got, got, ss.at[k], rs.at[k], core))
        k += 1
    for cp in near:
        cp.wait_send()
    for cp in side:
        cp.wait()


SUM_SCRATCH = [
    pltpu.VMEM((4, 96, 1024), BF),
    pltpu.VMEM((2, 96, 1024), BF),
    pltpu.VMEM((2, 96, 1024), BF),
]


def second_norm_body(part, tok, valid, gain, resid, h_all, got, mid, fin, own, ss, rs):
    b, y, z, x, c = place()
    meet([(b + 1 - 2 * c, y), (b, 1 - y)])
    sums = column_sum(part, got, mid, fin, ss, rs, b, y, c)
    for m in range(2):
        res = tok[m].astype(F32) + valid[m][:, :1] * sums[m]
        resid[m] = res
        normed, _ = norm_rows(res)
        own[m] = (normed * gain[1:2]).astype(BF)
    column_spread(own, h_all, ss, rs, 6, b, y, c)


def second_norm(part, tok, valid, gain):
    return comm_call(
        second_norm_body,
        "second_norm",
        4,
        [((2, 96, 1024), F32), ((4, 2, 96, 1024), BF)],
        SUM_SCRATCH + [pltpu.VMEM((2, 96, 1024), BF), dma(12), dma(12)],
        4,
    )(part, tok, valid, gain)


def second_back_body(part, resid, cot, valid, gain, rgrad, ggrad, br_all, got, mid, fin, own, ss, rs):
    b, y, z, x, c = place()
    meet([(b + 1 - 2 * c, y), (b, 1 - y)])
    sums = column_sum(part, got, mid, fin, ss, rs, b, y, c)
    total = jnp.zeros((1, 1024), F32)
    for m in range(2):
        normed, inv_std = norm_rows(resid[m])
        e = sums[m]
        g = e * gain[1:2]
        total = total + jnp.sum(e * normed, axis=0, keepdims=True)
        one = jnp.mean(g, axis=-1, keepdims=True)
        two = jnp.mean(g * normed, axis=-1, keepdims=True)
        rg = cot[m].astype(F32) + (g - one - normed * two) * inv_std
        rgrad[m] = rg
        own[m] = (valid[m][:, :1] * rg).astype(BF)
    ggrad[...] = jnp.broadcast_to(total, (8, 1024))
    column_spread(own, br_all, ss, rs, 6, b, y, c)


def second_back(part, resid, cot, valid, gain):
    return comm_call(
        second_back_body,
        "second_back",
        5,
        [((2, 96, 1024), F32), ((8, 1024), F32), ((4, 2, 96, 1024), BF)],
        SUM_SCRATCH + [pltpu.VMEM((2, 96, 1024), BF), dma(12), dma(12)],
        5,
    )(part, resid, cot, valid, gain)


def grad_heads_body(agrad, part, resid, valid, do, out, got, mid, fin, ss, rs):
    b, y, z, x, c = place()
    others = chips(b, c, y)
    meet([(b + 1 - 2 * c, y), (b, 1 - y)] + [peer for _, peer in others])
    j = b // 2
    cps = []
    for k, (jd, peer) in enumerate(others):
        col = pl.multiple_of((jd % 2) * 128, 128)
        cps.append(
            send(agrad.at[jd // 2, :, pl.ds(col, 128)], do.at[j], ss.at[6 + k], rs.at[6 + k], peer)
        )
    do[j] = agrad[z, :, pl.ds(pl.multiple_of(x * 128, 128), 128)]
    sums = column_sum(part, got, mid, fin, ss, rs, b, y, c)
    for m in range(2):
        out[m] = (resid[m] + valid[m][:, :1] * sums[m]).astype(BF)
    for cp in cps:
        cp.wait()


def grad_heads(agrad, part, resid, valid):
    return comm_call(
        grad_heads_body,
        "grad_heads",
        6,
        [((8, 192, 128), BF), ((2, 96, 1024), BF)],
        SUM_SCRATCH + [dma(13), dma(13)],
        4,
    )(agrad, part, resid, valid)


def grad_rows_body(dqkv, rows, ss, rs):
    b, y, z, x, c = place()
    others = chips(b, c, y)
    meet([peer for _, peer in others])
    col = pl.multiple_of(x * 384, 128)
    cps = []
    for k, (jd, peer) in enumerate(others):
        cps.append(send(dqkv.at[jd], rows.at[z, :, pl.ds(col, 384)], ss.at[k], rs.at[k], peer))
    rows[z, :, pl.ds(col, 384)] = dqkv[b // 2]
    for cp in cps:
        cp.wait()


def grad_rows(dqkv):
    return comm_call(
        grad_rows_body, "grad_rows", 7, [((4, 192, 768), BF)], [dma(7), dma(7)], 1
    )(dqkv)[0]


def first_back_body(part, tok, rgrad, gain, tgrad, ggrad, got, mid, fin, ss, rs):
    b, y, z, x, c = place()
    meet([(b + 1 - 2 * c, y), (b, 1 - y)])
    sums = column_sum(part, got, mid, fin, ss, rs, b, y, c)
    total = jnp.zeros((1, 1024), F32)
    for m in range(2):
        normed, inv_std = norm_rows(tok[m].astype(F32))
        e = sums[m]
        g = e * gain[0:1]
        total = total + jnp.sum(e * normed, axis=0, keepdims=True)
        one = jnp.mean(g, axis=-1, keepdims=True)
        two = jnp.mean(g * normed, axis=-1, keepdims=True)
        tgrad[m] = rgrad[m] + (g - one - normed * two) * inv_std
    ggrad[...] = jnp.broadcast_to(total, (8, 1024))


def first_back(part, tok, rgrad, gain):
    return comm_call(
        first_back_body,
        "first_back",
        8,
        [((2, 96, 1024), F32), ((8, 1024), F32)],
        SUM_SCRATCH + [dma(6), dma(6)],
        4,
    )(part, tok, rgrad, gain)


def last_dot(a, b):
    return lax.dot_general(a, b, (((1,), (1,)), ((), ())), preferred_element_type=F32)


def plain_dot(a, b):
    return lax.dot_general(a, b, (((1,), (0,)), ((), ())), preferred_element_type=F32)


def attend_body(qkv, seg_col, seg_row, out_low, out, lse):
    rows = out.shape[0]
    i = pl.program_id(0)
    at = pl.multiple_of(i * rows, rows)
    q = qkv[pl.ds(at, rows), 0:128]
    keys = qkv[:, 128:256]
    values = qkv[:, 256:384]
    low_half = lax.broadcasted_iota(jnp.int32, (rows, 128), 1) < HEAD_DIM
    mask = seg_col[:, 0:1] == seg_row[0:1, :]
    outs, norms = [], []
    for h in range(2):
        qh = jnp.where(low_half if h == 0 else ~low_half, q * SCALE, 0.0).astype(BF)
        scores = jnp.where(mask, last_dot(qh, keys), NEG)
        top = jnp.max(scores, axis=-1, keepdims=True)
        probs = jnp.exp(scores - top)
        total = jnp.sum(probs, axis=-1, keepdims=True)
        outs.append(plain_dot(probs.astype(BF), values) / total)
        norms.append(top + jnp.log(total))
    res = jnp.where(low_half, outs[0], outs[1])
    out[...] = res
    out_low[...] = res.astype(BF)
    lse[...] = jnp.where(low_half, norms[0], norms[1])


def attend(qkv, seg_col, seg_row):
    length = qkv.shape[0]
    rows = 256
    tile = pl.BlockSpec((rows, 128), lambda i: (i, 0))
    return pl.pallas_call(
        attend_body,
        grid=(length // rows,),
        in_specs=[
            pl.BlockSpec((length, 384), lambda i: (0, 0)),
            pl.BlockSpec((rows, 128), lambda i: (i, 0)),
            pl.BlockSpec((8, length), lambda i: (0, 0)),
        ],
        out_specs=[tile, tile, tile],
        out_shape=[
            jax.ShapeDtypeStruct((length, 128), BF),
            jax.ShapeDtypeStruct((length, 128), F32),
            jax.ShapeDtypeStruct((length, 128), F32),
        ],
        name="attend",
    )(qkv, seg_col, seg_row)


def attend_back_body(qkv, out, lse, do, seg_col, seg_row, dqkv, lse_t, delta, keys_t, dq_t):
    length = qkv.shape[0]
    rows = seg_col.shape[0]
    i = pl.program_id(0)
    at = pl.multiple_of(i * rows, rows)

    @pl.when(i == 0)
    def _():
        lse_t[...] = jnp.transpose(lse[...])
        prod = jnp.transpose(do[...].astype(F32) * out[...])
        delta[0:8] = jnp.broadcast_to(jnp.sum(prod[:HEAD_DIM], axis=0, keepdims=True), (8, length))
        delta[8:16] = jnp.broadcast_to(jnp.sum(prod[HEAD_DIM:], axis=0, keepdims=True), (8, length))
        keys_t[...] = jnp.transpose(qkv[:, 128:256].astype(F32)).astype(BF)
        dq_t[...] = jnp.zeros_like(dq_t)

    keys = qkv[pl.ds(at, rows), 128:256]
    values = qkv[pl.ds(at, rows), 256:384]
    q = qkv[:, 0:128]
    douts = do[...]
    low_half = lax.broadcasted_iota(jnp.int32, (rows, 128), 1) < HEAD_DIM
    low_rows = lax.broadcasted_iota(jnp.int32, (128, 1), 0) < HEAD_DIM
    mask = seg_col[:, 0:1] == seg_row[0:1, :]
    kgrads, vgrads, qgrads = [], [], []
    for h in range(2):
        pick = low_half if h == 0 else ~low_half
        kh = jnp.where(pick, keys * SCALE, 0.0).astype(BF)
        vh = jnp.where(pick, values, 0.0).astype(BF)
        scores = last_dot(kh, q)
        probs = jnp.where(mask, jnp.exp(scores - lse_t[h * HEAD_DIM : h * HEAD_DIM + 1]), 0.0)
        vgrads.append(plain_dot(probs.astype(BF), douts))
        pgrad = last_dot(vh, douts)
        sgrad = (probs * (pgrad - delta[h * 8 : h * 8 + 1])).astype(BF)
        kgrads.append(plain_dot(sgrad, q))
        qgrads.append(plain_dot(keys_t[:, pl.ds(at, rows)], sgrad))
    dq_t[...] += jnp.where(low_rows, qgrads[0], qgrads[1])
    dqkv[pl.ds(at, rows), 128:256] = (jnp.where(low_half, kgrads[0], kgrads[1]) * SCALE).astype(BF)
    dqkv[pl.ds(at, rows), 256:384] = jnp.where(low_half, vgrads[0], vgrads[1]).astype(BF)

    @pl.when(i == pl.num_programs(0) - 1)
    def _():
        dqkv[:, 0:128] = (jnp.transpose(dq_t[...]) * SCALE).astype(BF)


def attend_back(qkv, out, lse, do, seg_col, seg_row):
    length = qkv.shape[0]
    rows = 256
    whole = pl.BlockSpec((length, 128), lambda i: (0, 0))
    wide = pl.BlockSpec((length, 384), lambda i: (0, 0))
    return pl.pallas_call(
        attend_back_body,
        grid=(length // rows,),
        in_specs=[
            wide,
            whole,
            whole,
            whole,
            pl.BlockSpec((rows, 128), lambda i: (i, 0)),
            pl.BlockSpec((8, length), lambda i: (0, 0)),
        ],
        out_specs=wide,
        out_shape=jax.ShapeDtypeStruct((length, 384), BF),
        scratch_shapes=[
            pltpu.VMEM((128, length), F32),
            pltpu.VMEM((16, length), F32),
            pltpu.VMEM((128, length), BF),
            pltpu.VMEM((128, length), F32),
        ],
        name="attend_back",
    )(qkv, out, lse, do, seg_col, seg_row)


def flip(v, bit):
    return lax.ppermute(v, "band", [(i, i ^ bit) for i in range(16)])


def keep_half(v, bit_value, bit):
    half = v.shape[1] // 2
    mine = lax.dynamic_slice_in_dim(v, bit_value * half, half, 1)
    theirs = lax.dynamic_slice_in_dim(v, (1 - bit_value) * half, half, 1)
    return mine.astype(F32) + flip(theirs.astype(BF), bit).astype(F32)


def join_half(v, bit_value, bit):
    other = flip(v, bit)
    return jnp.where(
        bit_value == 0,
        jnp.concatenate([v, other], axis=1),
        jnp.concatenate([other, v], axis=1),
    )


def reduce_columns(v, halves):
    b, y, z, x, c = place()
    bits = ((x, 2), (z % 2, 4), (z // 2, 8))
    for value, bit in bits:
        v = keep_half(v, value, bit)
    v = v.astype(BF)
    if halves:
        mine = lax.dynamic_slice_in_dim(v, y, 1, 0)
        theirs = lax.ppermute(lax.dynamic_slice_in_dim(v, 1 - y, 1, 0), "seq", [(0, 1), (1, 0)])
        v = jnp.where(
            y == 0, jnp.concatenate([mine, theirs], 0), jnp.concatenate([theirs, mine], 0)
        )
    for value, bit in reversed(bits):
        v = join_half(v, value, bit)
    v = v[None]
    other = flip(v, 1)
    return jnp.where(c == 0, jnp.concatenate([v, other], 0), jnp.concatenate([other, v], 0))


def column_device(
    tokens,
    segment_ids,
    qkv_weight,
    out_weight,
    up_weight,
    down_weight,
    gain_first,
    gain_second,
    out_cotangent,
):
    b, y, z, x, c = place()
    my_seg = lax.dynamic_slice_in_dim(segment_ids, b * 96, 96, 1)
    valid = jnp.broadcast_to((my_seg >= 0).astype(F32)[:, :, None], (2, 96, 128))
    gains = jnp.pad(jnp.stack([gain_first, gain_second]).astype(F32), ((0, 6), (0, 0)))
    tok_all, seg_all, w_sel, gains_all = open_call(tokens, segment_ids, qkv_weight, gains)
    gain = jnp.transpose(gains_all, (1, 0, 2)).reshape(8, 1024)
    seg_all = seg_all.reshape(4, 1536)
    seg_z = lax.dynamic_slice_in_dim(seg_all, z, 1, 0)
    seg_row = jnp.broadcast_to(seg_z, (8, 1536))
    seg_col = jnp.broadcast_to(seg_z.reshape(1536, 1), (1536, 128))
    seg_here = lax.dynamic_slice_in_dim(seg_all, (z * 2 + x) * 192, 192, 1)
    valid_all = (seg_here >= 0).astype(F32).reshape(768, 1)
    w_sel = w_sel.reshape(1024, 768)
    normed, _ = norm_rows(tok_all.reshape(768, 1024).astype(F32))
    h_one = (normed * gain[0:1]).astype(BF)
    qkv = plain_dot(h_one, w_sel).astype(BF)
    att, up_sel = to_heads(qkv.reshape(4, 192, 768), up_weight)
    up_sel = up_sel.reshape(1024, 1024)
    att = att.reshape(1536, 384)
    out_low, out_full, lse = attend(att, seg_col, seg_row)
    attn_low, cot_all = from_heads(out_low.reshape(8, 192, 128), out_cotangent)
    attn_low = attn_low.reshape(768, 256)
    out_rows = lax.dynamic_slice_in_dim(out_weight, c * 256, 256, 0)
    part = plain_dot(attn_low, out_rows).astype(BF)
    resid, h_two = second_norm(part.reshape(4, 2, 96, 1024), tokens, valid, gain)
    h_two = h_two.reshape(768, 1024)
    pre_act = plain_dot(h_two, up_sel)
    hidden_low = jax.nn.gelu(pre_act, approximate=False).astype(BF)
    down_rows = lax.dynamic_slice_in_dim(down_weight, c * 1024, 1024, 0)
    grad_two = (valid_all * cot_all.reshape(768, 1024).astype(F32)).astype(BF)
    hidden_grad = last_dot(grad_two, down_rows)
    slope = 0.5 * (1.0 + lax.erf(pre_act * ROOT_HALF)) + pre_act * DENSITY * jnp.exp(
        -0.5 * pre_act * pre_act
    )
    pre_grad = (hidden_grad * slope).astype(BF)
    e_part = last_dot(pre_grad, up_sel).astype(BF)
    rgrad, gain_two_grad, branch = second_back(
        e_part.reshape(4, 2, 96, 1024), resid, out_cotangent, valid, gain
    )
    branch = branch.reshape(768, 1024)
    branch_two = plain_dot(hidden_low, down_rows).astype(BF)
    first_dot = lambda a, d: lax.dot_general(
        a, d, (((0,), (0,)), ((), ())), preferred_element_type=F32
    )
    down_grad = first_dot(hidden_low, grad_two)
    up_grad = first_dot(h_two, pre_grad)
    down_sum = reduce_columns(down_grad.reshape(1, 1024, 1024), False)
    up_sum = reduce_columns(up_grad.reshape(2, 512, 1024), True)
    attn_grad = last_dot(branch, out_rows).astype(BF)
    do, layer_out = grad_heads(
        attn_grad.reshape(4, 192, 256), branch_two.reshape(4, 2, 96, 1024), resid, valid
    )
    outproj_grad = first_dot(attn_low, branch)
    out_sum = reduce_columns(outproj_grad.reshape(1, 256, 1024), False)
    dqkv = attend_back(att, out_full, lse, do.reshape(1536, 128), seg_col, seg_row)
    dqkv_rows = grad_rows(dqkv.reshape(8, 192, 384)).reshape(768, 768)
    c_part = last_dot(dqkv_rows, w_sel).astype(BF)
    token_grad, gain_one_grad = first_back(c_part.reshape(4, 2, 96, 1024), tokens, rgrad, gain)
    qkv_grad = first_dot(h_one, dqkv_rows)
    qkv_sum = reduce_columns(qkv_grad.reshape(2, 512, 768), True)
    both = lax.psum(jnp.stack([gain_one_grad[0], gain_two_grad[0]]), ("band", "seq"))
    gain_out = lax.dynamic_slice_in_dim(both, y * 512, 512, 1)
    qkv_out = jnp.transpose(qkv_sum.reshape(2, 2, 512, 2, 3, 128), (2, 4, 1, 0, 3, 5))
    up_out = jnp.transpose(up_sum, (2, 1, 0, 3))
    return (
        layer_out,
        token_grad,
        qkv_out.reshape(512, 3072).astype(F32),
        out_sum.reshape(512, 1024).astype(F32),
        up_out.reshape(512, 4096).astype(F32),
        down_sum.reshape(2048, 1024).astype(F32),
        gain_out[0],
        gain_out[1],
    )


def solution(mesh):
    placed = (
        P("seq", "band", None),
        P("seq", None),
        P("seq", None),
        P("seq", None),
        P("seq", None),
        P("seq", None),
        P("seq"),
        P("seq"),
        P("seq", "band", None),
    )
    split = dict(mesh.shape) == {"band": 16, "seq": 2}
    return jax.shard_map(
        column_device if split else per_device,
        mesh=mesh,
        in_specs=placed,
        out_specs=(
            P("seq", "band", None),
            P("seq", "band", None),
            P("seq", None),
            P("seq", None),
            P("seq", None),
            P("seq", None),
            P("seq"),
            P("seq"),
        ),
        check_vma=False,
    )
```

```python
import functools
import math

import jax
import jax.numpy as jnp
from jax import lax
from jax.experimental import pallas as pl
from jax.experimental.pallas import tpu as pltpu
from jax.sharding import PartitionSpec as P

HEADS = 16
HEAD_DIM = 64


EPS = 1e-06
NEG = -1e30
ROOT_HALF = 0.7071067811865476
DENSITY = 0.3989422804014327


def layer_norm(values, gain):
    centre = values - jnp.mean(values, axis=-1, keepdims=True)
    inv_std = lax.rsqrt(jnp.mean(centre * centre, axis=-1, keepdims=True) + EPS)
    normed = centre * inv_std
    return (normed * gain, normed, inv_std)


def norm_back(grad_in, gain, normed, inv_std):
    scaled = grad_in * gain
    mean_one = jnp.mean(scaled, axis=-1, keepdims=True)
    mean_two = jnp.mean(scaled * normed, axis=-1, keepdims=True)
    gain_grad = jnp.sum((grad_in * normed).reshape(-1, grad_in.shape[-1]), axis=0)
    return (inv_std * (scaled - mean_one - normed * mean_two), gain_grad)


def split_heads(matrix):
    return matrix.reshape(matrix.shape[:-1] + (HEADS, HEAD_DIM))


def masked_scores(query_part, key_part, query_seg, key_seg):
    scores = jnp.einsum(
        "qhd,khd->hqk", query_part, key_part, preferred_element_type=jnp.float32
    ) * HEAD_DIM ** (-0.5)
    return (scores, (query_seg[:, None] == key_seg[None, :])[None])


def key_terms(
    query_part, dout_part, lse_part, delta_part, query_seg, key_part, value_part, key_seg
):
    scores, mask = masked_scores(query_part, key_part, query_seg, key_seg)
    probs = jnp.where(mask, jnp.exp(scores - lse_part[:, :, None]), 0.0)
    value_grad = jnp.einsum(
        "hqk,qhd->khd", probs.astype(jnp.bfloat16), dout_part, preferred_element_type=jnp.float32
    )
    prob_grad = jnp.einsum(
        "qhd,khd->hqk", dout_part, value_part, preferred_element_type=jnp.float32
    )
    score_grad = (probs * (prob_grad - delta_part[:, :, None])).astype(jnp.bfloat16)
    key_grad = jnp.einsum(
        "hqk,qhd->khd", score_grad, query_part, preferred_element_type=jnp.float32
    ) * HEAD_DIM ** (-0.5)
    return (key_grad, value_grad)


def online_step(query_part, query_seg):

    def step(state, item):
        key_block, value_block, seg_block = item
        run_max, run_sum, run_acc = state
        scores, mask = masked_scores(query_part, split_heads(key_block), query_seg, seg_block)
        masked = jnp.where(mask, scores, NEG)
        top = jnp.maximum(run_max, jnp.max(masked, axis=-1))
        correct = jnp.exp(run_max - top)
        probs = jnp.where(mask, jnp.exp(masked - top[:, :, None]), 0.0)
        update = jnp.einsum(
            "hqk,khd->hqd",
            probs.astype(jnp.bfloat16),
            split_heads(value_block),
            preferred_element_type=jnp.float32,
        )
        return (
            (
                top,
                run_sum * correct + jnp.sum(probs, axis=-1),
                run_acc * correct[:, :, None] + update,
            ),
            None,
        )

    return step


def per_device(
    tokens,
    segment_ids,
    qkv_weight,
    out_weight,
    up_weight,
    down_weight,
    gain_first,
    gain_second,
    out_cotangent,
):
    seqs_here = tokens.shape[0]
    tok_rows = tokens.shape[1]
    width = tokens.shape[2]
    my_seg = lax.dynamic_slice_in_dim(segment_ids, lax.axis_index("band") * tok_rows, tok_rows, 1)
    valid = (my_seg >= 0).astype(jnp.float32)[:, :, None]
    qkv_full, out_full, up_full, down_full, gain_one, gain_two = (
        lax.all_gather(qkv_weight, "seq", axis=0, tiled=True),
        lax.all_gather(out_weight, "seq", axis=0, tiled=True),
        lax.all_gather(up_weight, "seq", axis=0, tiled=True),
        lax.all_gather(down_weight, "seq", axis=0, tiled=True),
        lax.all_gather(gain_first, "seq", axis=0, tiled=True),
        lax.all_gather(gain_second, "seq", axis=0, tiled=True),
    )
    gain_one = gain_one.astype(jnp.float32)
    gain_two = gain_two.astype(jnp.float32)
    inputs = tokens.astype(jnp.float32)
    first_h, first_n, first_s = layer_norm(inputs, gain_one)
    first_low = first_h.astype(jnp.bfloat16)
    qkv_rows = jnp.einsum(
        "std,de->ste", first_low, qkv_full, preferred_element_type=jnp.float32
    ).astype(jnp.bfloat16)
    query_rows = qkv_rows[:, :, :width]
    key_rows = qkv_rows[:, :, width : 2 * width]
    value_rows = qkv_rows[:, :, 2 * width :]
    query_heads = split_heads(query_rows)

    def online(carry, pieces):
        key_piece, value_piece = pieces
        count = key_piece.shape[1]
        sub = math.gcd(count, 4 * tok_rows)
        results = []
        for member in range(seqs_here):
            state = (carry[0][member], carry[1][member], carry[2][member])
            stacked = (
                key_piece[member].reshape(count // sub, sub, width),
                value_piece[member].reshape(count // sub, sub, width),
                segment_ids[member].reshape(count // sub, sub),
            )
            state, _ = lax.scan(online_step(query_heads[member], my_seg[member]), state, stacked)
            results.append(state)
        return tuple((jnp.stack([result[part] for result in results]) for part in range(3)))

    start_state = (
        jnp.full((seqs_here, HEADS, tok_rows), NEG, jnp.float32),
        jnp.zeros((seqs_here, HEADS, tok_rows), jnp.float32),
        jnp.zeros((seqs_here, HEADS, tok_rows, HEAD_DIM), jnp.float32),
    )
    run_max, run_sum, run_acc = online(
        start_state,
        (
            lax.all_gather(key_rows, "band", axis=1, tiled=True),
            lax.all_gather(value_rows, "band", axis=1, tiled=True),
        ),
    )
    log_norm = run_max + jnp.log(run_sum)
    attn_heads = jnp.transpose(run_acc / run_sum[:, :, :, None], (0, 2, 1, 3))
    attn_rows = attn_heads.reshape(seqs_here, tok_rows, width)
    attn_low = attn_rows.astype(jnp.bfloat16)
    resid = inputs + valid * jnp.einsum(
        "std,de->ste", attn_low, out_full, preferred_element_type=jnp.float32
    )
    second_h, second_n, second_s = layer_norm(resid, gain_two)
    second_low = second_h.astype(jnp.bfloat16)
    pre_act = jnp.einsum("std,df->stf", second_low, up_full, preferred_element_type=jnp.float32)
    hidden_low = jax.nn.gelu(pre_act, approximate=False).astype(jnp.bfloat16)
    branch_two = jnp.einsum(
        "stf,fd->std", hidden_low, down_full, preferred_element_type=jnp.float32
    )
    layer_out = (resid + valid * branch_two).astype(jnp.bfloat16)
    grad_out = out_cotangent.astype(jnp.float32)
    grad_two = (valid * grad_out).astype(jnp.bfloat16)
    down_grad = jnp.einsum("stf,std->fd", hidden_low, grad_two, preferred_element_type=jnp.float32)
    hidden_grad = jnp.einsum("std,fd->stf", grad_two, down_full, preferred_element_type=jnp.float32)
    slope = 0.5 * (1.0 + lax.erf(pre_act * ROOT_HALF)) + pre_act * DENSITY * jnp.exp(
        -0.5 * pre_act * pre_act
    )
    pre_grad = (hidden_grad * slope).astype(jnp.bfloat16)
    up_grad = jnp.einsum("std,stf->df", second_low, pre_grad, preferred_element_type=jnp.float32)
    second_grad = jnp.einsum("stf,df->std", pre_grad, up_full, preferred_element_type=jnp.float32)
    norm_grad, gain_two_grad = norm_back(second_grad, gain_two, second_n, second_s)
    resid_grad = grad_out + norm_grad
    branch_grad = (valid * resid_grad).astype(jnp.bfloat16)
    outproj_grad = jnp.einsum(
        "std,ste->de", attn_low, branch_grad, preferred_element_type=jnp.float32
    )
    attn_grad = jnp.einsum(
        "ste,de->std", branch_grad, out_full, preferred_element_type=jnp.float32
    ).astype(jnp.bfloat16)
    dout_heads = split_heads(attn_grad)
    delta = jnp.transpose(jnp.sum(dout_heads.astype(jnp.float32) * attn_heads, axis=-1), (0, 2, 1))
    key_all, value_all = (
        lax.all_gather(key_rows, "band", axis=1, tiled=True),
        lax.all_gather(value_rows, "band", axis=1, tiled=True),
    )
    seq_len = key_all.shape[1]
    sub_all = math.gcd(seq_len, 4 * tok_rows)
    query_parts = []
    for member in range(seqs_here):
        blocks_all = (
            key_all[member].reshape(seq_len // sub_all, sub_all, width),
            value_all[member].reshape(seq_len // sub_all, sub_all, width),
            segment_ids[member].reshape(seq_len // sub_all, sub_all),
        )
        query_part = query_heads[member]
        dout_part = dout_heads[member]
        lse_part = log_norm[member]
        delta_part = delta[member]
        seg_part = my_seg[member]

        def query_step(
            total,
            item,
            query_part=query_part,
            dout_part=dout_part,
            lse_part=lse_part,
            delta_part=delta_part,
            seg_part=seg_part,
        ):
            key_block, value_block, seg_block = item
            scores, mask = masked_scores(query_part, split_heads(key_block), seg_part, seg_block)
            probs = jnp.where(mask, jnp.exp(scores - lse_part[:, :, None]), 0.0)
            prob_grad = jnp.einsum(
                "qhd,khd->hqk",
                dout_part,
                split_heads(value_block),
                preferred_element_type=jnp.float32,
            )
            score_grad = (probs * (prob_grad - delta_part[:, :, None])).astype(jnp.bfloat16)
            return (
                total
                + jnp.einsum(
                    "hqk,khd->qhd",
                    score_grad,
                    split_heads(key_block),
                    preferred_element_type=jnp.float32,
                ),
                None,
            )

        member_grad, _ = lax.scan(
            query_step, jnp.zeros((tok_rows, HEADS, HEAD_DIM), jnp.float32), blocks_all
        )
        query_parts.append(member_grad)
    query_grad = (jnp.stack(query_parts) * HEAD_DIM ** (-0.5)).reshape(seqs_here, tok_rows, width)
    count = lax.axis_size("band") * tok_rows
    sub = math.gcd(count, 4 * tok_rows)
    columns = []
    for member in range(seqs_here):
        key_part = key_all[member]
        value_part = value_all[member]
        seg_part = segment_ids[member]

        def one_block(item, member=member):
            key_block, value_block, seg_block = item
            key_grad, value_grad = key_terms(
                query_heads[member],
                dout_heads[member],
                log_norm[member],
                delta[member],
                my_seg[member],
                split_heads(key_block),
                split_heads(value_block),
                seg_block,
            )
            return jnp.concatenate(
                [key_grad.reshape(sub, width), value_grad.reshape(sub, width)], axis=-1
            )

        stacked = (
            key_part.reshape(count // sub, sub, width),
            value_part.reshape(count // sub, sub, width),
            seg_part.reshape(count // sub, sub),
        )
        columns.append(lax.map(one_block, stacked).reshape(count, 2 * width))
    both_grads = lax.psum_scatter(
        jnp.stack(columns, axis=1).astype(jnp.bfloat16), "band", scatter_dimension=0, tiled=True
    ).astype(jnp.float32)
    both_grads = jnp.transpose(both_grads, (1, 0, 2))
    key_grad = both_grads[:, :, :width]
    value_grad = both_grads[:, :, width:]
    qkv_grad_low = jnp.concatenate([query_grad, key_grad, value_grad], axis=-1).astype(jnp.bfloat16)
    qkv_grad = jnp.einsum(
        "std,ste->de", first_low, qkv_grad_low, preferred_element_type=jnp.float32
    )
    first_grad = jnp.einsum(
        "ste,de->std", qkv_grad_low, qkv_full, preferred_element_type=jnp.float32
    )
    in_grad, gain_one_grad = norm_back(first_grad, gain_one, first_n, first_s)
    token_grad = resid_grad + in_grad
    shares = (
        lax.psum_scatter(
            qkv_grad.astype(jnp.bfloat16), "seq", scatter_dimension=0, tiled=True
        ).astype(jnp.float32),
        lax.psum_scatter(
            outproj_grad.astype(jnp.bfloat16), "seq", scatter_dimension=0, tiled=True
        ).astype(jnp.float32),
        lax.psum_scatter(
            up_grad.astype(jnp.bfloat16), "seq", scatter_dimension=0, tiled=True
        ).astype(jnp.float32),
        lax.psum_scatter(
            down_grad.astype(jnp.bfloat16), "seq", scatter_dimension=0, tiled=True
        ).astype(jnp.float32),
        lax.psum_scatter(
            gain_one_grad.astype(jnp.bfloat16), "seq", scatter_dimension=0, tiled=True
        ).astype(jnp.float32),
        lax.psum_scatter(
            gain_two_grad.astype(jnp.bfloat16), "seq", scatter_dimension=0, tiled=True
        ).astype(jnp.float32),
    )
    summed = (
        lax.psum(shares[0].astype(jnp.bfloat16), "band").astype(jnp.float32),
        lax.psum(shares[1].astype(jnp.bfloat16), "band").astype(jnp.float32),
        lax.psum(shares[2].astype(jnp.bfloat16), "band").astype(jnp.float32),
        lax.psum(shares[3].astype(jnp.bfloat16), "band").astype(jnp.float32),
        lax.psum(shares[4].astype(jnp.bfloat16), "band").astype(jnp.float32),
        lax.psum(shares[5].astype(jnp.bfloat16), "band").astype(jnp.float32),
    )
    qkv_out, outproj_out, up_out, down_out, gain_one_out, gain_two_out = summed
    return (
        layer_out,
        token_grad,
        qkv_out,
        outproj_out,
        up_out,
        down_out,
        gain_one_out,
        gain_two_out,
    )


MESH = pl.DeviceIdType.MESH
BF = jnp.bfloat16
F32 = jnp.float32
SCALE = HEAD_DIM ** (-0.5)


def place():
    b = lax.axis_index("band")
    y = lax.axis_index("seq")
    return b, y, b // 4, (b // 2) % 2, b % 2


def meet(peers):
    sem = pltpu.get_barrier_semaphore()
    for peer in peers:
        pl.semaphore_signal(sem, inc=1, device_id=peer, device_id_type=MESH)
    pl.semaphore_wait(sem, len(peers))


def send(src, dst, ssem, rsem, peer):
    copy = pltpu.make_async_remote_copy(
        src_ref=src, dst_ref=dst, send_sem=ssem, recv_sem=rsem, device_id=peer, device_id_type=MESH
    )
    copy.start()
    return copy


def comm_call(body, name, cid, outs, scratch, n_in):
    vm = pl.BlockSpec(memory_space=pltpu.VMEM)
    return pl.pallas_call(
        body,
        out_shape=[jax.ShapeDtypeStruct(s, d) for s, d in outs],
        in_specs=[vm] * n_in,
        out_specs=[vm] * len(outs),
        scratch_shapes=scratch,
        compiler_params=pltpu.CompilerParams(collective_id=cid, has_side_effects=True),
        name=name,
    )


def dma(n):
    return pltpu.SemaphoreType.DMA((n,))


def norm_rows(v):
    centre = v - jnp.mean(v, axis=-1, keepdims=True)
    inv_std = lax.rsqrt(jnp.mean(centre * centre, axis=-1, keepdims=True) + EPS)
    return centre * inv_std, inv_std


def open_body(tok, seg, wqkv, gains, tok_all, seg_all, w_sel, gains_all, ss, rs):
    b, y, z, x, c = place()
    core, over = (b + 1 - 2 * c, y), (b, 1 - y)
    meet([core, over])
    cps = []
    for m in range(2):
        cps.append(send(tok.at[m], tok_all.at[2 * y + m, c], ss.at[m], rs.at[m], over))
    cps.append(send(seg, seg_all.at[y], ss.at[2], rs.at[2], over))
    cps.append(send(gains, gains_all.at[y], ss.at[3], rs.at[3], over))
    k = 4
    far = (1 - y) * 2 + c
    own = y * 2 + c
    for hp in range(2):
        for p in range(3):
            col = pl.multiple_of(p * 1024 + far * 256 + hp * 128, 128)
            dst = w_sel.at[y, :, pl.ds(hp * 384 + p * 128, 128)]
            cps.append(send(wqkv.at[:, pl.ds(col, 128)], dst, ss.at[k], rs.at[k], over))
            k += 1
    side = []
    for m in range(2):
        side.append(send(tok.at[m], tok_all.at[2 * y + m, c], ss.at[k], rs.at[k], core))
        k += 1
    for hp in range(2):
        for p in range(3):
            col = pl.multiple_of(p * 1024 + own * 256 + hp * 128, 128)
            w_sel[y, :, hp * 384 + p * 128 : hp * 384 + p * 128 + 128] = wqkv[:, pl.ds(col, 128)]
    for m in range(2):
        tok_all[2 * y + m, c] = tok[m]
    seg_all[y] = seg[...]
    gains_all[y] = gains[...]
    for m in range(2):
        cps[m].wait_recv()
        got = tok_all.at[2 * (1 - y) + m, c]
        side.append(send(got, got, ss.at[k], rs.at[k], core))
        k += 1
    for m in range(2):
        cps[m].wait_send()
    for cp in cps[2:] + side:
        cp.wait()


def open_call(tok, seg, wqkv, gains):
    return comm_call(
        open_body,
        "open_column",
        1,
        [((4, 2, 96, 1024), BF), ((2, 2, 1536), jnp.int32), ((2, 512, 768), BF), ((2, 8, 512), F32)],
        [dma(14), dma(14)],
        4,
    )(tok, seg, wqkv, gains)


def chips(b, c, y):
    j = b // 2
    res = []
    for k in range(1, 8):
        jd = (j + k) % 8
        res.append((jd, (jd * 2 + c, y)))
    return res


def to_heads_body(qkv, up, att, up_sel, ss, rs):
    b, y, z, x, c = place()
    over = (b, 1 - y)
    others = chips(b, c, y)
    meet([over] + [peer for _, peer in others])
    j = b // 2
    cps = []
    far = pl.multiple_of(((1 - y) * 2 + c) * 1024, 1024)
    own = pl.multiple_of((y * 2 + c) * 1024, 1024)
    cps.append(send(up.at[:, pl.ds(far, 1024)], up_sel.at[y], ss.at[0], rs.at[0], over))
    for k, (jd, peer) in enumerate(others):
        col = pl.multiple_of((jd % 2) * 384, 128)
        cps.append(
            send(qkv.at[jd // 2, :, pl.ds(col, 384)], att.at[j], ss.at[k + 1], rs.at[k + 1], peer)
        )
    att[j] = qkv[z, :, pl.ds(pl.multiple_of(x * 384, 128), 384)]
    up_sel[y] = up[:, pl.ds(own, 1024)]
    for cp in cps:
        cp.wait()


def to_heads(qkv, up):
    return comm_call(
        to_heads_body,
        "to_heads",
        2,
        [((8, 192, 384), BF), ((2, 512, 1024), BF)],
        [dma(8), dma(8)],
        2,
    )(qkv, up)


def from_heads_body(attn, cot, rows, cot_all, ss, rs):
    b, y, z, x, c = place()
    core, over = (b + 1 - 2 * c, y), (b, 1 - y)
    others = chips(b, c, y)
    meet([core, over] + [peer for _, peer in others])
    col = pl.multiple_of(x * 128, 128)
    cps, side = [], []
    for k, (jd, peer) in enumerate(others):
        cps.append(send(attn.at[jd], rows.at[z, :, pl.ds(col, 128)], ss.at[k], rs.at[k], peer))
    k = 7
    near = []
    for m in range(2):
        near.append(send(cot.at[m], cot_all.at[2 * y + m, c], ss.at[k], rs.at[k], over))
        k += 1
    for m in range(2):
        side.append(send(cot.at[m], cot_all.at[2 * y + m, c], ss.at[k], rs.at[k], core))
        k += 1
    rows[z, :, pl.ds(col, 128)] = attn[b // 2]
    for m in range(2):
        cot_all[2 * y + m, c] = cot[m]
    for m in range(2):
        near[m].wait_recv()
        got = cot_all.at[2 * (1 - y) + m, c]
        side.append(send(got, got, ss.at[k], rs.at[k], core))
        k += 1
    for cp in near:
        cp.wait_send()
    for cp in cps + side:
        cp.wait()


def from_heads(attn, cot):
    return comm_call(
        from_heads_body,
        "from_heads",
        3,
        [((4, 192, 256), BF), ((4, 2, 96, 1024), BF)],
        [dma(13), dma(13)],
        2,
    )(attn, cot)


def column_sum(part, got, mid, fin, ss, rs, b, y, c):
    core, over = (b + 1 - 2 * c, y), (b, 1 - y)
    first = []
    for m in range(2):
        q = 2 * (1 - y) + m
        first.append(send(part.at[q, 1 - c], got.at[q], ss.at[m], rs.at[m], core))
    for m in range(2):
        q = 2 * y + m
        first.append(send(part.at[q, 1 - c], got.at[q], ss.at[2 + m], rs.at[2 + m], core))
    second = []
    for m in range(2):
        q = 2 * (1 - y) + m
        first[m].wait_recv()
        mid[m] = (part[q, c].astype(F32) + got[q].astype(F32)).astype(BF)
        second.append(send(mid.at[m], fin.at[m], ss.at[4 + m], rs.at[4 + m], over))
    sums = []
    for m in range(2):
        q = 2 * y + m
        first[2 + m].wait_recv()
        second[m].wait_recv()
        sums.append(part[q, c].astype(F32) + got[q].astype(F32) + fin[m].astype(F32))
    for cp in first + second:
        cp.wait_send()
    return sums


def column_spread(own, full, ss, rs, k, b, y, c):
    core, over = (b + 1 - 2 * c, y), (b, 1 - y)
    near, side = [], []
    for m in range(2):
        near.append(send(own.at[m], full.at[2 * y + m, c], ss.at[k], rs.at[k], over))
        side.append(send(own.at[m], full.at[2 * y + m, c], ss.at[k + 1], rs.at[k + 1], core))
        k += 2
    for m in range(2):
        full[2 * y + m, c] = own[m]
    for m in range(2):
        near[m].wait_recv()
        got = full.at[2 * (1 - y) + m, c]
        side.append(send(got, got, ss.at[k], rs.at[k], core))
        k += 1
    for cp in near:
        cp.wait_send()
    for cp in side:
        cp.wait()


SUM_SCRATCH = [
    pltpu.VMEM((4, 96, 1024), BF),
    pltpu.VMEM((2, 96, 1024), BF),
    pltpu.VMEM((2, 96, 1024), BF),
]


def second_norm_body(part, tok, valid, gain, resid, h_all, got, mid, fin, own, ss, rs):
    b, y, z, x, c = place()
    meet([(b + 1 - 2 * c, y), (b, 1 - y)])
    sums = column_sum(part, got, mid, fin, ss, rs, b, y, c)
    for m in range(2):
        res = tok[m].astype(F32) + valid[m][:, :1] * sums[m]
        resid[m] = res
        normed, _ = norm_rows(res)
        own[m] = (normed * gain[1:2]).astype(BF)
    column_spread(own, h_all, ss, rs, 6, b, y, c)


def second_norm(part, tok, valid, gain):
    return comm_call(
        second_norm_body,
        "second_norm",
        4,
        [((2, 96, 1024), F32), ((4, 2, 96, 1024), BF)],
        SUM_SCRATCH + [pltpu.VMEM((2, 96, 1024), BF), dma(12), dma(12)],
        4,
    )(part, tok, valid, gain)


def second_back_body(part, resid, cot, valid, gain, rgrad, ggrad, br_all, got, mid, fin, own, ss, rs):
    b, y, z, x, c = place()
    meet([(b + 1 - 2 * c, y), (b, 1 - y)])
    sums = column_sum(part, got, mid, fin, ss, rs, b, y, c)
    total = jnp.zeros((1, 1024), F32)
    for m in range(2):
        normed, inv_std = norm_rows(resid[m])
        e = sums[m]
        g = e * gain[1:2]
        total = total + jnp.sum(e * normed, axis=0, keepdims=True)
        one = jnp.mean(g, axis=-1, keepdims=True)
        two = jnp.mean(g * normed, axis=-1, keepdims=True)
        rg = cot[m].astype(F32) + (g - one - normed * two) * inv_std
        rgrad[m] = rg
        own[m] = (valid[m][:, :1] * rg).astype(BF)
    ggrad[...] = jnp.broadcast_to(total, (8, 1024))
    column_spread(own, br_all, ss, rs, 6, b, y, c)


def second_back(part, resid, cot, valid, gain):
    return comm_call(
        second_back_body,
        "second_back",
        5,
        [((2, 96, 1024), F32), ((8, 1024), F32), ((4, 2, 96, 1024), BF)],
        SUM_SCRATCH + [pltpu.VMEM((2, 96, 1024), BF), dma(12), dma(12)],
        5,
    )(part, resid, cot, valid, gain)


def grad_heads_body(agrad, part, resid, valid, do, out, got, mid, fin, ss, rs):
    b, y, z, x, c = place()
    others = chips(b, c, y)
    meet([(b + 1 - 2 * c, y), (b, 1 - y)] + [peer for _, peer in others])
    j = b // 2
    cps = []
    for k, (jd, peer) in enumerate(others):
        col = pl.multiple_of((jd % 2) * 128, 128)
        cps.append(
            send(agrad.at[jd // 2, :, pl.ds(col, 128)], do.at[j], ss.at[6 + k], rs.at[6 + k], peer)
        )
    do[j] = agrad[z, :, pl.ds(pl.multiple_of(x * 128, 128), 128)]
    sums = column_sum(part, got, mid, fin, ss, rs, b, y, c)
    for m in range(2):
        out[m] = (resid[m] + valid[m][:, :1] * sums[m]).astype(BF)
    for cp in cps:
        cp.wait()


def grad_heads(agrad, part, resid, valid):
    return comm_call(
        grad_heads_body,
        "grad_heads",
        6,
        [((8, 192, 128), BF), ((2, 96, 1024), BF)],
        SUM_SCRATCH + [dma(13), dma(13)],
        4,
    )(agrad, part, resid, valid)


def grad_rows_body(dqkv, rows, ss, rs):
    b, y, z, x, c = place()
    others = chips(b, c, y)
    meet([peer for _, peer in others])
    col = pl.multiple_of(x * 384, 128)
    cps = []
    for k, (jd, peer) in enumerate(others):
        cps.append(send(dqkv.at[jd], rows.at[z, :, pl.ds(col, 384)], ss.at[k], rs.at[k], peer))
    rows[z, :, pl.ds(col, 384)] = dqkv[b // 2]
    for cp in cps:
        cp.wait()


def grad_rows(dqkv):
    return comm_call(
        grad_rows_body, "grad_rows", 7, [((4, 192, 768), BF)], [dma(7), dma(7)], 1
    )(dqkv)[0]


def first_back_body(part, tok, rgrad, gain, tgrad, ggrad, got, mid, fin, ss, rs):
    b, y, z, x, c = place()
    meet([(b + 1 - 2 * c, y), (b, 1 - y)])
    sums = column_sum(part, got, mid, fin, ss, rs, b, y, c)
    total = jnp.zeros((1, 1024), F32)
    for m in range(2):
        normed, inv_std = norm_rows(tok[m].astype(F32))
        e = sums[m]
        g = e * gain[0:1]
        total = total + jnp.sum(e * normed, axis=0, keepdims=True)
        one = jnp.mean(g, axis=-1, keepdims=True)
        two = jnp.mean(g * normed, axis=-1, keepdims=True)
        tgrad[m] = rgrad[m] + (g - one - normed * two) * inv_std
    ggrad[...] = jnp.broadcast_to(total, (8, 1024))


def first_back(part, tok, rgrad, gain):
    return comm_call(
        first_back_body,
        "first_back",
        8,
        [((2, 96, 1024), F32), ((8, 1024), F32)],
        SUM_SCRATCH + [dma(6), dma(6)],
        4,
    )(part, tok, rgrad, gain)


def last_dot(a, b):
    return lax.dot_general(a, b, (((1,), (1,)), ((), ())), preferred_element_type=F32)


def plain_dot(a, b):
    return lax.dot_general(a, b, (((1,), (0,)), ((), ())), preferred_element_type=F32)


def attend_body(qkv, seg_col, seg_row, out_low, out, lse):
    rows = out.shape[0]
    i = pl.program_id(0)
    at = pl.multiple_of(i * rows, rows)
    q = qkv[pl.ds(at, rows), 0:128]
    keys = qkv[:, 128:256]
    values = qkv[:, 256:384]
    low_half = lax.broadcasted_iota(jnp.int32, (rows, 128), 1) < HEAD_DIM
    mask = seg_col[:, 0:1] == seg_row[0:1, :]
    outs, norms = [], []
    for h in range(2):
        qh = jnp.where(low_half if h == 0 else ~low_half, q * SCALE, 0.0).astype(BF)
        scores = jnp.where(mask, last_dot(qh, keys), NEG)
        top = jnp.max(scores, axis=-1, keepdims=True)
        probs = jnp.exp(scores - top)
        total = jnp.sum(probs, axis=-1, keepdims=True)
        outs.append(plain_dot(probs.astype(BF), values) / total)
        norms.append(top + jnp.log(total))
    res = jnp.where(low_half, outs[0], outs[1])
    out[...] = res
    out_low[...] = res.astype(BF)
    lse[...] = jnp.where(low_half, norms[0], norms[1])


def attend(qkv, seg_col, seg_row):
    length = qkv.shape[0]
    rows = 256
    tile = pl.BlockSpec((rows, 128), lambda i: (i, 0))
    return pl.pallas_call(
        attend_body,
        grid=(length // rows,),
        in_specs=[
            pl.BlockSpec((length, 384), lambda i: (0, 0)),
            pl.BlockSpec((rows, 128), lambda i: (i, 0)),
            pl.BlockSpec((8, length), lambda i: (0, 0)),
        ],
        out_specs=[tile, tile, tile],
        out_shape=[
            jax.ShapeDtypeStruct((length, 128), BF),
            jax.ShapeDtypeStruct((length, 128), F32),
            jax.ShapeDtypeStruct((length, 128), F32),
        ],
        name="attend",
    )(qkv, seg_col, seg_row)


def attend_back_body(qkv, out, lse, do, seg_col, seg_row, dqkv, lse_t, delta, keys_t, dq_t):
    length = qkv.shape[0]
    rows = seg_col.shape[0]
    i = pl.program_id(0)
    at = pl.multiple_of(i * rows, rows)

    @pl.when(i == 0)
    def _():
        lse_t[...] = jnp.transpose(lse[...])
        prod = jnp.transpose(do[...].astype(F32) * out[...])
        delta[0:8] = jnp.broadcast_to(jnp.sum(prod[:HEAD_DIM], axis=0, keepdims=True), (8, length))
        delta[8:16] = jnp.broadcast_to(jnp.sum(prod[HEAD_DIM:], axis=0, keepdims=True), (8, length))
        keys_t[...] = jnp.transpose(qkv[:, 128:256].astype(F32)).astype(BF)
        dq_t[...] = jnp.zeros_like(dq_t)

    keys = qkv[pl.ds(at, rows), 128:256]
    values = qkv[pl.ds(at, rows), 256:384]
    q = qkv[:, 0:128]
    douts = do[...]
    low_half = lax.broadcasted_iota(jnp.int32, (rows, 128), 1) < HEAD_DIM
    low_rows = lax.broadcasted_iota(jnp.int32, (128, 1), 0) < HEAD_DIM
    mask = seg_col[:, 0:1] == seg_row[0:1, :]
    kgrads, vgrads, qgrads = [], [], []
    for h in range(2):
        pick = low_half if h == 0 else ~low_half
        kh = jnp.where(pick, keys * SCALE, 0.0).astype(BF)
        vh = jnp.where(pick, values, 0.0).astype(BF)
        scores = last_dot(kh, q)
        probs = jnp.where(mask, jnp.exp(scores - lse_t[h * HEAD_DIM : h * HEAD_DIM + 1]), 0.0)
        vgrads.append(plain_dot(probs.astype(BF), douts))
        pgrad = last_dot(vh, douts)
        sgrad = (probs * (pgrad - delta[h * 8 : h * 8 + 1])).astype(BF)
        kgrads.append(plain_dot(sgrad, q))
        qgrads.append(plain_dot(keys_t[:, pl.ds(at, rows)], sgrad))
    dq_t[...] += jnp.where(low_rows, qgrads[0], qgrads[1])
    dqkv[pl.ds(at, rows), 128:256] = (jnp.where(low_half, kgrads[0], kgrads[1]) * SCALE).astype(BF)
    dqkv[pl.ds(at, rows), 256:384] = jnp.where(low_half, vgrads[0], vgrads[1]).astype(BF)

    @pl.when(i == pl.num_programs(0) - 1)
    def _():
        dqkv[:, 0:128] = (jnp.transpose(dq_t[...]) * SCALE).astype(BF)


def attend_back(qkv, out, lse, do, seg_col, seg_row):
    length = qkv.shape[0]
    rows = 256
    whole = pl.BlockSpec((length, 128), lambda i: (0, 0))
    wide = pl.BlockSpec((length, 384), lambda i: (0, 0))
    return pl.pallas_call(
        attend_back_body,
        grid=(length // rows,),
        in_specs=[
            wide,
            whole,
            whole,
            whole,
            pl.BlockSpec((rows, 128), lambda i: (i, 0)),
            pl.BlockSpec((8, length), lambda i: (0, 0)),
        ],
        out_specs=wide,
        out_shape=jax.ShapeDtypeStruct((length, 384), BF),
        scratch_shapes=[
            pltpu.VMEM((128, length), F32),
            pltpu.VMEM((16, length), F32),
            pltpu.VMEM((128, length), BF),
            pltpu.VMEM((128, length), F32),
        ],
        name="attend_back",
    )(qkv, out, lse, do, seg_col, seg_row)


CHUNKS = 12
SWAPPED = ((4, 8), (9, 12))


def wsum_body(part, gg, full, gsum, r1, s1, r2, s2, r3, p3, tmp, g1, g2, g3, ss, rs, ls, gs, gr):
    b, y, z, x, c = place()
    others = chips(b, c, y)
    z0, zb = z % 2, z // 2
    core, over = (b + 1 - 2 * c, y), (b, 1 - y)
    px, p0, pb = (b + 2 - 4 * x, y), (b + 4 - 8 * z0, y), (b + 8 - 16 * zb, y)
    o1 = x * 256
    o2 = o1 + z0 * 128
    o3 = o2 + zb * 64

    def rows(start, size):
        return pl.ds(pl.multiple_of(start, 64), size)

    def remote(src, dst, stage, i, peer):
        return pltpu.make_async_remote_copy(
            src_ref=src,
            dst_ref=dst,
            send_sem=ss.at[stage, i],
            recv_sem=rs.at[stage, i],
            device_id=peer,
            device_id_type=MESH,
        )

    def c_x(i):
        return remote(part.at[i, :, rows((1 - x) * 256, 256)], r1.at[i], 0, i, px)

    def c_z0(i):
        return remote(s1.at[i, :, rows((1 - z0) * 128, 128)], r2.at[i], 1, i, p0)

    def c_zb(i):
        return remote(s2.at[i, :, rows((1 - zb) * 64, 64)], r3.at[i], 2, i, pb)

    def c_y(i):
        return remote(tmp.at[i], p3.at[i, y], 3, i, over)

    def c_gb(i):
        return remote(p3.at[i], full.at[i, c, :, rows(o3, 64)], 4, i, pb)

    def c_own(i):
        return pltpu.make_async_copy(p3.at[i], full.at[i, c, :, rows(o3, 64)], ls.at[i])

    def c_g0(i):
        src = full.at[i, c, :, rows(o2, 128)]
        return remote(src, src, 5, i, p0)

    def c_gx(i):
        src = full.at[i, c, :, rows(o1, 256)]
        return remote(src, src, 6, i, px)

    def c_core(i):
        src = full.at[i, c]
        return remote(src, src, 7, i, core)

    meet([core, over] + [peer for _, peer in others])

    @pl.loop(0, CHUNKS)
    def _(i):
        c_x(i).start()

    gcps = [send(gg, g1.at[0], gs.at[0], gr.at[0], core)]
    gcps[0].wait_recv()
    g1[1] = g1[0] + gg[...]
    gcps.append(send(g1.at[1], g2.at[0], gs.at[1], gr.at[1], over))
    gcps[1].wait_recv()
    j = b // 2
    g3[j] = g1[1] + g2[0]
    for k, (jd, peer) in enumerate(others):
        gcps.append(send(g3.at[j], g3.at[j], gs.at[2 + k], gr.at[2 + k], peer))

    def when_chunk(t, lag, act, ranges=((0, CHUNKS),)):
        for lo, hi in ranges:

            @pl.when((t - lag >= lo) & (t - lag < hi))
            def _():
                act(t - lag)

    def add_x(i):
        c_x(i).wait_recv()
        mine = part[i, :, rows(x * 256, 256)].astype(F32)
        s1[i] = (mine + r1[i].astype(F32)).astype(BF)
        c_z0(i).start()

    def add_z0(i):
        c_z0(i).wait_recv()
        mine = s1[i, :, rows(z0 * 128, 128)].astype(F32)
        s2[i] = (mine + r2[i].astype(F32)).astype(BF)
        c_zb(i).start()

    def add_zb_plain(i):
        c_zb(i).wait_recv()
        mine = s2[i, :, rows(zb * 64, 64)].astype(F32)
        p3[i] = (mine + r3[i].astype(F32)).astype(BF)
        c_gb(i).start()
        c_own(i).start()

    def add_zb_swap(i):
        c_zb(i).wait_recv()
        for h, dst in ((y, p3.at[i, y]), (1 - y, tmp.at[i])):
            mine = s2[i, h, rows(zb * 64, 64)].astype(F32)
            dst[...] = (mine + r3[i, h].astype(F32)).astype(BF)
        c_y(i).start()

    def take_y(i):
        c_y(i).wait_recv()
        c_gb(i).start()
        c_own(i).start()

    def grow_z0(i):
        c_gb(i).wait_recv()
        c_own(i).wait()
        c_g0(i).start()

    def grow_x(i):
        c_g0(i).wait_recv()
        c_gx(i).start()

    def grow_core(i):
        c_gx(i).wait_recv()
        c_core(i).start()

    plain = ((0, 4), (8, 9))

    @pl.loop(0, CHUNKS + 6)
    def _(t):
        when_chunk(t, 6, grow_core)
        when_chunk(t, 5, grow_x)
        when_chunk(t, 4, grow_z0)
        when_chunk(t, 3, take_y, SWAPPED)
        when_chunk(t, 2, add_zb_plain, plain)
        when_chunk(t, 2, add_zb_swap, SWAPPED)
        when_chunk(t, 1, add_z0)
        when_chunk(t, 0, add_x)

    @pl.loop(0, CHUNKS)
    def _(i):
        c_core(i).wait_recv()
        for cp in (c_x, c_z0, c_zb, c_gb, c_g0, c_gx, c_core):
            cp(i).wait_send()

    for lo, hi in SWAPPED:

        @pl.loop(lo, hi)
        def _(i):
            c_y(i).wait_send()

    for cp in gcps[:2]:
        cp.wait_send()
    for cp in gcps[2:]:
        cp.wait()
    total = g3[0]
    for k in range(1, 8):
        total = total + g3[k]
    gsum[...] = total


def weight_sums(part, gg):
    return pl.pallas_call(
        wsum_body,
        out_shape=[
            jax.ShapeDtypeStruct((CHUNKS, 2, 2, 512, 256), BF),
            jax.ShapeDtypeStruct((8, 1024), F32),
        ],
        in_specs=[pl.BlockSpec(memory_space=pltpu.VMEM)] * 2,
        out_specs=[pl.BlockSpec(memory_space=pl.ANY), pl.BlockSpec(memory_space=pltpu.VMEM)],
        scratch_shapes=[
            pltpu.VMEM((CHUNKS, 2, 256, 256), BF),
            pltpu.VMEM((CHUNKS, 2, 256, 256), BF),
            pltpu.VMEM((CHUNKS, 2, 128, 256), BF),
            pltpu.VMEM((CHUNKS, 2, 128, 256), BF),
            pltpu.VMEM((CHUNKS, 2, 64, 256), BF),
            pltpu.VMEM((CHUNKS, 2, 64, 256), BF),
            pltpu.VMEM((CHUNKS, 64, 256), BF),
            pltpu.VMEM((2, 8, 1024), F32),
            pltpu.VMEM((1, 8, 1024), F32),
            pltpu.VMEM((8, 8, 1024), F32),
            pltpu.SemaphoreType.DMA((8, CHUNKS)),
            pltpu.SemaphoreType.DMA((8, CHUNKS)),
            pltpu.SemaphoreType.DMA((CHUNKS,)),
            dma(9),
            dma(9),
        ],
        compiler_params=pltpu.CompilerParams(collective_id=9, has_side_effects=True),
        name="weight_sums",
    )(part, gg)


def widen_body(src, dst):
    for k in range(4):
        dst[:, k * 256 : k * 256 + 256] = src[k].astype(F32)


def widen_out_body(src, dst):
    for h in range(2):
        for k in range(2):
            col = (h * 2 + k) * 256
            dst[:, col : col + 256] = src[h, k * 256 : k * 256 + 256].astype(F32)


def widen_qkv_body(src, dst):
    for r in range(4):
        for t in range(6):
            col = (t % 3) * 1024 + r * 256 + (t // 3) * 128
            half = (t % 2) * 128
            dst[:, col : col + 128] = src[t // 2, r % 2, r // 2, :, half : half + 128].astype(F32)


def widen_all(full):
    down = pl.pallas_call(
        widen_body,
        grid=(4,),
        in_specs=[pl.BlockSpec((4, None, None, 512, 256), lambda r: (0, r // 2, r % 2, 0, 0))],
        out_specs=pl.BlockSpec((512, 1024), lambda r: (r, 0)),
        out_shape=jax.ShapeDtypeStruct((2048, 1024), F32),
        name="widen_down",
    )(full)
    up = pl.pallas_call(
        widen_body,
        grid=(4,),
        in_specs=[pl.BlockSpec((4, None, None, 512, 256), lambda r: (1, r % 2, r // 2, 0, 0))],
        out_specs=pl.BlockSpec((512, 1024), lambda r: (0, r)),
        out_shape=jax.ShapeDtypeStruct((512, 4096), F32),
        name="widen_up",
    )(full)
    out = pl.pallas_call(
        widen_out_body,
        grid=(2,),
        in_specs=[pl.BlockSpec((None, None, 2, 512, 256), lambda r: (8, r, 0, 0, 0))],
        out_specs=pl.BlockSpec((256, 1024), lambda r: (r, 0)),
        out_shape=jax.ShapeDtypeStruct((512, 1024), F32),
        name="widen_out",
    )(full)
    qkv = pl.pallas_call(
        widen_qkv_body,
        grid=(4,),
        in_specs=[pl.BlockSpec((3, 2, 2, 128, 256), lambda i: (3, 0, 0, i, 0))],
        out_specs=pl.BlockSpec((128, 3072), lambda i: (i, 0)),
        out_shape=jax.ShapeDtypeStruct((512, 3072), F32),
        name="widen_qkv",
    )(full)
    return down, up, out, qkv


def column_device(
    tokens,
    segment_ids,
    qkv_weight,
    out_weight,
    up_weight,
    down_weight,
    gain_first,
    gain_second,
    out_cotangent,
):
    b, y, z, x, c = place()
    my_seg = lax.dynamic_slice_in_dim(segment_ids, b * 96, 96, 1)
    valid = jnp.broadcast_to((my_seg >= 0).astype(F32)[:, :, None], (2, 96, 128))
    gains = jnp.pad(jnp.stack([gain_first, gain_second]).astype(F32), ((0, 6), (0, 0)))
    tok_all, seg_all, w_sel, gains_all = open_call(tokens, segment_ids, qkv_weight, gains)
    gain = jnp.transpose(gains_all, (1, 0, 2)).reshape(8, 1024)
    seg_all = seg_all.reshape(4, 1536)
    seg_z = lax.dynamic_slice_in_dim(seg_all, z, 1, 0)
    seg_row = jnp.broadcast_to(seg_z, (8, 1536))
    seg_col = jnp.broadcast_to(seg_z.reshape(1536, 1), (1536, 128))
    seg_here = lax.dynamic_slice_in_dim(seg_all, (z * 2 + x) * 192, 192, 1)
    valid_all = (seg_here >= 0).astype(F32).reshape(768, 1)
    w_sel = w_sel.reshape(1024, 768)
    normed, _ = norm_rows(tok_all.reshape(768, 1024).astype(F32))
    h_one = (normed * gain[0:1]).astype(BF)
    qkv = plain_dot(h_one, w_sel).astype(BF)
    att, up_sel = to_heads(qkv.reshape(4, 192, 768), up_weight)
    up_sel = up_sel.reshape(1024, 1024)
    att = att.reshape(1536, 384)
    out_low, out_full, lse = attend(att, seg_col, seg_row)
    attn_low, cot_all = from_heads(out_low.reshape(8, 192, 128), out_cotangent)
    attn_low = attn_low.reshape(768, 256)
    out_rows = lax.dynamic_slice_in_dim(out_weight, c * 256, 256, 0)
    part = plain_dot(attn_low, out_rows).astype(BF)
    resid, h_two = second_norm(part.reshape(4, 2, 96, 1024), tokens, valid, gain)
    h_two = h_two.reshape(768, 1024)
    pre_act = plain_dot(h_two, up_sel)
    hidden_low = jax.nn.gelu(pre_act, approximate=False).astype(BF)
    down_rows = lax.dynamic_slice_in_dim(down_weight, c * 1024, 1024, 0)
    grad_two = (valid_all * cot_all.reshape(768, 1024).astype(F32)).astype(BF)
    hidden_grad = last_dot(grad_two, down_rows)
    slope = 0.5 * (1.0 + lax.erf(pre_act * ROOT_HALF)) + pre_act * DENSITY * jnp.exp(
        -0.5 * pre_act * pre_act
    )
    pre_grad = (hidden_grad * slope).astype(BF)
    e_part = last_dot(pre_grad, up_sel).astype(BF)
    rgrad, gain_two_grad, branch = second_back(
        e_part.reshape(4, 2, 96, 1024), resid, out_cotangent, valid, gain
    )
    branch = branch.reshape(768, 1024)
    branch_two = plain_dot(hidden_low, down_rows).astype(BF)
    first_dot = lambda a, d: lax.dot_general(
        a, d, (((0,), (0,)), ((), ())), preferred_element_type=F32
    )
    down_grad = first_dot(hidden_low, grad_two)
    up_grad = first_dot(h_two, pre_grad)
    attn_grad = last_dot(branch, out_rows).astype(BF)
    do, layer_out = grad_heads(
        attn_grad.reshape(4, 192, 256), branch_two.reshape(4, 2, 96, 1024), resid, valid
    )
    outproj_grad = first_dot(attn_low, branch)
    dqkv = attend_back(att, out_full, lse, do.reshape(1536, 128), seg_col, seg_row)
    dqkv_rows = grad_rows(dqkv.reshape(8, 192, 384)).reshape(768, 768)
    c_part = last_dot(dqkv_rows, w_sel).astype(BF)
    token_grad, gain_one_grad = first_back(c_part.reshape(4, 2, 96, 1024), tokens, rgrad, gain)
    qkv_grad = first_dot(h_one, dqkv_rows)
    part = jnp.concatenate(
        [
            jnp.transpose(down_grad.astype(BF).reshape(2, 512, 4, 256), (2, 0, 1, 3)),
            jnp.transpose(up_grad.astype(BF).reshape(2, 512, 4, 256), (2, 0, 1, 3)),
            jnp.transpose(outproj_grad.astype(BF).reshape(256, 4, 256), (1, 0, 2)).reshape(
                1, 2, 512, 256
            ),
            jnp.transpose(qkv_grad.astype(BF).reshape(2, 512, 3, 256), (2, 0, 1, 3)),
        ],
        0,
    )
    rows8 = lax.broadcasted_iota(jnp.int32, (8, 1024), 0)
    full, gain_sum = weight_sums(part, jnp.where(rows8 == 0, gain_one_grad, gain_two_grad))
    down_out, up_out, out_out, qkv_out = widen_all(full)
    gain_out = lax.dynamic_slice_in_dim(gain_sum, y * 512, 512, 1)
    return (
        layer_out,
        token_grad,
        qkv_out,
        out_out,
        up_out,
        down_out,
        gain_out[0],
        gain_out[1],
    )


def solution(mesh):
    placed = (
        P("seq", "band", None),
        P("seq", None),
        P("seq", None),
        P("seq", None),
        P("seq", None),
        P("seq", None),
        P("seq"),
        P("seq"),
        P("seq", "band", None),
    )
    split = dict(mesh.shape) == {"band": 16, "seq": 2}
    return jax.shard_map(
        column_device if split else per_device,
        mesh=mesh,
        in_specs=placed,
        out_specs=(
            P("seq", "band", None),
            P("seq", "band", None),
            P("seq", None),
            P("seq", None),
            P("seq", None),
            P("seq", None),
            P("seq"),
            P("seq"),
        ),
        check_vma=False,
    )
```

```python
import functools
import math

import jax
import jax.numpy as jnp
from jax import lax
from jax.experimental import pallas as pl
from jax.experimental.pallas import tpu as pltpu
from jax.sharding import PartitionSpec as P

HEADS = 16
HEAD_DIM = 64


EPS = 1e-06
NEG = -1e30
ROOT_HALF = 0.7071067811865476
DENSITY = 0.3989422804014327


def layer_norm(values, gain):
    centre = values - jnp.mean(values, axis=-1, keepdims=True)
    inv_std = lax.rsqrt(jnp.mean(centre * centre, axis=-1, keepdims=True) + EPS)
    normed = centre * inv_std
    return (normed * gain, normed, inv_std)


def norm_back(grad_in, gain, normed, inv_std):
    scaled = grad_in * gain
    mean_one = jnp.mean(scaled, axis=-1, keepdims=True)
    mean_two = jnp.mean(scaled * normed, axis=-1, keepdims=True)
    gain_grad = jnp.sum((grad_in * normed).reshape(-1, grad_in.shape[-1]), axis=0)
    return (inv_std * (scaled - mean_one - normed * mean_two), gain_grad)


def split_heads(matrix):
    return matrix.reshape(matrix.shape[:-1] + (HEADS, HEAD_DIM))


def masked_scores(query_part, key_part, query_seg, key_seg):
    scores = jnp.einsum(
        "qhd,khd->hqk", query_part, key_part, preferred_element_type=jnp.float32
    ) * HEAD_DIM ** (-0.5)
    return (scores, (query_seg[:, None] == key_seg[None, :])[None])


def key_terms(
    query_part, dout_part, lse_part, delta_part, query_seg, key_part, value_part, key_seg
):
    scores, mask = masked_scores(query_part, key_part, query_seg, key_seg)
    probs = jnp.where(mask, jnp.exp(scores - lse_part[:, :, None]), 0.0)
    value_grad = jnp.einsum(
        "hqk,qhd->khd", probs.astype(jnp.bfloat16), dout_part, preferred_element_type=jnp.float32
    )
    prob_grad = jnp.einsum(
        "qhd,khd->hqk", dout_part, value_part, preferred_element_type=jnp.float32
    )
    score_grad = (probs * (prob_grad - delta_part[:, :, None])).astype(jnp.bfloat16)
    key_grad = jnp.einsum(
        "hqk,qhd->khd", score_grad, query_part, preferred_element_type=jnp.float32
    ) * HEAD_DIM ** (-0.5)
    return (key_grad, value_grad)


def online_step(query_part, query_seg):

    def step(state, item):
        key_block, value_block, seg_block = item
        run_max, run_sum, run_acc = state
        scores, mask = masked_scores(query_part, split_heads(key_block), query_seg, seg_block)
        masked = jnp.where(mask, scores, NEG)
        top = jnp.maximum(run_max, jnp.max(masked, axis=-1))
        correct = jnp.exp(run_max - top)
        probs = jnp.where(mask, jnp.exp(masked - top[:, :, None]), 0.0)
        update = jnp.einsum(
            "hqk,khd->hqd",
            probs.astype(jnp.bfloat16),
            split_heads(value_block),
            preferred_element_type=jnp.float32,
        )
        return (
            (
                top,
                run_sum * correct + jnp.sum(probs, axis=-1),
                run_acc * correct[:, :, None] + update,
            ),
            None,
        )

    return step


def per_device(
    tokens,
    segment_ids,
    qkv_weight,
    out_weight,
    up_weight,
    down_weight,
    gain_first,
    gain_second,
    out_cotangent,
):
    seqs_here = tokens.shape[0]
    tok_rows = tokens.shape[1]
    width = tokens.shape[2]
    my_seg = lax.dynamic_slice_in_dim(segment_ids, lax.axis_index("band") * tok_rows, tok_rows, 1)
    valid = (my_seg >= 0).astype(jnp.float32)[:, :, None]
    qkv_full, out_full, up_full, down_full, gain_one, gain_two = (
        lax.all_gather(qkv_weight, "seq", axis=0, tiled=True),
        lax.all_gather(out_weight, "seq", axis=0, tiled=True),
        lax.all_gather(up_weight, "seq", axis=0, tiled=True),
        lax.all_gather(down_weight, "seq", axis=0, tiled=True),
        lax.all_gather(gain_first, "seq", axis=0, tiled=True),
        lax.all_gather(gain_second, "seq", axis=0, tiled=True),
    )
    gain_one = gain_one.astype(jnp.float32)
    gain_two = gain_two.astype(jnp.float32)
    inputs = tokens.astype(jnp.float32)
    first_h, first_n, first_s = layer_norm(inputs, gain_one)
    first_low = first_h.astype(jnp.bfloat16)
    qkv_rows = jnp.einsum(
        "std,de->ste", first_low, qkv_full, preferred_element_type=jnp.float32
    ).astype(jnp.bfloat16)
    query_rows = qkv_rows[:, :, :width]
    key_rows = qkv_rows[:, :, width : 2 * width]
    value_rows = qkv_rows[:, :, 2 * width :]
    query_heads = split_heads(query_rows)

    def online(carry, pieces):
        key_piece, value_piece = pieces
        count = key_piece.shape[1]
        sub = math.gcd(count, 4 * tok_rows)
        results = []
        for member in range(seqs_here):
            state = (carry[0][member], carry[1][member], carry[2][member])
            stacked = (
                key_piece[member].reshape(count // sub, sub, width),
                value_piece[member].reshape(count // sub, sub, width),
                segment_ids[member].reshape(count // sub, sub),
            )
            state, _ = lax.scan(online_step(query_heads[member], my_seg[member]), state, stacked)
            results.append(state)
        return tuple((jnp.stack([result[part] for result in results]) for part in range(3)))

    start_state = (
        jnp.full((seqs_here, HEADS, tok_rows), NEG, jnp.float32),
        jnp.zeros((seqs_here, HEADS, tok_rows), jnp.float32),
        jnp.zeros((seqs_here, HEADS, tok_rows, HEAD_DIM), jnp.float32),
    )
    run_max, run_sum, run_acc = online(
        start_state,
        (
            lax.all_gather(key_rows, "band", axis=1, tiled=True),
            lax.all_gather(value_rows, "band", axis=1, tiled=True),
        ),
    )
    log_norm = run_max + jnp.log(run_sum)
    attn_heads = jnp.transpose(run_acc / run_sum[:, :, :, None], (0, 2, 1, 3))
    attn_rows = attn_heads.reshape(seqs_here, tok_rows, width)
    attn_low = attn_rows.astype(jnp.bfloat16)
    resid = inputs + valid * jnp.einsum(
        "std,de->ste", attn_low, out_full, preferred_element_type=jnp.float32
    )
    second_h, second_n, second_s = layer_norm(resid, gain_two)
    second_low = second_h.astype(jnp.bfloat16)
    pre_act = jnp.einsum("std,df->stf", second_low, up_full, preferred_element_type=jnp.float32)
    hidden_low = jax.nn.gelu(pre_act, approximate=False).astype(jnp.bfloat16)
    branch_two = jnp.einsum(
        "stf,fd->std", hidden_low, down_full, preferred_element_type=jnp.float32
    )
    layer_out = (resid + valid * branch_two).astype(jnp.bfloat16)
    grad_out = out_cotangent.astype(jnp.float32)
    grad_two = (valid * grad_out).astype(jnp.bfloat16)
    down_grad = jnp.einsum("stf,std->fd", hidden_low, grad_two, preferred_element_type=jnp.float32)
    hidden_grad = jnp.einsum("std,fd->stf", grad_two, down_full, preferred_element_type=jnp.float32)
    slope = 0.5 * (1.0 + lax.erf(pre_act * ROOT_HALF)) + pre_act * DENSITY * jnp.exp(
        -0.5 * pre_act * pre_act
    )
    pre_grad = (hidden_grad * slope).astype(jnp.bfloat16)
    up_grad = jnp.einsum("std,stf->df", second_low, pre_grad, preferred_element_type=jnp.float32)
    second_grad = jnp.einsum("stf,df->std", pre_grad, up_full, preferred_element_type=jnp.float32)
    norm_grad, gain_two_grad = norm_back(second_grad, gain_two, second_n, second_s)
    resid_grad = grad_out + norm_grad
    branch_grad = (valid * resid_grad).astype(jnp.bfloat16)
    outproj_grad = jnp.einsum(
        "std,ste->de", attn_low, branch_grad, preferred_element_type=jnp.float32
    )
    attn_grad = jnp.einsum(
        "ste,de->std", branch_grad, out_full, preferred_element_type=jnp.float32
    ).astype(jnp.bfloat16)
    dout_heads = split_heads(attn_grad)
    delta = jnp.transpose(jnp.sum(dout_heads.astype(jnp.float32) * attn_heads, axis=-1), (0, 2, 1))
    key_all, value_all = (
        lax.all_gather(key_rows, "band", axis=1, tiled=True),
        lax.all_gather(value_rows, "band", axis=1, tiled=True),
    )
    seq_len = key_all.shape[1]
    sub_all = math.gcd(seq_len, 4 * tok_rows)
    query_parts = []
    for member in range(seqs_here):
        blocks_all = (
            key_all[member].reshape(seq_len // sub_all, sub_all, width),
            value_all[member].reshape(seq_len // sub_all, sub_all, width),
            segment_ids[member].reshape(seq_len // sub_all, sub_all),
        )
        query_part = query_heads[member]
        dout_part = dout_heads[member]
        lse_part = log_norm[member]
        delta_part = delta[member]
        seg_part = my_seg[member]

        def query_step(
            total,
            item,
            query_part=query_part,
            dout_part=dout_part,
            lse_part=lse_part,
            delta_part=delta_part,
            seg_part=seg_part,
        ):
            key_block, value_block, seg_block = item
            scores, mask = masked_scores(query_part, split_heads(key_block), seg_part, seg_block)
            probs = jnp.where(mask, jnp.exp(scores - lse_part[:, :, None]), 0.0)
            prob_grad = jnp.einsum(
                "qhd,khd->hqk",
                dout_part,
                split_heads(value_block),
                preferred_element_type=jnp.float32,
            )
            score_grad = (probs * (prob_grad - delta_part[:, :, None])).astype(jnp.bfloat16)
            return (
                total
                + jnp.einsum(
                    "hqk,khd->qhd",
                    score_grad,
                    split_heads(key_block),
                    preferred_element_type=jnp.float32,
                ),
                None,
            )

        member_grad, _ = lax.scan(
            query_step, jnp.zeros((tok_rows, HEADS, HEAD_DIM), jnp.float32), blocks_all
        )
        query_parts.append(member_grad)
    query_grad = (jnp.stack(query_parts) * HEAD_DIM ** (-0.5)).reshape(seqs_here, tok_rows, width)
    count = lax.axis_size("band") * tok_rows
    sub = math.gcd(count, 4 * tok_rows)
    columns = []
    for member in range(seqs_here):
        key_part = key_all[member]
        value_part = value_all[member]
        seg_part = segment_ids[member]

        def one_block(item, member=member):
            key_block, value_block, seg_block = item
            key_grad, value_grad = key_terms(
                query_heads[member],
                dout_heads[member],
                log_norm[member],
                delta[member],
                my_seg[member],
                split_heads(key_block),
                split_heads(value_block),
                seg_block,
            )
            return jnp.concatenate(
                [key_grad.reshape(sub, width), value_grad.reshape(sub, width)], axis=-1
            )

        stacked = (
            key_part.reshape(count // sub, sub, width),
            value_part.reshape(count // sub, sub, width),
            seg_part.reshape(count // sub, sub),
        )
        columns.append(lax.map(one_block, stacked).reshape(count, 2 * width))
    both_grads = lax.psum_scatter(
        jnp.stack(columns, axis=1).astype(jnp.bfloat16), "band", scatter_dimension=0, tiled=True
    ).astype(jnp.float32)
    both_grads = jnp.transpose(both_grads, (1, 0, 2))
    key_grad = both_grads[:, :, :width]
    value_grad = both_grads[:, :, width:]
    qkv_grad_low = jnp.concatenate([query_grad, key_grad, value_grad], axis=-1).astype(jnp.bfloat16)
    qkv_grad = jnp.einsum(
        "std,ste->de", first_low, qkv_grad_low, preferred_element_type=jnp.float32
    )
    first_grad = jnp.einsum(
        "ste,de->std", qkv_grad_low, qkv_full, preferred_element_type=jnp.float32
    )
    in_grad, gain_one_grad = norm_back(first_grad, gain_one, first_n, first_s)
    token_grad = resid_grad + in_grad
    shares = (
        lax.psum_scatter(
            qkv_grad.astype(jnp.bfloat16), "seq", scatter_dimension=0, tiled=True
        ).astype(jnp.float32),
        lax.psum_scatter(
            outproj_grad.astype(jnp.bfloat16), "seq", scatter_dimension=0, tiled=True
        ).astype(jnp.float32),
        lax.psum_scatter(
            up_grad.astype(jnp.bfloat16), "seq", scatter_dimension=0, tiled=True
        ).astype(jnp.float32),
        lax.psum_scatter(
            down_grad.astype(jnp.bfloat16), "seq", scatter_dimension=0, tiled=True
        ).astype(jnp.float32),
        lax.psum_scatter(
            gain_one_grad.astype(jnp.bfloat16), "seq", scatter_dimension=0, tiled=True
        ).astype(jnp.float32),
        lax.psum_scatter(
            gain_two_grad.astype(jnp.bfloat16), "seq", scatter_dimension=0, tiled=True
        ).astype(jnp.float32),
    )
    summed = (
        lax.psum(shares[0].astype(jnp.bfloat16), "band").astype(jnp.float32),
        lax.psum(shares[1].astype(jnp.bfloat16), "band").astype(jnp.float32),
        lax.psum(shares[2].astype(jnp.bfloat16), "band").astype(jnp.float32),
        lax.psum(shares[3].astype(jnp.bfloat16), "band").astype(jnp.float32),
        lax.psum(shares[4].astype(jnp.bfloat16), "band").astype(jnp.float32),
        lax.psum(shares[5].astype(jnp.bfloat16), "band").astype(jnp.float32),
    )
    qkv_out, outproj_out, up_out, down_out, gain_one_out, gain_two_out = summed
    return (
        layer_out,
        token_grad,
        qkv_out,
        outproj_out,
        up_out,
        down_out,
        gain_one_out,
        gain_two_out,
    )


MESH = pl.DeviceIdType.MESH
BF = jnp.bfloat16
F32 = jnp.float32
SCALE = HEAD_DIM ** (-0.5)


def place():
    b = lax.axis_index("band")
    y = lax.axis_index("seq")
    return b, y, b // 4, (b // 2) % 2, b % 2


def meet(peers):
    sem = pltpu.get_barrier_semaphore()
    for peer in peers:
        pl.semaphore_signal(sem, inc=1, device_id=peer, device_id_type=MESH)
    pl.semaphore_wait(sem, len(peers))


def send(src, dst, ssem, rsem, peer):
    copy = pltpu.make_async_remote_copy(
        src_ref=src, dst_ref=dst, send_sem=ssem, recv_sem=rsem, device_id=peer, device_id_type=MESH
    )
    copy.start()
    return copy


def comm_call(body, name, cid, outs, scratch, n_in):
    vm = pl.BlockSpec(memory_space=pltpu.VMEM)
    return pl.pallas_call(
        body,
        out_shape=[jax.ShapeDtypeStruct(s, d) for s, d in outs],
        in_specs=[vm] * n_in,
        out_specs=[vm] * len(outs),
        scratch_shapes=scratch,
        compiler_params=pltpu.CompilerParams(collective_id=cid, has_side_effects=True),
        name=name,
    )


def dma(n):
    return pltpu.SemaphoreType.DMA((n,))


def norm_rows(v):
    centre = v - jnp.mean(v, axis=-1, keepdims=True)
    inv_std = lax.rsqrt(jnp.mean(centre * centre, axis=-1, keepdims=True) + EPS)
    return centre * inv_std, inv_std


def open_body(tok, seg, wqkv, gains, tok_all, seg_all, w_sel, gains_all, ss, rs):
    b, y, z, x, c = place()
    core, over = (b + 1 - 2 * c, y), (b, 1 - y)
    meet([core, over])
    cps = []
    for m in range(2):
        cps.append(send(tok.at[m], tok_all.at[2 * y + m, c], ss.at[m], rs.at[m], over))
    cps.append(send(seg, seg_all.at[y], ss.at[2], rs.at[2], over))
    cps.append(send(gains, gains_all.at[y], ss.at[3], rs.at[3], over))
    k = 4
    far = (1 - y) * 2 + c
    own = y * 2 + c
    for hp in range(2):
        for p in range(3):
            col = pl.multiple_of(p * 1024 + far * 256 + hp * 128, 128)
            dst = w_sel.at[y, :, pl.ds(hp * 384 + p * 128, 128)]
            cps.append(send(wqkv.at[:, pl.ds(col, 128)], dst, ss.at[k], rs.at[k], over))
            k += 1
    side = []
    for m in range(2):
        side.append(send(tok.at[m], tok_all.at[2 * y + m, c], ss.at[k], rs.at[k], core))
        k += 1
    for hp in range(2):
        for p in range(3):
            col = pl.multiple_of(p * 1024 + own * 256 + hp * 128, 128)
            w_sel[y, :, hp * 384 + p * 128 : hp * 384 + p * 128 + 128] = wqkv[:, pl.ds(col, 128)]
    for m in range(2):
        tok_all[2 * y + m, c] = tok[m]
    seg_all[y] = seg[...]
    gains_all[y] = gains[...]
    for m in range(2):
        cps[m].wait_recv()
        got = tok_all.at[2 * (1 - y) + m, c]
        side.append(send(got, got, ss.at[k], rs.at[k], core))
        k += 1
    for m in range(2):
        cps[m].wait_send()
    for cp in cps[2:] + side:
        cp.wait()


def open_call(tok, seg, wqkv, gains):
    return comm_call(
        open_body,
        "open_column",
        1,
        [((4, 2, 96, 1024), BF), ((2, 2, 1536), jnp.int32), ((2, 512, 768), BF), ((2, 8, 512), F32)],
        [dma(14), dma(14)],
        4,
    )(tok, seg, wqkv, gains)


def chips(b, c, y):
    j = b // 2
    res = []
    for k in range(1, 8):
        jd = (j + k) % 8
        res.append((jd, (jd * 2 + c, y)))
    return res


def to_heads_body(qkv, up, att, up_sel, ss, rs):
    b, y, z, x, c = place()
    over = (b, 1 - y)
    others = chips(b, c, y)
    meet([over] + [peer for _, peer in others])
    j = b // 2
    cps = []
    far = pl.multiple_of(((1 - y) * 2 + c) * 1024, 1024)
    own = pl.multiple_of((y * 2 + c) * 1024, 1024)
    cps.append(send(up.at[:, pl.ds(far, 1024)], up_sel.at[y], ss.at[0], rs.at[0], over))
    for k, (jd, peer) in enumerate(others):
        col = pl.multiple_of((jd % 2) * 384, 128)
        cps.append(
            send(qkv.at[jd // 2, :, pl.ds(col, 384)], att.at[j], ss.at[k + 1], rs.at[k + 1], peer)
        )
    att[j] = qkv[z, :, pl.ds(pl.multiple_of(x * 384, 128), 384)]
    up_sel[y] = up[:, pl.ds(own, 1024)]
    for cp in cps:
        cp.wait()


def to_heads(qkv, up):
    return comm_call(
        to_heads_body,
        "to_heads",
        2,
        [((8, 192, 384), BF), ((2, 512, 1024), BF)],
        [dma(8), dma(8)],
        2,
    )(qkv, up)


def column_sum(part, got, mid, fin, ss, rs, b, y, c):
    core, over = (b + 1 - 2 * c, y), (b, 1 - y)
    first = []
    for m in range(2):
        q = 2 * (1 - y) + m
        first.append(send(part.at[q, 1 - c], got.at[q], ss.at[m], rs.at[m], core))
    for m in range(2):
        q = 2 * y + m
        first.append(send(part.at[q, 1 - c], got.at[q], ss.at[2 + m], rs.at[2 + m], core))
    second = []
    for m in range(2):
        q = 2 * (1 - y) + m
        first[m].wait_recv()
        mid[m] = (part[q, c].astype(F32) + got[q].astype(F32)).astype(BF)
        second.append(send(mid.at[m], fin.at[m], ss.at[4 + m], rs.at[4 + m], over))
    sums = []
    for m in range(2):
        q = 2 * y + m
        first[2 + m].wait_recv()
        second[m].wait_recv()
        sums.append(part[q, c].astype(F32) + got[q].astype(F32) + fin[m].astype(F32))
    for cp in first + second:
        cp.wait_send()
    return sums


def column_spread(own, full, ss, rs, k, b, y, c):
    core, over = (b + 1 - 2 * c, y), (b, 1 - y)
    near, side = [], []
    for m in range(2):
        near.append(send(own.at[m], full.at[2 * y + m, c], ss.at[k], rs.at[k], over))
        side.append(send(own.at[m], full.at[2 * y + m, c], ss.at[k + 1], rs.at[k + 1], core))
        k += 2
    for m in range(2):
        full[2 * y + m, c] = own[m]
    for m in range(2):
        near[m].wait_recv()
        got = full.at[2 * (1 - y) + m, c]
        side.append(send(got, got, ss.at[k], rs.at[k], core))
        k += 1
    for cp in near:
        cp.wait_send()
    for cp in side:
        cp.wait()


SUM_SCRATCH = [
    pltpu.VMEM((4, 96, 1024), BF),
    pltpu.VMEM((2, 96, 1024), BF),
    pltpu.VMEM((2, 96, 1024), BF),
]


def first_dot(a, d):
    return lax.dot_general(a, d, (((0,), (0,)), ((), ())), preferred_element_type=F32)


def middle_body(
    att,
    cot,
    tok,
    valid,
    valid_all,
    gain,
    out_w,
    up_w,
    down_w,
    do,
    layer_out,
    rgrad,
    ggrad,
    part,
    rows,
    cot_all,
    h_all,
    b_all,
    buf,
    gots,
    mids,
    fins,
    own,
    grad_two,
    hgrad,
    hidden,
    pgrad,
    agrad,
    resid,
    a_s,
    a_r,
    c_s,
    c_r,
    r_s,
    r_r,
    s_s,
    s_r,
    d_s,
    d_r,
):
    b, y, z, x, c = place()
    core, over = (b + 1 - 2 * c, y), (b, 1 - y)
    j = b // 2
    others = chips(b, c, y)
    mine = pl.ds(pl.multiple_of(c * 96, 32), 96)
    theirs = pl.ds(pl.multiple_of((1 - c) * 96, 32), 96)
    far = [2 * (1 - y) + m for m in range(2)]
    near = [2 * y + m for m in range(2)]
    col = pl.multiple_of(x * 128, 128)
    meet([core, over] + [peer for _, peer in others])

    def sum_start(k, q, i):
        return send(buf.at[k, q, theirs], gots.at[k, q], r_s.at[k, i], r_r.at[k, i], core)

    def sum_over(k, m, first):
        first.wait_recv()
        q = far[m]
        mids[k, m] = (buf[k, q, mine].astype(F32) + gots[k, q].astype(F32)).astype(BF)
        return send(mids.at[k, m], fins.at[k, m], r_s.at[k, 4 + m], r_r.at[k, 4 + m], over)

    def sum_end(k, m, first, second):
        first.wait_recv()
        second.wait_recv()
        q = near[m]
        return buf[k, q, mine].astype(F32) + gots[k, q].astype(F32) + fins[k, m].astype(F32)

    def spread_start(k, m, full):
        to = full.at[near[m], mine]
        full[near[m], mine] = own[k, m]
        return (
            send(own.at[k, m], to, s_s.at[k, m], s_r.at[k, m], over),
            send(own.at[k, m], to, s_s.at[k, 2 + m], s_r.at[k, 2 + m], core),
        )

    def spread_pass(k, m, full, pair):
        pair[0].wait_recv()
        got = full.at[far[m], mine]
        return send(got, got, s_s.at[k, 4 + m], s_r.at[k, 4 + m], core)

    done = []
    for k, (jd, peer) in enumerate(others):
        done.append(send(att.at[jd], rows.at[z, :, pl.ds(col, 128)], a_s.at[k], a_r.at[k], peer))
    cots = []
    for m in range(2):
        to = cot_all.at[near[m], mine]
        cots.append(send(cot.at[m], to, c_s.at[m], c_r.at[m], over))
    for m in range(2):
        to = cot_all.at[near[m], mine]
        cots.append(send(cot.at[m], to, c_s.at[2 + m], c_r.at[2 + m], core))
        cot_all[near[m], mine] = cot[m]
    rows[z, :, pl.ds(col, 128)] = att[j]
    for cp in done:
        cp.wait_recv()

    out_rows = out_w[pl.ds(pl.multiple_of(c * 256, 256), 256)]
    firsts = []
    for i, q in enumerate(far + near):
        buf[0, q] = plain_dot(rows[q], out_rows).astype(BF)
        firsts.append(sum_start(0, q, i))
    seconds = [sum_over(0, m, firsts[m]) for m in range(2)]

    down_rows = down_w[pl.ds(pl.multiple_of(c * 1024, 1024), 1024)]

    def hidden_gradient(q):
        grad_two[q] = (valid_all[q][:, :1] * cot_all[q].astype(F32)).astype(BF)
        hgrad[q] = last_dot(grad_two[q], down_rows)

    for m in range(2):
        cots[2 + m].wait_recv()
        hidden_gradient(near[m])
    passed = []
    for m in range(2):
        cots[m].wait_recv()
        got = cot_all.at[far[m], mine]
        passed.append(send(got, got, c_s.at[4 + m], c_r.at[4 + m], core))
    for m in range(2):
        passed[m].wait_recv()
        hidden_gradient(far[m])

    spread = []
    for m in range(2):
        res = tok[m].astype(F32) + valid[m][:, :1] * sum_end(0, m, firsts[2 + m], seconds[m])
        resid[m] = res
        normed, _ = norm_rows(res)
        own[0, m] = (normed * gain[1:2]).astype(BF)
        spread.append(spread_start(0, m, h_all))
    done += firsts + seconds

    def hidden_units(q):
        pre = plain_dot(h_all[q], up_w[...])
        phi = 0.5 * (1.0 + lax.erf(pre * ROOT_HALF))
        hidden[q] = (pre * phi).astype(BF)
        slope = phi + pre * DENSITY * jnp.exp(-0.5 * pre * pre)
        pgrad[q] = (hgrad[q] * slope).astype(BF)
        buf[1, q] = last_dot(pgrad[q], up_w[...]).astype(BF)

    def second_branch(q, i):
        buf[2, q] = plain_dot(hidden[q], down_rows).astype(BF)
        return sum_start(2, q, i)

    firsts, lasts = [None] * 4, [None] * 4
    for m in range(2):
        spread[m][1].wait_recv()
        hidden_units(near[m])
        firsts[2 + m] = sum_start(1, near[m], 2 + m)
    passed2, seconds = [], []
    for m in range(2):
        passed2.append(spread_pass(0, m, h_all, spread[m]))
        passed2[m].wait_recv()
        hidden_units(far[m])
        firsts[m] = sum_start(1, far[m], m)
        lasts[2 + m] = second_branch(near[m], 2 + m)
        seconds.append(sum_over(1, m, firsts[m]))

    def weight_gradient(left, right, first_chunk):
        for i in range(4):
            block = left[:, :, i * 256 : i * 256 + 256].reshape(768, 256)
            res = first_dot(block, right[...].reshape(768, 1024)).astype(BF)
            for k in range(4):
                part[first_chunk + k, i // 2, (i % 2) * 256 : (i % 2) * 256 + 256] = res[
                    :, k * 256 : k * 256 + 256
                ]

    weight_gradient(hidden, grad_two, 0)

    total = jnp.zeros((1, 1024), F32)
    bspread = []
    for m in range(2):
        e = sum_end(1, m, firsts[2 + m], seconds[m])
        normed, inv_std = norm_rows(resid[m])
        g = e * gain[1:2]
        total = total + jnp.sum(e * normed, axis=0, keepdims=True)
        one = jnp.mean(g, axis=-1, keepdims=True)
        two = jnp.mean(g * normed, axis=-1, keepdims=True)
        rg = cot[m].astype(F32) + (g - one - normed * two) * inv_std
        rgrad[m] = rg
        own[1, m] = (valid[m][:, :1] * rg).astype(BF)
        bspread.append(spread_start(1, m, b_all))
    ggrad[...] = jnp.broadcast_to(total, (8, 1024))
    done += firsts + seconds

    for m in range(2):
        lasts[m] = second_branch(far[m], m)
    lseconds = [sum_over(2, m, lasts[m]) for m in range(2)]
    weight_gradient(h_all, pgrad, 4)

    def grad_copy(q, xd, i):
        dest = q * 2 + xd
        return dest, pltpu.make_async_remote_copy(
            src_ref=agrad.at[q, :, pl.ds(xd * 128, 128)],
            dst_ref=do.at[j],
            send_sem=d_s.at[i, xd],
            recv_sem=d_r.at[j],
            device_id=(dest * 2 + c, y),
            device_id_type=MESH,
        )

    def attention_gradient(q, i):
        agrad[q] = last_dot(b_all[q], out_rows).astype(BF)
        for xd in range(2):
            dest, cp = grad_copy(q, xd, i)

            @pl.when(dest != j)
            def _():
                cp.start()

            @pl.when(dest == j)
            def _():
                do[j] = agrad[q, :, xd * 128 : xd * 128 + 128]

    for m in range(2):
        bspread[m][1].wait_recv()
        attention_gradient(near[m], 2 + m)
    passed3 = []
    for m in range(2):
        passed3.append(spread_pass(1, m, b_all, bspread[m]))
        passed3[m].wait_recv()
        attention_gradient(far[m], m)

    res = first_dot(rows[...].reshape(768, 256), b_all[...].reshape(768, 1024)).astype(BF)
    for h in range(2):
        for k in range(2):
            at = (h * 2 + k) * 256
            part[8, h, k * 256 : k * 256 + 256] = res[:, at : at + 256]

    for m in range(2):
        branch = sum_end(2, m, lasts[2 + m], lseconds[m])
        layer_out[m] = (resid[m] + valid[m][:, :1] * branch).astype(BF)
    done += lasts + lseconds + cots + passed + passed2 + passed3
    for pair in spread + bspread:
        done += list(pair)
    for cp in done:
        cp.wait_send()
    for i, q in enumerate(far + near):
        for xd in range(2):
            dest, cp = grad_copy(q, xd, i)

            @pl.when(dest != j)
            def _():
                cp.wait_send()

    for k in range(1, 8):
        js = (j + k) % 8
        pltpu.make_async_remote_copy(
            src_ref=agrad.at[0, :, pl.ds(0, 128)],
            dst_ref=do.at[js],
            send_sem=d_s.at[0, 0],
            recv_sem=d_r.at[js],
            device_id=core,
            device_id_type=MESH,
        ).wait_recv()


def middle(att, cot, tok, valid, valid_all, gain, out_w, up_w, down_w):
    rows192 = (4, 192, 1024)
    return comm_call(
        middle_body,
        "middle",
        3,
        [
            ((8, 192, 128), BF),
            ((2, 96, 1024), BF),
            ((2, 96, 1024), F32),
            ((8, 1024), F32),
            ((9, 2, 512, 256), BF),
        ],
        [
            pltpu.VMEM((4, 192, 256), BF),
            pltpu.VMEM(rows192, BF),
            pltpu.VMEM(rows192, BF),
            pltpu.VMEM(rows192, BF),
            pltpu.VMEM((3,) + rows192, BF),
            pltpu.VMEM((3, 4, 96, 1024), BF),
            pltpu.VMEM((3, 2, 96, 1024), BF),
            pltpu.VMEM((3, 2, 96, 1024), BF),
            pltpu.VMEM((2, 2, 96, 1024), BF),
            pltpu.VMEM(rows192, BF),
            pltpu.VMEM(rows192, F32),
            pltpu.VMEM(rows192, BF),
            pltpu.VMEM(rows192, BF),
            pltpu.VMEM((4, 192, 256), BF),
            pltpu.VMEM((2, 96, 1024), F32),
            dma(7),
            dma(7),
            dma(6),
            dma(6),
            pltpu.SemaphoreType.DMA((3, 6)),
            pltpu.SemaphoreType.DMA((3, 6)),
            pltpu.SemaphoreType.DMA((2, 6)),
            pltpu.SemaphoreType.DMA((2, 6)),
            pltpu.SemaphoreType.DMA((4, 2)),
            dma(8),
        ],
        9,
    )(att, cot, tok, valid, valid_all, gain, out_w, up_w, down_w)


def grad_rows_body(dqkv, rows, ss, rs):
    b, y, z, x, c = place()
    others = chips(b, c, y)
    meet([peer for _, peer in others])
    col = pl.multiple_of(x * 384, 128)
    cps = []
    for k, (jd, peer) in enumerate(others):
        cps.append(send(dqkv.at[jd], rows.at[z, :, pl.ds(col, 384)], ss.at[k], rs.at[k], peer))
    rows[z, :, pl.ds(col, 384)] = dqkv[b // 2]
    for cp in cps:
        cp.wait()


def grad_rows(dqkv):
    return comm_call(
        grad_rows_body, "grad_rows", 7, [((4, 192, 768), BF)], [dma(7), dma(7)], 1
    )(dqkv)[0]


def first_back_body(part, tok, rgrad, gain, tgrad, ggrad, got, mid, fin, ss, rs):
    b, y, z, x, c = place()
    meet([(b + 1 - 2 * c, y), (b, 1 - y)])
    sums = column_sum(part, got, mid, fin, ss, rs, b, y, c)
    total = jnp.zeros((1, 1024), F32)
    for m in range(2):
        normed, inv_std = norm_rows(tok[m].astype(F32))
        e = sums[m]
        g = e * gain[0:1]
        total = total + jnp.sum(e * normed, axis=0, keepdims=True)
        one = jnp.mean(g, axis=-1, keepdims=True)
        two = jnp.mean(g * normed, axis=-1, keepdims=True)
        tgrad[m] = rgrad[m] + (g - one - normed * two) * inv_std
    ggrad[...] = jnp.broadcast_to(total, (8, 1024))


def first_back(part, tok, rgrad, gain):
    return comm_call(
        first_back_body,
        "first_back",
        8,
        [((2, 96, 1024), F32), ((8, 1024), F32)],
        SUM_SCRATCH + [dma(6), dma(6)],
        4,
    )(part, tok, rgrad, gain)


def last_dot(a, b):
    return lax.dot_general(a, b, (((1,), (1,)), ((), ())), preferred_element_type=F32)


def plain_dot(a, b):
    return lax.dot_general(a, b, (((1,), (0,)), ((), ())), preferred_element_type=F32)


def attend_body(qkv, seg_col, seg_row, out_low, out, lse):
    rows = out.shape[0]
    i = pl.program_id(0)
    at = pl.multiple_of(i * rows, rows)
    q = qkv[pl.ds(at, rows), 0:128]
    keys = qkv[:, 128:256]
    values = qkv[:, 256:384]
    low_half = lax.broadcasted_iota(jnp.int32, (rows, 128), 1) < HEAD_DIM
    mask = seg_col[:, 0:1] == seg_row[0:1, :]
    outs, norms = [], []
    for h in range(2):
        qh = jnp.where(low_half if h == 0 else ~low_half, q * SCALE, 0.0).astype(BF)
        scores = jnp.where(mask, last_dot(qh, keys), NEG)
        top = jnp.max(scores, axis=-1, keepdims=True)
        probs = jnp.exp(scores - top)
        total = jnp.sum(probs, axis=-1, keepdims=True)
        outs.append(plain_dot(probs.astype(BF), values) / total)
        norms.append(top + jnp.log(total))
    res = jnp.where(low_half, outs[0], outs[1])
    out[...] = res
    out_low[...] = res.astype(BF)
    lse[...] = jnp.where(low_half, norms[0], norms[1])


def attend(qkv, seg_col, seg_row):
    length = qkv.shape[0]
    rows = 256
    tile = pl.BlockSpec((rows, 128), lambda i: (i, 0))
    return pl.pallas_call(
        attend_body,
        grid=(length // rows,),
        in_specs=[
            pl.BlockSpec((length, 384), lambda i: (0, 0)),
            pl.BlockSpec((rows, 128), lambda i: (i, 0)),
            pl.BlockSpec((8, length), lambda i: (0, 0)),
        ],
        out_specs=[tile, tile, tile],
        out_shape=[
            jax.ShapeDtypeStruct((length, 128), BF),
            jax.ShapeDtypeStruct((length, 128), F32),
            jax.ShapeDtypeStruct((length, 128), F32),
        ],
        name="attend",
    )(qkv, seg_col, seg_row)


def attend_back_body(qkv, out, lse, do, seg_col, seg_row, dqkv, lse_t, delta, keys_t, dq_t):
    length = qkv.shape[0]
    rows = seg_col.shape[0]
    i = pl.program_id(0)
    at = pl.multiple_of(i * rows, rows)

    @pl.when(i == 0)
    def _():
        lse_t[...] = jnp.transpose(lse[...])
        prod = jnp.transpose(do[...].astype(F32) * out[...])
        delta[0:8] = jnp.broadcast_to(jnp.sum(prod[:HEAD_DIM], axis=0, keepdims=True), (8, length))
        delta[8:16] = jnp.broadcast_to(jnp.sum(prod[HEAD_DIM:], axis=0, keepdims=True), (8, length))
        keys_t[...] = jnp.transpose(qkv[:, 128:256].astype(F32)).astype(BF)
        dq_t[...] = jnp.zeros_like(dq_t)

    keys = qkv[pl.ds(at, rows), 128:256]
    values = qkv[pl.ds(at, rows), 256:384]
    q = qkv[:, 0:128]
    douts = do[...]
    low_half = lax.broadcasted_iota(jnp.int32, (rows, 128), 1) < HEAD_DIM
    low_rows = lax.broadcasted_iota(jnp.int32, (128, 1), 0) < HEAD_DIM
    mask = seg_col[:, 0:1] == seg_row[0:1, :]
    kgrads, vgrads, qgrads = [], [], []
    for h in range(2):
        pick = low_half if h == 0 else ~low_half
        kh = jnp.where(pick, keys * SCALE, 0.0).astype(BF)
        vh = jnp.where(pick, values, 0.0).astype(BF)
        scores = last_dot(kh, q)
        probs = jnp.where(mask, jnp.exp(scores - lse_t[h * HEAD_DIM : h * HEAD_DIM + 1]), 0.0)
        vgrads.append(plain_dot(probs.astype(BF), douts))
        pgrad = last_dot(vh, douts)
        sgrad = (probs * (pgrad - delta[h * 8 : h * 8 + 1])).astype(BF)
        kgrads.append(plain_dot(sgrad, q))
        qgrads.append(plain_dot(keys_t[:, pl.ds(at, rows)], sgrad))
    dq_t[...] += jnp.where(low_rows, qgrads[0], qgrads[1])
    dqkv[pl.ds(at, rows), 128:256] = (jnp.where(low_half, kgrads[0], kgrads[1]) * SCALE).astype(BF)
    dqkv[pl.ds(at, rows), 256:384] = jnp.where(low_half, vgrads[0], vgrads[1]).astype(BF)

    @pl.when(i == pl.num_programs(0) - 1)
    def _():
        dqkv[:, 0:128] = (jnp.transpose(dq_t[...]) * SCALE).astype(BF)


def attend_back(qkv, out, lse, do, seg_col, seg_row):
    length = qkv.shape[0]
    rows = 256
    whole = pl.BlockSpec((length, 128), lambda i: (0, 0))
    wide = pl.BlockSpec((length, 384), lambda i: (0, 0))
    return pl.pallas_call(
        attend_back_body,
        grid=(length // rows,),
        in_specs=[
            wide,
            whole,
            whole,
            whole,
            pl.BlockSpec((rows, 128), lambda i: (i, 0)),
            pl.BlockSpec((8, length), lambda i: (0, 0)),
        ],
        out_specs=wide,
        out_shape=jax.ShapeDtypeStruct((length, 384), BF),
        scratch_shapes=[
            pltpu.VMEM((128, length), F32),
            pltpu.VMEM((16, length), F32),
            pltpu.VMEM((128, length), BF),
            pltpu.VMEM((128, length), F32),
        ],
        name="attend_back",
    )(qkv, out, lse, do, seg_col, seg_row)


CHUNKS = 12
SWAPPED = ((4, 8), (9, 12))


def wsum_body(part, gg, full, gsum, r1, s1, r2, s2, r3, p3, tmp, g1, g2, g3, ss, rs, ls, gs, gr):
    b, y, z, x, c = place()
    others = chips(b, c, y)
    z0, zb = z % 2, z // 2
    core, over = (b + 1 - 2 * c, y), (b, 1 - y)
    px, p0, pb = (b + 2 - 4 * x, y), (b + 4 - 8 * z0, y), (b + 8 - 16 * zb, y)
    o1 = x * 256
    o2 = o1 + z0 * 128
    o3 = o2 + zb * 64

    def rows(start, size):
        return pl.ds(pl.multiple_of(start, 64), size)

    def remote(src, dst, stage, i, peer):
        return pltpu.make_async_remote_copy(
            src_ref=src,
            dst_ref=dst,
            send_sem=ss.at[stage, i],
            recv_sem=rs.at[stage, i],
            device_id=peer,
            device_id_type=MESH,
        )

    def c_x(i):
        return remote(part.at[i, :, rows((1 - x) * 256, 256)], r1.at[i], 0, i, px)

    def c_z0(i):
        return remote(s1.at[i, :, rows((1 - z0) * 128, 128)], r2.at[i], 1, i, p0)

    def c_zb(i):
        return remote(s2.at[i, :, rows((1 - zb) * 64, 64)], r3.at[i], 2, i, pb)

    def c_y(i):
        return remote(tmp.at[i], p3.at[i, y], 3, i, over)

    def c_gb(i):
        return remote(p3.at[i], full.at[i, c, :, rows(o3, 64)], 4, i, pb)

    def c_own(i):
        return pltpu.make_async_copy(p3.at[i], full.at[i, c, :, rows(o3, 64)], ls.at[i])

    def c_g0(i):
        src = full.at[i, c, :, rows(o2, 128)]
        return remote(src, src, 5, i, p0)

    def c_gx(i):
        src = full.at[i, c, :, rows(o1, 256)]
        return remote(src, src, 6, i, px)

    def c_core(i):
        src = full.at[i, c]
        return remote(src, src, 7, i, core)

    meet([core, over] + [peer for _, peer in others])

    @pl.loop(0, CHUNKS)
    def _(i):
        c_x(i).start()

    gcps = [send(gg, g1.at[0], gs.at[0], gr.at[0], core)]
    gcps[0].wait_recv()
    g1[1] = g1[0] + gg[...]
    gcps.append(send(g1.at[1], g2.at[0], gs.at[1], gr.at[1], over))
    gcps[1].wait_recv()
    j = b // 2
    g3[j] = g1[1] + g2[0]
    for k, (jd, peer) in enumerate(others):
        gcps.append(send(g3.at[j], g3.at[j], gs.at[2 + k], gr.at[2 + k], peer))

    def when_chunk(t, lag, act, ranges=((0, CHUNKS),)):
        for lo, hi in ranges:

            @pl.when((t - lag >= lo) & (t - lag < hi))
            def _():
                act(t - lag)

    def add_x(i):
        c_x(i).wait_recv()
        mine = part[i, :, rows(x * 256, 256)].astype(F32)
        s1[i] = (mine + r1[i].astype(F32)).astype(BF)
        c_z0(i).start()

    def add_z0(i):
        c_z0(i).wait_recv()
        mine = s1[i, :, rows(z0 * 128, 128)].astype(F32)
        s2[i] = (mine + r2[i].astype(F32)).astype(BF)
        c_zb(i).start()

    def add_zb_plain(i):
        c_zb(i).wait_recv()
        mine = s2[i, :, rows(zb * 64, 64)].astype(F32)
        p3[i] = (mine + r3[i].astype(F32)).astype(BF)
        c_gb(i).start()
        c_own(i).start()

    def add_zb_swap(i):
        c_zb(i).wait_recv()
        for h, dst in ((y, p3.at[i, y]), (1 - y, tmp.at[i])):
            mine = s2[i, h, rows(zb * 64, 64)].astype(F32)
            dst[...] = (mine + r3[i, h].astype(F32)).astype(BF)
        c_y(i).start()

    def take_y(i):
        c_y(i).wait_recv()
        c_gb(i).start()
        c_own(i).start()

    def grow_z0(i):
        c_gb(i).wait_recv()
        c_own(i).wait()
        c_g0(i).start()

    def grow_x(i):
        c_g0(i).wait_recv()
        c_gx(i).start()

    def grow_core(i):
        c_gx(i).wait_recv()
        c_core(i).start()

    plain = ((0, 4), (8, 9))

    @pl.loop(0, CHUNKS + 6)
    def _(t):
        when_chunk(t, 6, grow_core)
        when_chunk(t, 5, grow_x)
        when_chunk(t, 4, grow_z0)
        when_chunk(t, 3, take_y, SWAPPED)
        when_chunk(t, 2, add_zb_plain, plain)
        when_chunk(t, 2, add_zb_swap, SWAPPED)
        when_chunk(t, 1, add_z0)
        when_chunk(t, 0, add_x)

    @pl.loop(0, CHUNKS)
    def _(i):
        c_core(i).wait_recv()
        for cp in (c_x, c_z0, c_zb, c_gb, c_g0, c_gx, c_core):
            cp(i).wait_send()

    for lo, hi in SWAPPED:

        @pl.loop(lo, hi)
        def _(i):
            c_y(i).wait_send()

    for cp in gcps[:2]:
        cp.wait_send()
    for cp in gcps[2:]:
        cp.wait()
    total = g3[0]
    for k in range(1, 8):
        total = total + g3[k]
    gsum[...] = total


def weight_sums(part, gg):
    return pl.pallas_call(
        wsum_body,
        out_shape=[
            jax.ShapeDtypeStruct((CHUNKS, 2, 2, 512, 256), BF),
            jax.ShapeDtypeStruct((8, 1024), F32),
        ],
        in_specs=[pl.BlockSpec(memory_space=pltpu.VMEM)] * 2,
        out_specs=[pl.BlockSpec(memory_space=pl.ANY), pl.BlockSpec(memory_space=pltpu.VMEM)],
        scratch_shapes=[
            pltpu.VMEM((CHUNKS, 2, 256, 256), BF),
            pltpu.VMEM((CHUNKS, 2, 256, 256), BF),
            pltpu.VMEM((CHUNKS, 2, 128, 256), BF),
            pltpu.VMEM((CHUNKS, 2, 128, 256), BF),
            pltpu.VMEM((CHUNKS, 2, 64, 256), BF),
            pltpu.VMEM((CHUNKS, 2, 64, 256), BF),
            pltpu.VMEM((CHUNKS, 64, 256), BF),
            pltpu.VMEM((2, 8, 1024), F32),
            pltpu.VMEM((1, 8, 1024), F32),
            pltpu.VMEM((8, 8, 1024), F32),
            pltpu.SemaphoreType.DMA((8, CHUNKS)),
            pltpu.SemaphoreType.DMA((8, CHUNKS)),
            pltpu.SemaphoreType.DMA((CHUNKS,)),
            dma(9),
            dma(9),
        ],
        compiler_params=pltpu.CompilerParams(collective_id=9, has_side_effects=True),
        name="weight_sums",
    )(part, gg)


def widen_body(src, dst):
    for k in range(4):
        dst[:, k * 256 : k * 256 + 256] = src[k].astype(F32)


def widen_out_body(src, dst):
    for h in range(2):
        for k in range(2):
            col = (h * 2 + k) * 256
            dst[:, col : col + 256] = src[h, k * 256 : k * 256 + 256].astype(F32)


def widen_qkv_body(src, dst):
    for r in range(4):
        for t in range(6):
            col = (t % 3) * 1024 + r * 256 + (t // 3) * 128
            half = (t % 2) * 128
            dst[:, col : col + 128] = src[t // 2, r % 2, r // 2, :, half : half + 128].astype(F32)


def widen_all(full):
    down = pl.pallas_call(
        widen_body,
        grid=(4,),
        in_specs=[pl.BlockSpec((4, None, None, 512, 256), lambda r: (0, r // 2, r % 2, 0, 0))],
        out_specs=pl.BlockSpec((512, 1024), lambda r: (r, 0)),
        out_shape=jax.ShapeDtypeStruct((2048, 1024), F32),
        name="widen_down",
    )(full)
    up = pl.pallas_call(
        widen_body,
        grid=(4,),
        in_specs=[pl.BlockSpec((4, None, None, 512, 256), lambda r: (1, r % 2, r // 2, 0, 0))],
        out_specs=pl.BlockSpec((512, 1024), lambda r: (0, r)),
        out_shape=jax.ShapeDtypeStruct((512, 4096), F32),
        name="widen_up",
    )(full)
    out = pl.pallas_call(
        widen_out_body,
        grid=(2,),
        in_specs=[pl.BlockSpec((None, None, 2, 512, 256), lambda r: (8, r, 0, 0, 0))],
        out_specs=pl.BlockSpec((256, 1024), lambda r: (r, 0)),
        out_shape=jax.ShapeDtypeStruct((512, 1024), F32),
        name="widen_out",
    )(full)
    qkv = pl.pallas_call(
        widen_qkv_body,
        grid=(4,),
        in_specs=[pl.BlockSpec((3, 2, 2, 128, 256), lambda i: (3, 0, 0, i, 0))],
        out_specs=pl.BlockSpec((128, 3072), lambda i: (i, 0)),
        out_shape=jax.ShapeDtypeStruct((512, 3072), F32),
        name="widen_qkv",
    )(full)
    return down, up, out, qkv


def column_device(
    tokens,
    segment_ids,
    qkv_weight,
    out_weight,
    up_weight,
    down_weight,
    gain_first,
    gain_second,
    out_cotangent,
):
    b, y, z, x, c = place()
    my_seg = lax.dynamic_slice_in_dim(segment_ids, b * 96, 96, 1)
    valid = jnp.broadcast_to((my_seg >= 0).astype(F32)[:, :, None], (2, 96, 128))
    gains = jnp.pad(jnp.stack([gain_first, gain_second]).astype(F32), ((0, 6), (0, 0)))
    tok_all, seg_all, w_sel, gains_all = open_call(tokens, segment_ids, qkv_weight, gains)
    gain = jnp.transpose(gains_all, (1, 0, 2)).reshape(8, 1024)
    seg_all = seg_all.reshape(4, 1536)
    seg_z = lax.dynamic_slice_in_dim(seg_all, z, 1, 0)
    seg_row = jnp.broadcast_to(seg_z, (8, 1536))
    seg_col = jnp.broadcast_to(seg_z.reshape(1536, 1), (1536, 128))
    seg_here = lax.dynamic_slice_in_dim(seg_all, (z * 2 + x) * 192, 192, 1)
    valid_all = jnp.broadcast_to((seg_here >= 0).astype(F32)[:, :, None], (4, 192, 128))
    w_sel = w_sel.reshape(1024, 768)
    normed, _ = norm_rows(tok_all.reshape(768, 1024).astype(F32))
    h_one = (normed * gain[0:1]).astype(BF)
    qkv = plain_dot(h_one, w_sel).astype(BF)
    att, up_sel = to_heads(qkv.reshape(4, 192, 768), up_weight)
    up_sel = up_sel.reshape(1024, 1024)
    att = att.reshape(1536, 384)
    out_low, out_full, lse = attend(att, seg_col, seg_row)
    do, layer_out, rgrad, gain_two_grad, part = middle(
        out_low.reshape(8, 192, 128),
        out_cotangent,
        tokens,
        valid,
        valid_all,
        gain,
        out_weight,
        up_sel,
        down_weight,
    )
    dqkv = attend_back(att, out_full, lse, do.reshape(1536, 128), seg_col, seg_row)
    dqkv_rows = grad_rows(dqkv.reshape(8, 192, 384)).reshape(768, 768)
    c_part = last_dot(dqkv_rows, w_sel).astype(BF)
    token_grad, gain_one_grad = first_back(c_part.reshape(4, 2, 96, 1024), tokens, rgrad, gain)
    qkv_grad = first_dot(h_one, dqkv_rows)
    part = jnp.concatenate(
        [part, jnp.transpose(qkv_grad.astype(BF).reshape(2, 512, 3, 256), (2, 0, 1, 3))], 0
    )
    rows8 = lax.broadcasted_iota(jnp.int32, (8, 1024), 0)
    full, gain_sum = weight_sums(part, jnp.where(rows8 == 0, gain_one_grad, gain_two_grad))
    down_out, up_out, out_out, qkv_out = widen_all(full)
    gain_out = lax.dynamic_slice_in_dim(gain_sum, y * 512, 512, 1)
    return (
        layer_out,
        token_grad,
        qkv_out,
        out_out,
        up_out,
        down_out,
        gain_out[0],
        gain_out[1],
    )


def solution(mesh):
    placed = (
        P("seq", "band", None),
        P("seq", None),
        P("seq", None),
        P("seq", None),
        P("seq", None),
        P("seq", None),
        P("seq"),
        P("seq"),
        P("seq", "band", None),
    )
    split = dict(mesh.shape) == {"band": 16, "seq": 2}
    return jax.shard_map(
        column_device if split else per_device,
        mesh=mesh,
        in_specs=placed,
        out_specs=(
            P("seq", "band", None),
            P("seq", "band", None),
            P("seq", None),
            P("seq", None),
            P("seq", None),
            P("seq", None),
            P("seq"),
            P("seq"),
        ),
        check_vma=False,
    )
```

```python
import functools
import math

import jax
import jax.numpy as jnp
from jax import lax
from jax.experimental import pallas as pl
from jax.experimental.pallas import tpu as pltpu
from jax.sharding import PartitionSpec as P

HEADS = 16
HEAD_DIM = 64


EPS = 1e-06
NEG = -1e30
ROOT_HALF = 0.7071067811865476
DENSITY = 0.3989422804014327


def layer_norm(values, gain):
    centre = values - jnp.mean(values, axis=-1, keepdims=True)
    inv_std = lax.rsqrt(jnp.mean(centre * centre, axis=-1, keepdims=True) + EPS)
    normed = centre * inv_std
    return (normed * gain, normed, inv_std)


def norm_back(grad_in, gain, normed, inv_std):
    scaled = grad_in * gain
    mean_one = jnp.mean(scaled, axis=-1, keepdims=True)
    mean_two = jnp.mean(scaled * normed, axis=-1, keepdims=True)
    gain_grad = jnp.sum((grad_in * normed).reshape(-1, grad_in.shape[-1]), axis=0)
    return (inv_std * (scaled - mean_one - normed * mean_two), gain_grad)


def split_heads(matrix):
    return matrix.reshape(matrix.shape[:-1] + (HEADS, HEAD_DIM))


def masked_scores(query_part, key_part, query_seg, key_seg):
    scores = jnp.einsum(
        "qhd,khd->hqk", query_part, key_part, preferred_element_type=jnp.float32
    ) * HEAD_DIM ** (-0.5)
    return (scores, (query_seg[:, None] == key_seg[None, :])[None])


def key_terms(
    query_part, dout_part, lse_part, delta_part, query_seg, key_part, value_part, key_seg
):
    scores, mask = masked_scores(query_part, key_part, query_seg, key_seg)
    probs = jnp.where(mask, jnp.exp(scores - lse_part[:, :, None]), 0.0)
    value_grad = jnp.einsum(
        "hqk,qhd->khd", probs.astype(jnp.bfloat16), dout_part, preferred_element_type=jnp.float32
    )
    prob_grad = jnp.einsum(
        "qhd,khd->hqk", dout_part, value_part, preferred_element_type=jnp.float32
    )
    score_grad = (probs * (prob_grad - delta_part[:, :, None])).astype(jnp.bfloat16)
    key_grad = jnp.einsum(
        "hqk,qhd->khd", score_grad, query_part, preferred_element_type=jnp.float32
    ) * HEAD_DIM ** (-0.5)
    return (key_grad, value_grad)


def online_step(query_part, query_seg):

    def step(state, item):
        key_block, value_block, seg_block = item
        run_max, run_sum, run_acc = state
        scores, mask = masked_scores(query_part, split_heads(key_block), query_seg, seg_block)
        masked = jnp.where(mask, scores, NEG)
        top = jnp.maximum(run_max, jnp.max(masked, axis=-1))
        correct = jnp.exp(run_max - top)
        probs = jnp.where(mask, jnp.exp(masked - top[:, :, None]), 0.0)
        update = jnp.einsum(
            "hqk,khd->hqd",
            probs.astype(jnp.bfloat16),
            split_heads(value_block),
            preferred_element_type=jnp.float32,
        )
        return (
            (
                top,
                run_sum * correct + jnp.sum(probs, axis=-1),
                run_acc * correct[:, :, None] + update,
            ),
            None,
        )

    return step


def per_device(
    tokens,
    segment_ids,
    qkv_weight,
    out_weight,
    up_weight,
    down_weight,
    gain_first,
    gain_second,
    out_cotangent,
):
    seqs_here = tokens.shape[0]
    tok_rows = tokens.shape[1]
    width = tokens.shape[2]
    my_seg = lax.dynamic_slice_in_dim(segment_ids, lax.axis_index("band") * tok_rows, tok_rows, 1)
    valid = (my_seg >= 0).astype(jnp.float32)[:, :, None]
    qkv_full, out_full, up_full, down_full, gain_one, gain_two = (
        lax.all_gather(qkv_weight, "seq", axis=0, tiled=True),
        lax.all_gather(out_weight, "seq", axis=0, tiled=True),
        lax.all_gather(up_weight, "seq", axis=0, tiled=True),
        lax.all_gather(down_weight, "seq", axis=0, tiled=True),
        lax.all_gather(gain_first, "seq", axis=0, tiled=True),
        lax.all_gather(gain_second, "seq", axis=0, tiled=True),
    )
    gain_one = gain_one.astype(jnp.float32)
    gain_two = gain_two.astype(jnp.float32)
    inputs = tokens.astype(jnp.float32)
    first_h, first_n, first_s = layer_norm(inputs, gain_one)
    first_low = first_h.astype(jnp.bfloat16)
    qkv_rows = jnp.einsum(
        "std,de->ste", first_low, qkv_full, preferred_element_type=jnp.float32
    ).astype(jnp.bfloat16)
    query_rows = qkv_rows[:, :, :width]
    key_rows = qkv_rows[:, :, width : 2 * width]
    value_rows = qkv_rows[:, :, 2 * width :]
    query_heads = split_heads(query_rows)

    def online(carry, pieces):
        key_piece, value_piece = pieces
        count = key_piece.shape[1]
        sub = math.gcd(count, 4 * tok_rows)
        results = []
        for member in range(seqs_here):
            state = (carry[0][member], carry[1][member], carry[2][member])
            stacked = (
                key_piece[member].reshape(count // sub, sub, width),
                value_piece[member].reshape(count // sub, sub, width),
                segment_ids[member].reshape(count // sub, sub),
            )
            state, _ = lax.scan(online_step(query_heads[member], my_seg[member]), state, stacked)
            results.append(state)
        return tuple((jnp.stack([result[part] for result in results]) for part in range(3)))

    start_state = (
        jnp.full((seqs_here, HEADS, tok_rows), NEG, jnp.float32),
        jnp.zeros((seqs_here, HEADS, tok_rows), jnp.float32),
        jnp.zeros((seqs_here, HEADS, tok_rows, HEAD_DIM), jnp.float32),
    )
    run_max, run_sum, run_acc = online(
        start_state,
        (
            lax.all_gather(key_rows, "band", axis=1, tiled=True),
            lax.all_gather(value_rows, "band", axis=1, tiled=True),
        ),
    )
    log_norm = run_max + jnp.log(run_sum)
    attn_heads = jnp.transpose(run_acc / run_sum[:, :, :, None], (0, 2, 1, 3))
    attn_rows = attn_heads.reshape(seqs_here, tok_rows, width)
    attn_low = attn_rows.astype(jnp.bfloat16)
    resid = inputs + valid * jnp.einsum(
        "std,de->ste", attn_low, out_full, preferred_element_type=jnp.float32
    )
    second_h, second_n, second_s = layer_norm(resid, gain_two)
    second_low = second_h.astype(jnp.bfloat16)
    pre_act = jnp.einsum("std,df->stf", second_low, up_full, preferred_element_type=jnp.float32)
    hidden_low = jax.nn.gelu(pre_act, approximate=False).astype(jnp.bfloat16)
    branch_two = jnp.einsum(
        "stf,fd->std", hidden_low, down_full, preferred_element_type=jnp.float32
    )
    layer_out = (resid + valid * branch_two).astype(jnp.bfloat16)
    grad_out = out_cotangent.astype(jnp.float32)
    grad_two = (valid * grad_out).astype(jnp.bfloat16)
    down_grad = jnp.einsum("stf,std->fd", hidden_low, grad_two, preferred_element_type=jnp.float32)
    hidden_grad = jnp.einsum("std,fd->stf", grad_two, down_full, preferred_element_type=jnp.float32)
    slope = 0.5 * (1.0 + lax.erf(pre_act * ROOT_HALF)) + pre_act * DENSITY * jnp.exp(
        -0.5 * pre_act * pre_act
    )
    pre_grad = (hidden_grad * slope).astype(jnp.bfloat16)
    up_grad = jnp.einsum("std,stf->df", second_low, pre_grad, preferred_element_type=jnp.float32)
    second_grad = jnp.einsum("stf,df->std", pre_grad, up_full, preferred_element_type=jnp.float32)
    norm_grad, gain_two_grad = norm_back(second_grad, gain_two, second_n, second_s)
    resid_grad = grad_out + norm_grad
    branch_grad = (valid * resid_grad).astype(jnp.bfloat16)
    outproj_grad = jnp.einsum(
        "std,ste->de", attn_low, branch_grad, preferred_element_type=jnp.float32
    )
    attn_grad = jnp.einsum(
        "ste,de->std", branch_grad, out_full, preferred_element_type=jnp.float32
    ).astype(jnp.bfloat16)
    dout_heads = split_heads(attn_grad)
    delta = jnp.transpose(jnp.sum(dout_heads.astype(jnp.float32) * attn_heads, axis=-1), (0, 2, 1))
    key_all, value_all = (
        lax.all_gather(key_rows, "band", axis=1, tiled=True),
        lax.all_gather(value_rows, "band", axis=1, tiled=True),
    )
    seq_len = key_all.shape[1]
    sub_all = math.gcd(seq_len, 4 * tok_rows)
    query_parts = []
    for member in range(seqs_here):
        blocks_all = (
            key_all[member].reshape(seq_len // sub_all, sub_all, width),
            value_all[member].reshape(seq_len // sub_all, sub_all, width),
            segment_ids[member].reshape(seq_len // sub_all, sub_all),
        )
        query_part = query_heads[member]
        dout_part = dout_heads[member]
        lse_part = log_norm[member]
        delta_part = delta[member]
        seg_part = my_seg[member]

        def query_step(
            total,
            item,
            query_part=query_part,
            dout_part=dout_part,
            lse_part=lse_part,
            delta_part=delta_part,
            seg_part=seg_part,
        ):
            key_block, value_block, seg_block = item
            scores, mask = masked_scores(query_part, split_heads(key_block), seg_part, seg_block)
            probs = jnp.where(mask, jnp.exp(scores - lse_part[:, :, None]), 0.0)
            prob_grad = jnp.einsum(
                "qhd,khd->hqk",
                dout_part,
                split_heads(value_block),
                preferred_element_type=jnp.float32,
            )
            score_grad = (probs * (prob_grad - delta_part[:, :, None])).astype(jnp.bfloat16)
            return (
                total
                + jnp.einsum(
                    "hqk,khd->qhd",
                    score_grad,
                    split_heads(key_block),
                    preferred_element_type=jnp.float32,
                ),
                None,
            )

        member_grad, _ = lax.scan(
            query_step, jnp.zeros((tok_rows, HEADS, HEAD_DIM), jnp.float32), blocks_all
        )
        query_parts.append(member_grad)
    query_grad = (jnp.stack(query_parts) * HEAD_DIM ** (-0.5)).reshape(seqs_here, tok_rows, width)
    count = lax.axis_size("band") * tok_rows
    sub = math.gcd(count, 4 * tok_rows)
    columns = []
    for member in range(seqs_here):
        key_part = key_all[member]
        value_part = value_all[member]
        seg_part = segment_ids[member]

        def one_block(item, member=member):
            key_block, value_block, seg_block = item
            key_grad, value_grad = key_terms(
                query_heads[member],
                dout_heads[member],
                log_norm[member],
                delta[member],
                my_seg[member],
                split_heads(key_block),
                split_heads(value_block),
                seg_block,
            )
            return jnp.concatenate(
                [key_grad.reshape(sub, width), value_grad.reshape(sub, width)], axis=-1
            )

        stacked = (
            key_part.reshape(count // sub, sub, width),
            value_part.reshape(count // sub, sub, width),
            seg_part.reshape(count // sub, sub),
        )
        columns.append(lax.map(one_block, stacked).reshape(count, 2 * width))
    both_grads = lax.psum_scatter(
        jnp.stack(columns, axis=1).astype(jnp.bfloat16), "band", scatter_dimension=0, tiled=True
    ).astype(jnp.float32)
    both_grads = jnp.transpose(both_grads, (1, 0, 2))
    key_grad = both_grads[:, :, :width]
    value_grad = both_grads[:, :, width:]
    qkv_grad_low = jnp.concatenate([query_grad, key_grad, value_grad], axis=-1).astype(jnp.bfloat16)
    qkv_grad = jnp.einsum(
        "std,ste->de", first_low, qkv_grad_low, preferred_element_type=jnp.float32
    )
    first_grad = jnp.einsum(
        "ste,de->std", qkv_grad_low, qkv_full, preferred_element_type=jnp.float32
    )
    in_grad, gain_one_grad = norm_back(first_grad, gain_one, first_n, first_s)
    token_grad = resid_grad + in_grad
    shares = (
        lax.psum_scatter(
            qkv_grad.astype(jnp.bfloat16), "seq", scatter_dimension=0, tiled=True
        ).astype(jnp.float32),
        lax.psum_scatter(
            outproj_grad.astype(jnp.bfloat16), "seq", scatter_dimension=0, tiled=True
        ).astype(jnp.float32),
        lax.psum_scatter(
            up_grad.astype(jnp.bfloat16), "seq", scatter_dimension=0, tiled=True
        ).astype(jnp.float32),
        lax.psum_scatter(
            down_grad.astype(jnp.bfloat16), "seq", scatter_dimension=0, tiled=True
        ).astype(jnp.float32),
        lax.psum_scatter(
            gain_one_grad.astype(jnp.bfloat16), "seq", scatter_dimension=0, tiled=True
        ).astype(jnp.float32),
        lax.psum_scatter(
            gain_two_grad.astype(jnp.bfloat16), "seq", scatter_dimension=0, tiled=True
        ).astype(jnp.float32),
    )
    summed = (
        lax.psum(shares[0].astype(jnp.bfloat16), "band").astype(jnp.float32),
        lax.psum(shares[1].astype(jnp.bfloat16), "band").astype(jnp.float32),
        lax.psum(shares[2].astype(jnp.bfloat16), "band").astype(jnp.float32),
        lax.psum(shares[3].astype(jnp.bfloat16), "band").astype(jnp.float32),
        lax.psum(shares[4].astype(jnp.bfloat16), "band").astype(jnp.float32),
        lax.psum(shares[5].astype(jnp.bfloat16), "band").astype(jnp.float32),
    )
    qkv_out, outproj_out, up_out, down_out, gain_one_out, gain_two_out = summed
    return (
        layer_out,
        token_grad,
        qkv_out,
        outproj_out,
        up_out,
        down_out,
        gain_one_out,
        gain_two_out,
    )


MESH = pl.DeviceIdType.MESH
BF = jnp.bfloat16
F32 = jnp.float32
SCALE = HEAD_DIM ** (-0.5)


def place():
    b = lax.axis_index("band")
    y = lax.axis_index("seq")
    return b, y, b // 4, (b // 2) % 2, b % 2


def meet(peers):
    sem = pltpu.get_barrier_semaphore()
    for peer in peers:
        pl.semaphore_signal(sem, inc=1, device_id=peer, device_id_type=MESH)
    pl.semaphore_wait(sem, len(peers))


def send(src, dst, ssem, rsem, peer):
    copy = pltpu.make_async_remote_copy(
        src_ref=src, dst_ref=dst, send_sem=ssem, recv_sem=rsem, device_id=peer, device_id_type=MESH
    )
    copy.start()
    return copy


def comm_call(body, name, cid, outs, scratch, n_in):
    vm = pl.BlockSpec(memory_space=pltpu.VMEM)
    return pl.pallas_call(
        body,
        out_shape=[jax.ShapeDtypeStruct(s, d) for s, d in outs],
        in_specs=[vm] * n_in,
        out_specs=[vm] * len(outs),
        scratch_shapes=scratch,
        compiler_params=pltpu.CompilerParams(collective_id=cid, has_side_effects=True),
        name=name,
    )


def dma(n):
    return pltpu.SemaphoreType.DMA((n,))


def norm_rows(v):
    centre = v - jnp.mean(v, axis=-1, keepdims=True)
    inv_std = lax.rsqrt(jnp.mean(centre * centre, axis=-1, keepdims=True) + EPS)
    return centre * inv_std, inv_std


def open_body(tok, seg, wqkv, gains, tok_all, seg_all, w_sel, gains_all, ss, rs):
    b, y, z, x, c = place()
    core, over = (b + 1 - 2 * c, y), (b, 1 - y)
    meet([core, over])
    cps = []
    for m in range(2):
        cps.append(send(tok.at[m], tok_all.at[2 * y + m, c], ss.at[m], rs.at[m], over))
    cps.append(send(seg, seg_all.at[y], ss.at[2], rs.at[2], over))
    cps.append(send(gains, gains_all.at[y], ss.at[3], rs.at[3], over))
    k = 4
    far = (1 - y) * 2 + c
    own = y * 2 + c
    for hp in range(2):
        for p in range(3):
            col = pl.multiple_of(p * 1024 + far * 256 + hp * 128, 128)
            dst = w_sel.at[y, :, pl.ds(hp * 384 + p * 128, 128)]
            cps.append(send(wqkv.at[:, pl.ds(col, 128)], dst, ss.at[k], rs.at[k], over))
            k += 1
    side = []
    for m in range(2):
        side.append(send(tok.at[m], tok_all.at[2 * y + m, c], ss.at[k], rs.at[k], core))
        k += 1
    for hp in range(2):
        for p in range(3):
            col = pl.multiple_of(p * 1024 + own * 256 + hp * 128, 128)
            w_sel[y, :, hp * 384 + p * 128 : hp * 384 + p * 128 + 128] = wqkv[:, pl.ds(col, 128)]
    for m in range(2):
        tok_all[2 * y + m, c] = tok[m]
    seg_all[y] = seg[...]
    gains_all[y] = gains[...]
    for m in range(2):
        cps[m].wait_recv()
        got = tok_all.at[2 * (1 - y) + m, c]
        side.append(send(got, got, ss.at[k], rs.at[k], core))
        k += 1
    for m in range(2):
        cps[m].wait_send()
    for cp in cps[2:] + side:
        cp.wait()


def open_call(tok, seg, wqkv, gains):
    return comm_call(
        open_body,
        "open_column",
        1,
        [((4, 2, 96, 1024), BF), ((2, 2, 1536), jnp.int32), ((2, 512, 768), BF), ((2, 8, 512), F32)],
        [dma(14), dma(14)],
        4,
    )(tok, seg, wqkv, gains)


def chips(b, c, y):
    j = b // 2
    res = []
    for k in range(1, 8):
        jd = (j + k) % 8
        res.append((jd, (jd * 2 + c, y)))
    return res


def to_heads_body(qkv, up, att, up_sel, ss, rs):
    b, y, z, x, c = place()
    over = (b, 1 - y)
    others = chips(b, c, y)
    meet([over] + [peer for _, peer in others])
    j = b // 2
    cps = []
    far = pl.multiple_of(((1 - y) * 2 + c) * 1024, 1024)
    own = pl.multiple_of((y * 2 + c) * 1024, 1024)
    cps.append(send(up.at[:, pl.ds(far, 1024)], up_sel.at[y], ss.at[0], rs.at[0], over))
    for k, (jd, peer) in enumerate(others):
        col = pl.multiple_of((jd % 2) * 384, 128)
        cps.append(
            send(qkv.at[jd // 2, :, pl.ds(col, 384)], att.at[j], ss.at[k + 1], rs.at[k + 1], peer)
        )
    att[j] = qkv[z, :, pl.ds(pl.multiple_of(x * 384, 128), 384)]
    up_sel[y] = up[:, pl.ds(own, 1024)]
    for cp in cps:
        cp.wait()


def to_heads(qkv, up):
    return comm_call(
        to_heads_body,
        "to_heads",
        2,
        [((8, 192, 384), BF), ((2, 512, 1024), BF)],
        [dma(8), dma(8)],
        2,
    )(qkv, up)


def first_dot(a, d):
    return lax.dot_general(a, d, (((0,), (0,)), ((), ())), preferred_element_type=F32)


def middle_body(
    att,
    cot,
    tok,
    valid,
    valid_all,
    gain,
    out_w,
    up_w,
    down_w,
    do,
    layer_out,
    rgrad,
    ggrad,
    part,
    rows,
    cot_all,
    h_all,
    b_all,
    buf,
    gots,
    mids,
    fins,
    own,
    grad_two,
    hgrad,
    hidden,
    pgrad,
    agrad,
    resid,
    a_s,
    a_r,
    c_s,
    c_r,
    r_s,
    r_r,
    s_s,
    s_r,
    d_s,
    d_r,
):
    b, y, z, x, c = place()
    core, over = (b + 1 - 2 * c, y), (b, 1 - y)
    j = b // 2
    others = chips(b, c, y)
    mine = pl.ds(pl.multiple_of(c * 96, 32), 96)
    theirs = pl.ds(pl.multiple_of((1 - c) * 96, 32), 96)
    far = [2 * (1 - y) + m for m in range(2)]
    near = [2 * y + m for m in range(2)]
    col = pl.multiple_of(x * 128, 128)
    meet([core, over] + [peer for _, peer in others])

    def sum_start(k, q, i):
        return send(buf.at[k, q, theirs], gots.at[k, q], r_s.at[k, i], r_r.at[k, i], core)

    def sum_over(k, m, first):
        first.wait_recv()
        q = far[m]
        mids[k, m] = (buf[k, q, mine].astype(F32) + gots[k, q].astype(F32)).astype(BF)
        return send(mids.at[k, m], fins.at[k, m], r_s.at[k, 4 + m], r_r.at[k, 4 + m], over)

    def sum_end(k, m, first, second):
        first.wait_recv()
        second.wait_recv()
        q = near[m]
        return buf[k, q, mine].astype(F32) + gots[k, q].astype(F32) + fins[k, m].astype(F32)

    def spread_start(k, m, full):
        to = full.at[near[m], mine]
        full[near[m], mine] = own[k, m]
        return (
            send(own.at[k, m], to, s_s.at[k, m], s_r.at[k, m], over),
            send(own.at[k, m], to, s_s.at[k, 2 + m], s_r.at[k, 2 + m], core),
        )

    def spread_pass(k, m, full, pair):
        pair[0].wait_recv()
        got = full.at[far[m], mine]
        return send(got, got, s_s.at[k, 4 + m], s_r.at[k, 4 + m], core)

    done = []
    for k, (jd, peer) in enumerate(others):
        done.append(send(att.at[jd], rows.at[z, :, pl.ds(col, 128)], a_s.at[k], a_r.at[k], peer))
    cots = []
    for m in range(2):
        to = cot_all.at[near[m], mine]
        cots.append(send(cot.at[m], to, c_s.at[m], c_r.at[m], over))
    for m in range(2):
        to = cot_all.at[near[m], mine]
        cots.append(send(cot.at[m], to, c_s.at[2 + m], c_r.at[2 + m], core))
        cot_all[near[m], mine] = cot[m]
    rows[z, :, pl.ds(col, 128)] = att[j]
    for cp in done:
        cp.wait_recv()

    out_rows = out_w[pl.ds(pl.multiple_of(c * 256, 256), 256)]
    firsts = []
    for i, q in enumerate(far + near):
        buf[0, q] = plain_dot(rows[q], out_rows).astype(BF)
        firsts.append(sum_start(0, q, i))
    seconds = [sum_over(0, m, firsts[m]) for m in range(2)]

    down_rows = down_w[pl.ds(pl.multiple_of(c * 1024, 1024), 1024)]

    def hidden_gradient(q):
        grad_two[q] = (valid_all[q][:, :1] * cot_all[q].astype(F32)).astype(BF)
        hgrad[q] = last_dot(grad_two[q], down_rows)

    for m in range(2):
        cots[2 + m].wait_recv()
        hidden_gradient(near[m])
    passed = []
    for m in range(2):
        cots[m].wait_recv()
        got = cot_all.at[far[m], mine]
        passed.append(send(got, got, c_s.at[4 + m], c_r.at[4 + m], core))
    for m in range(2):
        passed[m].wait_recv()
        hidden_gradient(far[m])

    spread = []
    for m in range(2):
        res = tok[m].astype(F32) + valid[m][:, :1] * sum_end(0, m, firsts[2 + m], seconds[m])
        resid[m] = res
        normed, _ = norm_rows(res)
        own[0, m] = (normed * gain[1:2]).astype(BF)
        spread.append(spread_start(0, m, h_all))
    done += firsts + seconds

    def hidden_units(q):
        pre = plain_dot(h_all[q], up_w[...])
        phi = 0.5 * (1.0 + lax.erf(pre * ROOT_HALF))
        hidden[q] = (pre * phi).astype(BF)
        slope = phi + pre * DENSITY * jnp.exp(-0.5 * pre * pre)
        pgrad[q] = (hgrad[q] * slope).astype(BF)
        buf[1, q] = last_dot(pgrad[q], up_w[...]).astype(BF)

    def second_branch(q, i):
        buf[2, q] = plain_dot(hidden[q], down_rows).astype(BF)
        return sum_start(2, q, i)

    firsts, lasts = [None] * 4, [None] * 4
    for m in range(2):
        spread[m][1].wait_recv()
        hidden_units(near[m])
        firsts[2 + m] = sum_start(1, near[m], 2 + m)
    passed2, seconds = [], []
    for m in range(2):
        passed2.append(spread_pass(0, m, h_all, spread[m]))
        passed2[m].wait_recv()
        hidden_units(far[m])
        firsts[m] = sum_start(1, far[m], m)
        lasts[2 + m] = second_branch(near[m], 2 + m)
        seconds.append(sum_over(1, m, firsts[m]))

    def weight_gradient(left, right, first_chunk):
        for i in range(4):
            block = left[:, :, i * 256 : i * 256 + 256].reshape(768, 256)
            res = first_dot(block, right[...].reshape(768, 1024)).astype(BF)
            for k in range(4):
                part[first_chunk + k, i // 2, (i % 2) * 256 : (i % 2) * 256 + 256] = res[
                    :, k * 256 : k * 256 + 256
                ]

    weight_gradient(hidden, grad_two, 0)

    total = jnp.zeros((1, 1024), F32)
    bspread = []
    for m in range(2):
        e = sum_end(1, m, firsts[2 + m], seconds[m])
        normed, inv_std = norm_rows(resid[m])
        g = e * gain[1:2]
        total = total + jnp.sum(e * normed, axis=0, keepdims=True)
        one = jnp.mean(g, axis=-1, keepdims=True)
        two = jnp.mean(g * normed, axis=-1, keepdims=True)
        rg = cot[m].astype(F32) + (g - one - normed * two) * inv_std
        rgrad[m] = rg
        own[1, m] = (valid[m][:, :1] * rg).astype(BF)
        bspread.append(spread_start(1, m, b_all))
    ggrad[...] = jnp.broadcast_to(total, (8, 1024))
    done += firsts + seconds

    for m in range(2):
        lasts[m] = second_branch(far[m], m)
    lseconds = [sum_over(2, m, lasts[m]) for m in range(2)]
    weight_gradient(h_all, pgrad, 4)

    def grad_copy(q, xd, i):
        dest = q * 2 + xd
        return dest, pltpu.make_async_remote_copy(
            src_ref=agrad.at[q, :, pl.ds(xd * 128, 128)],
            dst_ref=do.at[j],
            send_sem=d_s.at[i, xd],
            recv_sem=d_r.at[j],
            device_id=(dest * 2 + c, y),
            device_id_type=MESH,
        )

    def attention_gradient(q, i):
        agrad[q] = last_dot(b_all[q], out_rows).astype(BF)
        for xd in range(2):
            dest, cp = grad_copy(q, xd, i)

            @pl.when(dest != j)
            def _():
                cp.start()

            @pl.when(dest == j)
            def _():
                do[j] = agrad[q, :, xd * 128 : xd * 128 + 128]

    for m in range(2):
        bspread[m][1].wait_recv()
        attention_gradient(near[m], 2 + m)
    passed3 = []
    for m in range(2):
        passed3.append(spread_pass(1, m, b_all, bspread[m]))
        passed3[m].wait_recv()
        attention_gradient(far[m], m)

    res = first_dot(rows[...].reshape(768, 256), b_all[...].reshape(768, 1024)).astype(BF)
    for h in range(2):
        for k in range(2):
            at = (h * 2 + k) * 256
            part[8, h, k * 256 : k * 256 + 256] = res[:, at : at + 256]

    for m in range(2):
        branch = sum_end(2, m, lasts[2 + m], lseconds[m])
        layer_out[m] = (resid[m] + valid[m][:, :1] * branch).astype(BF)
    done += lasts + lseconds + cots + passed + passed2 + passed3
    for pair in spread + bspread:
        done += list(pair)
    for cp in done:
        cp.wait_send()
    for i, q in enumerate(far + near):
        for xd in range(2):
            dest, cp = grad_copy(q, xd, i)

            @pl.when(dest != j)
            def _():
                cp.wait_send()

    for k in range(1, 8):
        js = (j + k) % 8
        pltpu.make_async_remote_copy(
            src_ref=agrad.at[0, :, pl.ds(0, 128)],
            dst_ref=do.at[js],
            send_sem=d_s.at[0, 0],
            recv_sem=d_r.at[js],
            device_id=core,
            device_id_type=MESH,
        ).wait_recv()


def middle(att, cot, tok, valid, valid_all, gain, out_w, up_w, down_w):
    rows192 = (4, 192, 1024)
    return comm_call(
        middle_body,
        "middle",
        3,
        [
            ((8, 192, 128), BF),
            ((2, 96, 1024), BF),
            ((2, 96, 1024), F32),
            ((8, 1024), F32),
            ((9, 2, 512, 256), BF),
        ],
        [
            pltpu.VMEM((4, 192, 256), BF),
            pltpu.VMEM(rows192, BF),
            pltpu.VMEM(rows192, BF),
            pltpu.VMEM(rows192, BF),
            pltpu.VMEM((3,) + rows192, BF),
            pltpu.VMEM((3, 4, 96, 1024), BF),
            pltpu.VMEM((3, 2, 96, 1024), BF),
            pltpu.VMEM((3, 2, 96, 1024), BF),
            pltpu.VMEM((2, 2, 96, 1024), BF),
            pltpu.VMEM(rows192, BF),
            pltpu.VMEM(rows192, F32),
            pltpu.VMEM(rows192, BF),
            pltpu.VMEM(rows192, BF),
            pltpu.VMEM((4, 192, 256), BF),
            pltpu.VMEM((2, 96, 1024), F32),
            dma(7),
            dma(7),
            dma(6),
            dma(6),
            pltpu.SemaphoreType.DMA((3, 6)),
            pltpu.SemaphoreType.DMA((3, 6)),
            pltpu.SemaphoreType.DMA((2, 6)),
            pltpu.SemaphoreType.DMA((2, 6)),
            pltpu.SemaphoreType.DMA((4, 2)),
            dma(8),
        ],
        9,
    )(att, cot, tok, valid, valid_all, gain, out_w, up_w, down_w)


def last_dot(a, b):
    return lax.dot_general(a, b, (((1,), (1,)), ((), ())), preferred_element_type=F32)


def plain_dot(a, b):
    return lax.dot_general(a, b, (((1,), (0,)), ((), ())), preferred_element_type=F32)


def attend_body(qkv, seg_col, seg_row, out_low, out, lse):
    rows = out.shape[0]
    i = pl.program_id(0)
    at = pl.multiple_of(i * rows, rows)
    q = qkv[pl.ds(at, rows), 0:128]
    keys = qkv[:, 128:256]
    values = qkv[:, 256:384]
    low_half = lax.broadcasted_iota(jnp.int32, (rows, 128), 1) < HEAD_DIM
    mask = seg_col[:, 0:1] == seg_row[0:1, :]
    outs, norms = [], []
    for h in range(2):
        qh = jnp.where(low_half if h == 0 else ~low_half, q * SCALE, 0.0).astype(BF)
        scores = jnp.where(mask, last_dot(qh, keys), NEG)
        top = jnp.max(scores, axis=-1, keepdims=True)
        probs = jnp.exp(scores - top)
        total = jnp.sum(probs, axis=-1, keepdims=True)
        outs.append(plain_dot(probs.astype(BF), values) / total)
        norms.append(top + jnp.log(total))
    res = jnp.where(low_half, outs[0], outs[1])
    out[...] = res
    out_low[...] = res.astype(BF)
    lse[...] = jnp.where(low_half, norms[0], norms[1])


def attend(qkv, seg_col, seg_row):
    length = qkv.shape[0]
    rows = 256
    tile = pl.BlockSpec((rows, 128), lambda i: (i, 0))
    return pl.pallas_call(
        attend_body,
        grid=(length // rows,),
        in_specs=[
            pl.BlockSpec((length, 384), lambda i: (0, 0)),
            pl.BlockSpec((rows, 128), lambda i: (i, 0)),
            pl.BlockSpec((8, length), lambda i: (0, 0)),
        ],
        out_specs=[tile, tile, tile],
        out_shape=[
            jax.ShapeDtypeStruct((length, 128), BF),
            jax.ShapeDtypeStruct((length, 128), F32),
            jax.ShapeDtypeStruct((length, 128), F32),
        ],
        name="attend",
    )(qkv, seg_col, seg_row)


def attend_back_body(qkv, out, lse, do, seg_col, seg_row, dqkv, lse_t, delta, keys_t, dq_t):
    length = qkv.shape[0]
    rows = seg_col.shape[0]
    i = pl.program_id(0)
    at = pl.multiple_of(i * rows, rows)

    @pl.when(i == 0)
    def _():
        lse_t[...] = jnp.transpose(lse[...])
        prod = jnp.transpose(do[...].astype(F32) * out[...])
        delta[0:8] = jnp.broadcast_to(jnp.sum(prod[:HEAD_DIM], axis=0, keepdims=True), (8, length))
        delta[8:16] = jnp.broadcast_to(jnp.sum(prod[HEAD_DIM:], axis=0, keepdims=True), (8, length))
        keys_t[...] = jnp.transpose(qkv[:, 128:256].astype(F32)).astype(BF)
        dq_t[...] = jnp.zeros_like(dq_t)

    keys = qkv[pl.ds(at, rows), 128:256]
    values = qkv[pl.ds(at, rows), 256:384]
    q = qkv[:, 0:128]
    douts = do[...]
    low_half = lax.broadcasted_iota(jnp.int32, (rows, 128), 1) < HEAD_DIM
    low_rows = lax.broadcasted_iota(jnp.int32, (128, 1), 0) < HEAD_DIM
    mask = seg_col[:, 0:1] == seg_row[0:1, :]
    kgrads, vgrads, qgrads = [], [], []
    for h in range(2):
        pick = low_half if h == 0 else ~low_half
        kh = jnp.where(pick, keys * SCALE, 0.0).astype(BF)
        vh = jnp.where(pick, values, 0.0).astype(BF)
        scores = last_dot(kh, q)
        probs = jnp.where(mask, jnp.exp(scores - lse_t[h * HEAD_DIM : h * HEAD_DIM + 1]), 0.0)
        vgrads.append(plain_dot(probs.astype(BF), douts))
        pgrad = last_dot(vh, douts)
        sgrad = (probs * (pgrad - delta[h * 8 : h * 8 + 1])).astype(BF)
        kgrads.append(plain_dot(sgrad, q))
        qgrads.append(plain_dot(keys_t[:, pl.ds(at, rows)], sgrad))
    dq_t[...] += jnp.where(low_rows, qgrads[0], qgrads[1])
    dqkv[pl.ds(at, rows), 128:256] = (jnp.where(low_half, kgrads[0], kgrads[1]) * SCALE).astype(BF)
    dqkv[pl.ds(at, rows), 256:384] = jnp.where(low_half, vgrads[0], vgrads[1]).astype(BF)

    @pl.when(i == pl.num_programs(0) - 1)
    def _():
        dqkv[:, 0:128] = (jnp.transpose(dq_t[...]) * SCALE).astype(BF)


def attend_back(qkv, out, lse, do, seg_col, seg_row):
    length = qkv.shape[0]
    rows = 256
    whole = pl.BlockSpec((length, 128), lambda i: (0, 0))
    wide = pl.BlockSpec((length, 384), lambda i: (0, 0))
    return pl.pallas_call(
        attend_back_body,
        grid=(length // rows,),
        in_specs=[
            wide,
            whole,
            whole,
            whole,
            pl.BlockSpec((rows, 128), lambda i: (i, 0)),
            pl.BlockSpec((8, length), lambda i: (0, 0)),
        ],
        out_specs=wide,
        out_shape=jax.ShapeDtypeStruct((length, 384), BF),
        scratch_shapes=[
            pltpu.VMEM((128, length), F32),
            pltpu.VMEM((16, length), F32),
            pltpu.VMEM((128, length), BF),
            pltpu.VMEM((128, length), F32),
        ],
        name="attend_back",
    )(qkv, out, lse, do, seg_col, seg_row)


CHUNKS = 12
SWAPPED = ((4, 8), (9, 12))
PLAIN = ((0, 4), (8, 9))
STAGES = 5


def chunk_sums(part, full, r1, r2, r3, p3, tmp, ss, rs, ls):
    b, y, z, x, c = place()
    z0, zb = z % 2, z // 2
    core, over = (b + 1 - 2 * c, y), (b, 1 - y)
    px, p0, pb = (b + 2 - 4 * x, y), (b + 4 - 8 * z0, y), (b + 8 - 16 * zb, y)
    o1 = x * 256
    o2 = o1 + z0 * 128
    o3 = o2 + zb * 64

    def rows(at, size):
        return pl.ds(pl.multiple_of(at, 64), size)

    def remote(src, dst, stage, i, peer):
        return pltpu.make_async_remote_copy(
            src_ref=src,
            dst_ref=dst,
            send_sem=ss.at[stage, i],
            recv_sem=rs.at[stage, i],
            device_id=peer,
            device_id_type=MESH,
        )

    def c_x(i):
        return remote(part.at[i, :, rows((1 - x) * 256, 256)], r1.at[i], 0, i, px)

    def c_z0(i):
        return remote(part.at[i, :, rows(o1 + (1 - z0) * 128, 128)], r2.at[i], 1, i, p0)

    def c_zb(i):
        return remote(part.at[i, :, rows(o2 + (1 - zb) * 64, 64)], r3.at[i], 2, i, pb)

    def c_y(i):
        return remote(tmp.at[i], p3.at[i, y], 3, i, over)

    def c_gb(i):
        return remote(p3.at[i], full.at[i, c, :, rows(o3, 64)], 4, i, pb)

    def c_own(i):
        return pltpu.make_async_copy(p3.at[i], full.at[i, c, :, rows(o3, 64)], ls.at[i])

    def c_g0(i):
        src = full.at[i, c, :, rows(o2, 128)]
        return remote(src, src, 5, i, p0)

    def c_gx(i):
        src = full.at[i, c, :, rows(o1, 256)]
        return remote(src, src, 6, i, px)

    def c_core(i):
        src = full.at[i, c]
        return remote(src, src, 7, i, core)

    def add_x(i):
        c_x(i).wait_recv()
        mine = part[i, :, rows(o1, 256)].astype(F32)
        part[i, :, rows(o1, 256)] = (mine + r1[i].astype(F32)).astype(BF)
        c_z0(i).start()

    def add_z0(i):
        c_z0(i).wait_recv()
        mine = part[i, :, rows(o2, 128)].astype(F32)
        part[i, :, rows(o2, 128)] = (mine + r2[i].astype(F32)).astype(BF)
        c_zb(i).start()

    def add_zb_plain(i):
        c_zb(i).wait_recv()
        mine = part[i, :, rows(o3, 64)].astype(F32)
        p3[i] = (mine + r3[i].astype(F32)).astype(BF)
        c_gb(i).start()
        c_own(i).start()

    def add_zb_swap(i):
        c_zb(i).wait_recv()
        for h, dst in ((y, p3.at[i, y]), (1 - y, tmp.at[i])):
            mine = part[i, h, rows(o3, 64)].astype(F32)
            dst[...] = (mine + r3[i, h].astype(F32)).astype(BF)
        c_y(i).start()

    def take_y(i):
        c_y(i).wait_recv()
        c_gb(i).start()
        c_own(i).start()

    def grow_z0(i):
        c_gb(i).wait_recv()
        c_own(i).wait()
        c_g0(i).start()

    def grow_x(i):
        c_g0(i).wait_recv()
        c_gx(i).start()

    def when_chunk(i, act, ranges=((0, CHUNKS),)):
        for lo, hi in ranges:
            if isinstance(i, int):
                if lo <= i < hi:
                    act(i)
                continue

            @pl.when((i >= lo) & (i < hi))
            def _():
                act(i)

    def tick(t):
        when_chunk(t - 5, grow_x)
        when_chunk(t - 4, grow_z0)
        when_chunk(t - 3, take_y, SWAPPED)
        when_chunk(t - 2, add_zb_plain, PLAIN)
        when_chunk(t - 2, add_zb_swap, SWAPPED)
        when_chunk(t - 1, add_z0)
        when_chunk(t, add_x)

    def finish():
        @pl.loop(0, CHUNKS)
        def _(i):
            c_gx(i).wait_recv()
            c_core(i).start()

        @pl.loop(0, CHUNKS)
        def _(i):
            c_core(i).wait_recv()
            for cp in (c_x, c_z0, c_zb, c_gb, c_g0, c_gx, c_core):
                cp(i).wait_send()

        for lo, hi in SWAPPED:

            @pl.loop(lo, hi)
            def _(i):
                c_y(i).wait_send()

    def start(i):
        c_x(i).start()

    return start, tick, finish


def chunk_scratch():
    return [
        pltpu.VMEM((CHUNKS, 2, 512, 256), BF),
        pltpu.VMEM((CHUNKS, 2, 256, 256), BF),
        pltpu.VMEM((CHUNKS, 2, 128, 256), BF),
        pltpu.VMEM((CHUNKS, 2, 64, 256), BF),
        pltpu.VMEM((CHUNKS, 2, 64, 256), BF),
        pltpu.VMEM((CHUNKS, 64, 256), BF),
        pltpu.SemaphoreType.DMA((8, CHUNKS)),
        pltpu.SemaphoreType.DMA((8, CHUNKS)),
        pltpu.SemaphoreType.DMA((CHUNKS,)),
    ]


def tail_body(
    dqkv,
    parts,
    w_sel,
    h_one,
    tok,
    rgrad,
    gain,
    gg,
    tgrad,
    full,
    gsum,
    rows,
    buf,
    gots,
    mids,
    fins,
    g1,
    g2,
    g3,
    a_s,
    a_r,
    r_s,
    r_r,
    g_s,
    g_r,
    l_s,
    part,
    r1,
    r2,
    r3,
    p3,
    tmp,
    ss,
    rs,
    ls,
):
    b, y, z, x, c = place()
    core, over = (b + 1 - 2 * c, y), (b, 1 - y)
    j = b // 2
    others = chips(b, c, y)
    mine = pl.ds(pl.multiple_of(c * 96, 32), 96)
    theirs = pl.ds(pl.multiple_of((1 - c) * 96, 32), 96)
    far = [2 * (1 - y) + m for m in range(2)]
    near = [2 * y + m for m in range(2)]
    start, tick, finish = chunk_sums(part, full, r1, r2, r3, p3, tmp, ss, rs, ls)
    load = pltpu.make_async_copy(parts, part.at[0:9], l_s.at[0])
    load.start()
    meet([core, over] + [peer for _, peer in others])
    col = pl.multiple_of(x * 384, 128)
    done = []
    for k, (jd, peer) in enumerate(others):
        done.append(send(dqkv.at[jd], rows.at[z, :, pl.ds(col, 384)], a_s.at[k], a_r.at[k], peer))
    rows[z, :, pl.ds(col, 384)] = dqkv[j]
    load.wait()
    for i in range(9):
        start(i)
    for t in range(2):
        tick(t)
    for cp in done:
        cp.wait_recv()
    firsts = []
    for i, q in enumerate(far + near):
        buf[q] = last_dot(rows[q], w_sel[...]).astype(BF)
        firsts.append(
            send(buf.at[q, theirs], gots.at[q], r_s.at[i], r_r.at[i], core)
        )
    seconds = []
    for m in range(2):
        firsts[m].wait_recv()
        q = far[m]
        mids[m] = (buf[q, mine].astype(F32) + gots[q].astype(F32)).astype(BF)
        seconds.append(send(mids.at[m], fins.at[m], r_s.at[4 + m], r_r.at[4 + m], over))
    for i in range(4):
        block = h_one[:, :, i * 256 : i * 256 + 256].reshape(768, 256)
        res = first_dot(block, rows[...].reshape(768, 768)).astype(BF)
        for k in range(3):
            part[9 + k, i // 2, (i % 2) * 256 : (i % 2) * 256 + 256] = res[
                :, k * 256 : k * 256 + 256
            ]
    for i in range(9, 12):
        start(i)
    total = jnp.zeros((1, 1024), F32)
    for m in range(2):
        tick(2 + m)
        firsts[2 + m].wait_recv()
        seconds[m].wait_recv()
        q = near[m]
        e = buf[q, mine].astype(F32) + gots[q].astype(F32) + fins[m].astype(F32)
        normed, inv_std = norm_rows(tok[m].astype(F32))
        g = e * gain[0:1]
        total = total + jnp.sum(e * normed, axis=0, keepdims=True)
        one = jnp.mean(g, axis=-1, keepdims=True)
        two = jnp.mean(g * normed, axis=-1, keepdims=True)
        tgrad[m] = rgrad[m] + (g - one - normed * two) * inv_std
    g1[1] = jnp.where(lax.broadcasted_iota(jnp.int32, (8, 1024), 0) == 0, total, gg[...])
    gcps = [send(g1.at[1], g1.at[0], g_s.at[0], g_r.at[0], core)]
    tick(4)
    gcps[0].wait_recv()
    g2[1] = g1[0] + g1[1]
    gcps.append(send(g2.at[1], g2.at[0], g_s.at[1], g_r.at[1], over))
    tick(5)
    gcps[1].wait_recv()
    g3[j] = g2[1] + g2[0]
    for k, (jd, peer) in enumerate(others):
        gcps.append(send(g3.at[j], g3.at[j], g_s.at[2 + k], g_r.at[2 + k], peer))

    @pl.loop(6, CHUNKS + STAGES)
    def _(t):
        tick(t)

    finish()
    for cp in gcps[:2] + done + firsts + seconds:
        cp.wait_send()
    for cp in gcps[2:]:
        cp.wait()
    res = g3[0]
    for k in range(1, 8):
        res = res + g3[k]
    gsum[...] = res


def tail(dqkv, parts, w_sel, h_one, tok, rgrad, gain, gg):
    vm = pl.BlockSpec(memory_space=pltpu.VMEM)
    hbm = pl.BlockSpec(memory_space=pl.ANY)
    return pl.pallas_call(
        tail_body,
        out_shape=[
            jax.ShapeDtypeStruct((2, 96, 1024), F32),
            jax.ShapeDtypeStruct((CHUNKS, 2, 2, 512, 256), BF),
            jax.ShapeDtypeStruct((8, 1024), F32),
        ],
        in_specs=[vm, hbm] + [vm] * 6,
        out_specs=[vm, hbm, vm],
        scratch_shapes=[
            pltpu.VMEM((4, 192, 768), BF),
            pltpu.VMEM((4, 192, 1024), BF),
            pltpu.VMEM((4, 96, 1024), BF),
            pltpu.VMEM((2, 96, 1024), BF),
            pltpu.VMEM((2, 96, 1024), BF),
            pltpu.VMEM((2, 8, 1024), F32),
            pltpu.VMEM((2, 8, 1024), F32),
            pltpu.VMEM((8, 8, 1024), F32),
            dma(7),
            dma(7),
            dma(6),
            dma(6),
            dma(9),
            dma(9),
            dma(1),
        ]
        + chunk_scratch(),
        compiler_params=pltpu.CompilerParams(collective_id=4, has_side_effects=True),
        name="tail",
    )(dqkv, parts, w_sel, h_one, tok, rgrad, gain, gg)


def widen_body(src, dst):
    for k in range(4):
        dst[:, k * 256 : k * 256 + 256] = src[k].astype(F32)


def widen_out_body(src, dst):
    for h in range(2):
        for k in range(2):
            col = (h * 2 + k) * 256
            dst[:, col : col + 256] = src[h, k * 256 : k * 256 + 256].astype(F32)


def widen_qkv_body(src, dst):
    for r in range(4):
        for t in range(6):
            col = (t % 3) * 1024 + r * 256 + (t // 3) * 128
            half = (t % 2) * 128
            dst[:, col : col + 128] = src[t // 2, r % 2, r // 2, :, half : half + 128].astype(F32)


def widen_all(full):
    down = pl.pallas_call(
        widen_body,
        grid=(4,),
        in_specs=[pl.BlockSpec((4, None, None, 512, 256), lambda r: (0, r // 2, r % 2, 0, 0))],
        out_specs=pl.BlockSpec((512, 1024), lambda r: (r, 0)),
        out_shape=jax.ShapeDtypeStruct((2048, 1024), F32),
        name="widen_down",
    )(full)
    up = pl.pallas_call(
        widen_body,
        grid=(4,),
        in_specs=[pl.BlockSpec((4, None, None, 512, 256), lambda r: (1, r % 2, r // 2, 0, 0))],
        out_specs=pl.BlockSpec((512, 1024), lambda r: (0, r)),
        out_shape=jax.ShapeDtypeStruct((512, 4096), F32),
        name="widen_up",
    )(full)
    out = pl.pallas_call(
        widen_out_body,
        grid=(2,),
        in_specs=[pl.BlockSpec((None, None, 2, 512, 256), lambda r: (8, r, 0, 0, 0))],
        out_specs=pl.BlockSpec((256, 1024), lambda r: (r, 0)),
        out_shape=jax.ShapeDtypeStruct((512, 1024), F32),
        name="widen_out",
    )(full)
    qkv = pl.pallas_call(
        widen_qkv_body,
        grid=(4,),
        in_specs=[pl.BlockSpec((3, 2, 2, 128, 256), lambda i: (3, 0, 0, i, 0))],
        out_specs=pl.BlockSpec((128, 3072), lambda i: (i, 0)),
        out_shape=jax.ShapeDtypeStruct((512, 3072), F32),
        name="widen_qkv",
    )(full)
    return down, up, out, qkv


def column_device(
    tokens,
    segment_ids,
    qkv_weight,
    out_weight,
    up_weight,
    down_weight,
    gain_first,
    gain_second,
    out_cotangent,
):
    b, y, z, x, c = place()
    my_seg = lax.dynamic_slice_in_dim(segment_ids, b * 96, 96, 1)
    valid = jnp.broadcast_to((my_seg >= 0).astype(F32)[:, :, None], (2, 96, 128))
    gains = jnp.pad(jnp.stack([gain_first, gain_second]).astype(F32), ((0, 6), (0, 0)))
    tok_all, seg_all, w_sel, gains_all = open_call(tokens, segment_ids, qkv_weight, gains)
    gain = jnp.transpose(gains_all, (1, 0, 2)).reshape(8, 1024)
    seg_all = seg_all.reshape(4, 1536)
    seg_z = lax.dynamic_slice_in_dim(seg_all, z, 1, 0)
    seg_row = jnp.broadcast_to(seg_z, (8, 1536))
    seg_col = jnp.broadcast_to(seg_z.reshape(1536, 1), (1536, 128))
    seg_here = lax.dynamic_slice_in_dim(seg_all, (z * 2 + x) * 192, 192, 1)
    valid_all = jnp.broadcast_to((seg_here >= 0).astype(F32)[:, :, None], (4, 192, 128))
    w_sel = w_sel.reshape(1024, 768)
    normed, _ = norm_rows(tok_all.reshape(768, 1024).astype(F32))
    h_one = (normed * gain[0:1]).astype(BF)
    qkv = plain_dot(h_one, w_sel).astype(BF)
    att, up_sel = to_heads(qkv.reshape(4, 192, 768), up_weight)
    up_sel = up_sel.reshape(1024, 1024)
    att = att.reshape(1536, 384)
    out_low, out_full, lse = attend(att, seg_col, seg_row)
    do, layer_out, rgrad, gain_two_grad, part = middle(
        out_low.reshape(8, 192, 128),
        out_cotangent,
        tokens,
        valid,
        valid_all,
        gain,
        out_weight,
        up_sel,
        down_weight,
    )
    dqkv = attend_back(att, out_full, lse, do.reshape(1536, 128), seg_col, seg_row)
    token_grad, full, gain_sum = tail(
        dqkv.reshape(8, 192, 384),
        part,
        w_sel,
        h_one.reshape(4, 192, 1024),
        tokens,
        rgrad,
        gain,
        gain_two_grad,
    )
    down_out, up_out, out_out, qkv_out = widen_all(full)
    gain_out = lax.dynamic_slice_in_dim(gain_sum, y * 512, 512, 1)
    return (
        layer_out,
        token_grad,
        qkv_out,
        out_out,
        up_out,
        down_out,
        gain_out[0],
        gain_out[1],
    )


def solution(mesh):
    placed = (
        P("seq", "band", None),
        P("seq", None),
        P("seq", None),
        P("seq", None),
        P("seq", None),
        P("seq", None),
        P("seq"),
        P("seq"),
        P("seq", "band", None),
    )
    split = dict(mesh.shape) == {"band": 16, "seq": 2}
    return jax.shard_map(
        column_device if split else per_device,
        mesh=mesh,
        in_specs=placed,
        out_specs=(
            P("seq", "band", None),
            P("seq", "band", None),
            P("seq", None),
            P("seq", None),
            P("seq", None),
            P("seq", None),
            P("seq"),
            P("seq"),
        ),
        check_vma=False,
    )
```
